32 devices in a mesh: fsdp: 4 (over z), ctx: 4 (over y, core), tp: 2 (over x).
Axes of the slice: x: 2, y: 2, z: 4, core: 2. Of those that a mesh axis runs over, the one named last changes fastest.
Arguments:
- tokens: bfloat16 [4, 512, 1536], P('fsdp', 'ctx'), may hold values from -6 to 6
- cotangent: bfloat16 [4, 512, 1536], P('fsdp', 'ctx'), may hold values from -6 to 6
- prefix: int32 [4], P('fsdp'), may hold values from 51 to 256
- norm_one: bfloat16 [1536], P(('fsdp', 'ctx')), may hold values from 0.25 to 1.75
- w_query: bfloat16 [1536, 768], P(('fsdp', 'ctx'), 'tp'), may hold values from -0.078125 to 0.078125
- w_key: bfloat16 [1536, 768], P(('fsdp', 'ctx'), 'tp'), may hold values from -0.078125 to 0.078125
- value_projection_weight: bfloat16 [1536, 768], P(('fsdp', 'ctx'), 'tp'), may hold values from -0.15625 to 0.15625
- w_out: bfloat16 [768, 1536], P('tp', ('fsdp', 'ctx')), may hold values from -1.25 to 1.25
- position_bias_matrix: bfloat16 [12, 32], P('tp'), may hold values from -3 to 3
- norm_two: bfloat16 [1536], P(('fsdp', 'ctx')), may hold values from 0.25 to 1.75
- w_gate: bfloat16 [1536, 3968], P(('fsdp', 'ctx'), 'tp'), may hold values from -0.15625 to 0.15625
- w_up: bfloat16 [1536, 3968], P(('fsdp', 'ctx'), 'tp'), may hold values from -0.15625 to 0.15625
- w_down: bfloat16 [3968, 1536], P('tp', ('fsdp', 'ctx')), may hold values from -0.09375 to 0.09375
Outputs:
- mixed: bfloat16 [4, 512, 1536], P('fsdp', 'ctx')
- input_grad: bfloat16 [4, 512, 1536], P('fsdp', 'ctx')
- grad_norm_one: float32 [1536], P(('fsdp', 'ctx'))
- grad_query: float32 [1536, 768], P(('fsdp', 'ctx'), 'tp')
- grad_key: float32 [1536, 768], P(('fsdp', 'ctx'), 'tp')
- grad_value: float32 [1536, 768], P(('fsdp', 'ctx'), 'tp')
- grad_out: float32 [768, 1536], P('tp', ('fsdp', 'ctx'))
- grad_table: float32 [12, 32], P('tp')
- grad_norm_two: float32 [1536], P(('fsdp', 'ctx'))
- grad_gate: float32 [1536, 3968], P(('fsdp', 'ctx'), 'tp')
- grad_up: float32 [1536, 3968], P(('fsdp', 'ctx'), 'tp')
- grad_down: float32 [3968, 1536], P('tp', ('fsdp', 'ctx'))
The draws below stay inside these ranges and needn't reach their ends.
Inputs may be any that keep to these rules, and one draw needn't show every extreme that they name: `prefix`: each sequence's number of leading bytes that all of its bytes see.
All inputs are finite; a program needn't handle non-finite values.
Results may differ from the reference program's by a relative error of at most 0.019.
Values may be sent and summed in bfloat16 or wider, within the bound.
No kernel may reach another device: no remote copies, remote signals or barrier semaphores. Data moves between devices by JAX's collectives and lax.ppermute only.
A program may use at most 192 MiB of HBM per device.

```python
import jax
import jax.numpy as jnp
from jax import lax

D = 1536
HEADS = 12
HEAD = 64
FF = 3968
NB = 32
INNER = 768
LEN = 512
SEQS = 4


def plant(array, rng, smallest, largest):
    shape = array.shape
    spot = [jax.random.randint(jax.random.fold_in(rng, axis), (), 0, shape[axis]) for axis in range(len(shape))]
    array = array.at[tuple(spot)].set(smallest)
    longest = shape.index(max(shape))
    spot[longest] = (spot[longest] + 1) % shape[longest]
    return array.at[tuple(spot)].set(largest)


def block_scale(own_key, shape, cuts, smallest, high):
    level, own = 1.0, jax.random.fold_in(own_key, 6)
    for axis_at, blocks in cuts:
        heights = jnp.exp(jax.random.uniform(jax.random.fold_in(own, axis_at), (blocks,), jnp.float32, smallest / len(cuts), high / len(cuts)))
        level = level * jnp.repeat(heights, shape[axis_at] // blocks).reshape([-1 if axis == axis_at else 1 for axis in range(len(shape))])
    return level


def noise(key, extent, deviation, limit, shards=(), kind=jnp.bfloat16):
    values = deviation * jax.random.normal(key, extent, jnp.float32)
    if shards:
        values = values * block_scale(key, extent, shards, -0.22, 0.18)
    return jnp.clip(values, -limit, limit).astype(kind)


def setup_inputs(seed: int = 0) -> dict:
    arg_keys = jax.random.split(jax.random.key(seed), 14)
    return {
        "tokens": noise(arg_keys[0], (SEQS, LEN, D), 1.0, 6.0, ((0, 4), (1, 4))),
        "cotangent": noise(arg_keys[1], (SEQS, LEN, D), 1.0, 6.0, ((0, 4), (1, 4))),
        "prefix": plant(jax.random.randint(arg_keys[2], (SEQS,), LEN // 10, LEN // 2 + 1), jax.random.fold_in(arg_keys[2], 1), LEN // 10, (LEN // 2 + 1) - 1).astype(jnp.int32),
        "norm_one": jnp.clip(1.0 + 0.15 * jax.random.normal(arg_keys[3], (D,), jnp.float32), 0.25, 1.75).astype(jnp.bfloat16),
        "w_query": noise(arg_keys[4], (D, INNER), (4 * D) ** -0.5, 0.078125, ((0, 16), (1, 2))),
        "w_key": noise(arg_keys[5], (D, INNER), (4 * D) ** -0.5, 0.078125, ((0, 16), (1, 2))),
        "value_projection_weight": noise(arg_keys[6], (D, INNER), D ** -0.5, 0.15625, ((0, 16), (1, 2))),
        "w_out": noise(arg_keys[7], (INNER, D), (INNER // 32) ** -0.5, 1.25, ((0, 2), (1, 16))),
        "position_bias_matrix": noise(arg_keys[8], (HEADS, NB), 0.5, 3.0, ((0, 2),)),
        "norm_two": jnp.clip(1.0 + 0.15 * jax.random.normal(arg_keys[9], (D,), jnp.float32), 0.25, 1.75).astype(jnp.bfloat16),
        "w_gate": noise(arg_keys[10], (D, FF), D ** -0.5, 0.15625, ((0, 16), (1, 2))),
        "w_up": noise(arg_keys[11], (D, FF), D ** -0.5, 0.15625, ((0, 16), (1, 2))),
        "w_down": noise(arg_keys[12], (FF, D), FF ** -0.5, 0.09375, ((0, 2), (1, 16))),
    }


@jax.custom_vjp
def low(v):
    return lax.optimization_barrier(v.astype(jnp.bfloat16)).astype(jnp.float32)

@jax.custom_vjp
def low_back(v):
    return v

def low_keep(v):
    return (low(v), None)

def low_pass(kept, grad):
    return (grad,)

def back_keep(v):
    return (v, None)

def back_low(kept, grad):
    return (low(grad),)
low.defvjp(low_keep, low_pass)
low_back.defvjp(back_keep, back_low)
epsilon = 1e-06
masked_value = -1e+30
far_bounds = (12, 16, 23, 32, 46, 64, 91)
highest = lax.Precision.HIGHEST

def bucket_of(relative):
    relative_offset = jnp.abs(relative)
    far_bucket = jnp.full(relative_offset.shape, NB // 4, jnp.int32)
    for threshold in far_bounds:
        far_bucket = far_bucket + (relative_offset >= threshold).astype(jnp.int32)
    return jnp.where(relative_offset < NB // 4, relative_offset, far_bucket) + NB // 2 * (relative > 0).astype(jnp.int32)

def rms_norm(values, gain):
    scale = lax.rsqrt(lax.optimization_barrier(jnp.mean(values * values, axis=-1, keepdims=True)) + epsilon)
    return values * scale * gain

def matmul(left, right):
    return jnp.dot(left, right, precision=highest)

def forward(params, inputs, prefix_len):
    gain_one, query_weight, key_weight, value_weight, out_weight, table_rows, gain_two, gate_weight, up_weight, down_weight = params
    length = inputs.shape[0]
    attn_input = low(rms_norm(inputs, gain_one))
    queries = low(low_back(matmul(attn_input, query_weight))).reshape(length, HEADS, HEAD)
    key_rows = low(low_back(matmul(attn_input, key_weight))).reshape(length, HEADS, HEAD)
    values = low(low_back(matmul(attn_input, value_weight))).reshape(length, HEADS, HEAD)
    block_rows = min(512, length)
    key_pos = jnp.arange(length, dtype=jnp.int32)

    def attend(block_start):
        query_block = lax.dynamic_slice_in_dim(queries, block_start, block_rows, 0)
        query_pos = block_start + jnp.arange(block_rows, dtype=jnp.int32)
        relative = key_pos[None, :] - query_pos[:, None]
        raw_scores = jnp.einsum('qhe,khe->hqk', query_block, key_rows, precision=highest) + table_rows[:, bucket_of(relative)]
        scores = low_back(raw_scores)
        allowed = (key_pos[None, :] <= query_pos[:, None]) | (key_pos[None, :] < prefix_len)
        scores = jnp.where(allowed[None], scores, masked_value)
        weights = low(jax.nn.softmax(scores, axis=-1))
        attended = jnp.einsum('hqk,khe->qhe', weights, values, precision=highest)
        return low(low_back(attended)).reshape(block_rows, HEADS * HEAD)
    starts = (jnp.arange(length // block_rows) * block_rows).astype(jnp.int32)
    attended = lax.map(jax.checkpoint(attend), starts).reshape(length, HEADS * HEAD)
    residual = inputs + low_back(matmul(attended, out_weight))
    ffn_input = low(rms_norm(residual, gain_two))
    gate_value = low_back(matmul(ffn_input, gate_weight))
    up_value = low_back(matmul(ffn_input, up_weight))
    hidden = low(jax.nn.gelu(gate_value, approximate=True) * up_value)
    return residual + low_back(matmul(hidden, down_weight))

def reference(tokens, cotangent, prefix, norm_one, w_query, w_key, value_projection_weight, w_out, position_bias_matrix, norm_two, w_gate, w_up, w_down):
    params = tuple((weight_arg.astype(jnp.float32) for weight_arg in (norm_one, w_query, w_key, value_projection_weight, w_out, position_bias_matrix, norm_two, w_gate, w_up, w_down)))

    def single_sequence(totals, token_sequence):
        inputs, out_grad, prefix_len = token_sequence
        mixed, pull_back = jax.vjp(lambda weights_now, values_now: forward(weights_now, values_now, prefix_len), params, inputs.astype(jnp.float32))
        weight_grads, inputs_grad = pull_back(out_grad.astype(jnp.float32))
        totals = jax.tree.map(lambda left, right: left + right, totals, weight_grads)
        return (totals, (mixed.astype(jnp.bfloat16), inputs_grad.astype(jnp.bfloat16)))
    zeros = tuple((jnp.zeros(weight_arg.shape, jnp.float32) for weight_arg in params))
    totals, outputs = lax.scan(single_sequence, zeros, (tokens, cotangent, prefix))
    mixed, input_grad = outputs
    return (mixed, input_grad, totals[0], totals[1], totals[2], totals[3], totals[4], totals[5], totals[6], totals[7], totals[8], totals[9])
```

```python
import functools

import jax
import jax.numpy as jnp
from jax import lax
from jax.experimental import pallas as pl
from jax.experimental.pallas import tpu as pltpu
from jax.sharding import Mesh, PartitionSpec as P

epsilon = 1e-06
masked_value = -1e30
far_bounds = (12, 16, 23, 32, 46, 64, 91)
f32 = jnp.float32
bf16 = jnp.bfloat16
Z = ("zh", "zl")


def bucket_of(relative, buckets):
    offset = jnp.abs(relative)
    far = jnp.full(offset.shape, buckets // 4, jnp.int32)
    for threshold in far_bounds:
        far = far + (offset >= threshold).astype(jnp.int32)
    return jnp.where(offset < buckets // 4, offset, far) + buckets // 2 * (relative > 0).astype(
        jnp.int32
    )


def dot(left, right, dims=((1,), (0,))):
    return lax.dot_general(left, right, (dims, ((), ())), preferred_element_type=f32)


def dot_nt(left, right):
    return dot(left, right, ((1,), (1,)))


def dot_tn(left, right):
    return dot(left, right, ((0,), (0,)))


def fetch(value, axis, step):
    size = lax.axis_size(axis)
    return lax.ppermute(value, axis, [((i + step) % size, i) for i in range(size)])


def gather(value, axis):
    return [value] + [fetch(value, axis, e) for e in range(1, lax.axis_size(axis))]


def scatter(pieces, axis):
    size = lax.axis_size(axis)
    total = pieces[0]
    for e in range(1, size):
        total = total + fetch(pieces[e].astype(bf16), axis, size - e).astype(f32)
    return total


def place(pieces, axis):
    size, here = len(pieces), lax.axis_index(axis)
    if size == 1:
        return pieces[0][None]
    if size == 2:
        first = here == 0
        return jnp.stack(
            [jnp.where(first, pieces[0], pieces[1]), jnp.where(first, pieces[1], pieces[0])]
        )
    stack = jnp.zeros((size, *pieces[0].shape), pieces[0].dtype)
    for e, piece in enumerate(pieces):
        stack = lax.dynamic_update_slice_in_dim(stack, piece[None], (here + e) % size, 0)
    return stack


def pick(stack, axis, step=0):
    size = lax.axis_size(axis)
    if size == 1:
        return stack[0]
    here = (lax.axis_index(axis) + step) % size
    if size == 2:
        return jnp.where(here == 0, stack[0], stack[1])
    return lax.dynamic_index_in_dim(stack, here, 0, keepdims=False)


def pair_sum(value, axis):
    rounded = value.astype(bf16)
    return rounded.astype(f32) + fetch(rounded, axis, 1).astype(f32)


def inv_scale(values):
    return lax.rsqrt(jnp.mean(values * values, axis=-1, keepdims=True) + epsilon)


def norm_back(scale, normed, grad_normed):
    return scale * (grad_normed - normed * jnp.mean(grad_normed * normed, axis=-1, keepdims=True))


def gelu_tanh(values):
    return jax.nn.gelu(values, approximate=True)


def bias_block(line_ref, head, start, rows):
    line = line_ref[pl.ds(head, 1), pl.ds(pl.multiple_of(start, rows), 2 * rows)]
    spread = jnp.broadcast_to(line, (rows, 2 * rows))
    return pltpu.roll(spread, 0, 1, stride=1, stride_axis=0)[:, rows:]


def attend_kernel(sizes, place_ref, qkv_ref, line_ref, probs_ref, attended_ref):
    rows, heads, width, query_blocks, key_blocks, span = sizes
    prefix = place_ref[key_blocks]
    inner = heads * width
    for head in range(heads):
        lanes = slice(head * width, (head + 1) * width)
        keys = qkv_ref[:, inner + head * width : inner + (head + 1) * width]
        values = qkv_ref[:, 2 * inner + head * width : 2 * inner + (head + 1) * width]
        for at, block in enumerate(query_blocks):
            query_block = place_ref[block]
            queries = qkv_ref[block * rows : (block + 1) * rows, lanes]
            raw = dot_nt(queries, keys)
            query_pos = query_block * rows + lax.broadcasted_iota(jnp.int32, (rows, rows), 0)
            parts = []
            for key_at in range(key_blocks):
                key_block = place_ref[key_at]
                start = (key_block - query_block) * rows + span - rows
                key_pos = key_block * rows + lax.broadcasted_iota(jnp.int32, (rows, rows), 1)
                allowed = (key_pos <= query_pos) | (key_pos < prefix)
                biased = raw[:, key_at * rows : (key_at + 1) * rows] + bias_block(
                    line_ref, head, start, rows
                )
                parts.append(jnp.where(allowed, biased, masked_value))
            scores = jnp.concatenate(parts, axis=1)
            top = jnp.max(scores, axis=1, keepdims=True)
            powers = jnp.exp(scores - top)
            probs = powers / jnp.sum(powers, axis=1, keepdims=True)
            probs_ref[head, at * rows : (at + 1) * rows, :] = probs
            attended_ref[at * rows : (at + 1) * rows, lanes] = dot(
                probs.astype(bf16), values
            ).astype(bf16)


def attend_back_kernel(
    sizes, place_ref, qkv_ref, probs_ref, d_attended_ref, d_query_ref, d_keys_ref, lines_ref
):
    rows, heads, width, query_blocks, key_blocks, span = sizes
    inner = heads * width
    lines_ref[...] = jnp.zeros_like(lines_ref)
    up, down = (lax.broadcasted_iota(jnp.int32, (rows, rows), axis) for axis in (0, 1))
    flip = (up + down == rows - 1).astype(bf16)
    for head in range(heads):
        lanes = slice(head * width, (head + 1) * width)
        keys = qkv_ref[:, inner + head * width : inner + (head + 1) * width]
        values = qkv_ref[:, 2 * inner + head * width : 2 * inner + (head + 1) * width]
        d_key, d_value = None, None
        for at, block in enumerate(query_blocks):
            query_block = place_ref[block]
            queries = qkv_ref[block * rows : (block + 1) * rows, lanes]
            d_attended = d_attended_ref[at * rows : (at + 1) * rows, lanes]
            probs = probs_ref[head, at * rows : (at + 1) * rows, :]
            d_probs = dot_nt(d_attended, values)
            delta = jnp.sum(probs * d_probs, axis=1, keepdims=True)
            d_scores = (probs * (d_probs - delta)).astype(bf16)
            d_query_ref[at * rows : (at + 1) * rows, lanes] = dot(d_scores, keys).astype(bf16)
            key_part = dot_tn(d_scores, queries)
            value_part = dot_tn(probs.astype(bf16), d_attended)
            d_key = key_part if d_key is None else d_key + key_part
            d_value = value_part if d_value is None else d_value + value_part
            upward = dot(flip, d_scores)
            for key_at in range(key_blocks):
                start = (place_ref[key_at] - query_block) * rows + span - rows
                piece = upward[:, key_at * rows : (key_at + 1) * rows]
                padded = jnp.concatenate([piece, jnp.zeros_like(piece)], axis=1)
                turned = pltpu.roll(padded, 1, 1, stride=1, stride_axis=0)
                where = pl.ds(pl.multiple_of(start, rows), 2 * rows)
                lines_ref[pl.ds(head, 1), where] += jnp.sum(turned, axis=0, keepdims=True)
        d_keys_ref[:, lanes] = d_key
        d_keys_ref[:, inner + head * width : inner + (head + 1) * width] = d_value


VMEM = pl.BlockSpec(memory_space=pltpu.VMEM)
SMEM = pl.BlockSpec(memory_space=pltpu.SMEM)


def attend(sizes, places, qkv, lines):
    rows, heads, width, query_blocks, key_blocks, span = sizes
    queries = len(query_blocks) * rows
    return pl.pallas_call(
        functools.partial(attend_kernel, sizes),
        out_shape=(
            jax.ShapeDtypeStruct((heads, queries, span), f32),
            jax.ShapeDtypeStruct((queries, heads * width), bf16),
        ),
        in_specs=[SMEM, VMEM, VMEM],
        out_specs=(VMEM, VMEM),
        name="attend",
    )(places, qkv, lines)


def attend_back(sizes, places, qkv, probs, d_attended):
    rows, heads, width, query_blocks, key_blocks, span = sizes
    queries = len(query_blocks) * rows
    return pl.pallas_call(
        functools.partial(attend_back_kernel, sizes),
        out_shape=(
            jax.ShapeDtypeStruct((queries, heads * width), bf16),
            jax.ShapeDtypeStruct((span, 2 * heads * width), f32),
            jax.ShapeDtypeStruct((8, 2 * span), f32),
        ),
        in_specs=[SMEM, VMEM, VMEM, VMEM],
        out_specs=(VMEM, VMEM, VMEM),
        name="attend_back",
    )(places, qkv, probs, d_attended)


def hold(value, *others):
    return lax.optimization_barrier((value, *others))[0]


def local(
    tokens,
    cotangent,
    prefix,
    norm_one,
    w_query,
    w_key,
    w_value,
    w_out,
    position_bias_matrix,
    norm_two,
    w_gate,
    w_up,
    w_down,
):
    outer = lax.axis_size("yh")
    deep = lax.axis_size("zh")
    rows, wide = tokens.shape[1:]
    part = w_query.shape[0]
    heads_dev, buckets = position_bias_matrix.shape
    heads = heads_dev // 2
    width = w_query.shape[1] // heads_dev
    inner = heads * width
    hidden_dev = w_gate.shape[1]
    quarter = -(-hidden_dev // 512) * 128
    length = rows * outer * 4

    mats = [w_query, w_key, w_value, w_out.T]
    packs = jnp.stack(
        [jnp.concatenate([m[:, h * inner : (h + 1) * inner] for m in mats], 1) for h in range(2)]
    )
    pack = place([pick(packs, "yl"), fetch(pick(packs, "yl", 1), "yl", 1)], "yl")
    pack_here = pack
    for axis in ("zh", "zl", "yh", "k"):
        pack = place(gather(pack, axis), axis)
        if axis == "zl":
            pack_deep = pack
    attn_w = pack.transpose(3, 2, 1, 4, 0, 5, 6).reshape(wide, 4 * inner)
    qkv_w, out_w = attn_w[:, : 3 * inner], attn_w[:, 3 * inner :]

    gains = jnp.stack([norm_one, norm_two])
    for axis in ("k", "yl", "yh", "zl", "zh"):
        gains = place(gather(gains, axis), axis)
    gains = gains.transpose(5, 0, 1, 2, 3, 4, 6).reshape(2, wide).astype(f32)
    gain_one, gain_two = gains[:1], gains[1:]

    token_rows = [tokens[0]]
    for axis in ("yl", "yh"):
        token_rows = [piece for group in zip(*[gather(b, axis) for b in token_rows]) for piece in group]
    token_rows = jnp.stack(token_rows)
    token_rows = jnp.stack(gather(token_rows, "k"), 1).reshape(length, wide)
    token_rows = token_rows.astype(f32)
    attn_input = (token_rows * inv_scale(token_rows) * gain_one).astype(bf16)
    yh, yl, k = (lax.axis_index(a) for a in ("yh", "yl", "k"))
    places = jnp.stack(
        [
            ((yh + e) % outer) * 4 + ((yl + a) % 2) * 2 + (k + b) % 2
            for e in range(outer)
            for a in range(2)
            for b in range(2)
        ]
        + [prefix[0]]
    ).astype(jnp.int32)
    sizes = (rows, heads, width, (0, 2), 4 * outer, length)

    table = pick(position_bias_matrix.reshape(2, heads, buckets), "yl")
    distance = jnp.arange(2 * length, dtype=jnp.int32) - length
    indicator = (
        bucket_of(distance, buckets)[None] == jnp.arange(buckets, dtype=jnp.int32)[:, None]
    ).astype(f32)
    lines = jnp.einsum("hb,bd->hd", table.astype(f32), indicator, precision="highest")
    lines = jnp.pad(lines, ((0, 8 - heads), (0, 0)))

    pad = ((0, 0), (0, 4 * quarter - hidden_dev))
    mats = [jnp.pad(m, pad) for m in (w_gate, w_up, w_down.T)]
    halves = jnp.stack(
        [
            jnp.stack([m[:, (2 * h + c) * quarter : (2 * h + c + 1) * quarter] for h in range(2) for m in mats])
            for c in range(2)
        ]
    )
    mine = place([pick(halves, "k"), fetch(pick(halves, "k", 1), "k", 1)], "k")
    mine = mine.reshape(2, 2, 3, part, quarter).transpose(2, 1, 0, 3, 4).reshape(3, 2, 2 * part, quarter)

    def level_zl(m):
        return place([pick(mine[m], "zl"), fetch(pick(mine[m], "zl", 1), "zl", 1)], "zl")

    def level_zh(value):
        return place(gather(value, "zh"), "zh")

    def level_y(value):
        for axis in ("yl", "yh"):
            value = place(gather(value, axis), axis)
        return value.transpose(2, 3, 0, 1, 4, 5).reshape(wide, quarter)

    near = [hold(level_zl(m), pack_here) for m in range(3)]
    far_gate = level_zh(hold(near[0], pack_deep))
    qkv = dot(attn_input, qkv_w).astype(bf16)
    probs, attended = attend(sizes, places, qkv, lines)
    out_part = dot_nt(attended, out_w)
    out_part, far_gate = lax.optimization_barrier((out_part, far_gate))
    far_up = level_zh(hold(near[1], far_gate))
    out_sum = scatter([out_part[:rows], out_part[rows:]], "yl")
    out_sum, far_up = lax.optimization_barrier((out_sum, far_up))
    far_down = level_zh(hold(near[2], far_up))
    gate_w = level_y(hold(far_gate, out_sum))
    inputs = tokens[0].astype(f32)
    residual = inputs + pair_sum(out_sum, "x")
    scale_two = inv_scale(residual)
    normed_two = residual * scale_two
    low_two = (normed_two * gain_two).astype(bf16)
    low_two, far_down, gate_w = lax.optimization_barrier((low_two, far_down, gate_w))
    up_w = level_y(hold(far_up, low_two))

    def spread(value):
        further = fetch(value, "zl", 1)
        return jnp.concatenate([value, fetch(value, "k", 1), further, fetch(further, "k", 1)], 0)

    def join(total):
        total = total.reshape(2, 2, rows, wide)
        core = [total[a, 0] + fetch(total[a, 1].astype(bf16), "k", 1).astype(f32) for a in range(2)]
        return pair_sum(scatter(core, "zl"), "x")

    ffn_rows = spread(low_two)
    ffn_rows, up_w = lax.optimization_barrier((ffn_rows, up_w))
    down_w = level_y(hold(far_down, up_w))
    grad_rows = spread(hold(cotangent[0], ffn_rows))
    gate_value = dot(ffn_rows, gate_w)
    up_value = dot(ffn_rows, up_w)
    activated, gelu_pull = jax.vjp(gelu_tanh, gate_value)
    hidden = (activated * up_value).astype(bf16)
    d_hidden = dot(grad_rows, down_w)
    d_gate = gelu_pull(d_hidden * up_value)[0].astype(bf16)
    d_up = (d_hidden * activated).astype(bf16)
    d_ffn = join(dot_nt(d_gate, gate_w) + dot_nt(d_up, up_w))
    d_residual = cotangent[0].astype(f32) + norm_back(scale_two, normed_two, d_ffn * gain_two)
    d_attn = d_residual.astype(bf16)

    def grad_y(left, right):
        total = dot_tn(left, right).reshape(deep, 2, outer, 2, 2 * part, quarter)
        total = total.transpose(3, 2, 0, 1, 4, 5)
        total = scatter([pick(total, "yl", e) for e in range(2)], "yl")
        return scatter([pick(total, "yh", e) for e in range(outer)], "yh")

    def grad_z(total):
        total = scatter([pick(total, "zh", e) for e in range(deep)], "zh")
        other = fetch(pick(total, "zl", 1).astype(bf16), "zl", 1).astype(f32)
        total = place([pick(total, "zl"), other], "zl")
        return total.reshape(2, 2, part, quarter).transpose(1, 0, 2, 3)

    grads = [grad_y(grad_rows, hidden), grad_y(ffn_rows, d_gate), grad_y(ffn_rows, d_up)]
    grads = jnp.stack([grad_z(g) for g in grads], 1)
    grads = place([pick(grads, "k"), fetch(pick(grads, "k", 1), "k", 1)], "k")
    grads = grads.transpose(1, 3, 2, 0, 4).reshape(3, part, 4 * quarter)[:, :, :hidden_dev]
    grad_down, grad_gate, grad_up = grads[0].T, grads[1], grads[2]
    gain_two_part = jnp.sum(
        grad_gate * w_gate.astype(f32) + grad_up * w_up.astype(f32), axis=1
    ) / norm_two.astype(f32)

    d_rows = jnp.concatenate([d_attn, fetch(d_attn, "yl", 1)], 0)
    d_attended = dot(d_rows, out_w).astype(bf16)
    d_query, d_keys, d_lines = attend_back(sizes, places, qkv, probs, d_attended)
    d_keys = d_keys.reshape(outer, 2, 2, rows, 2 * inner)
    d_keys = scatter([d_keys[:, :, b] for b in range(2)], "k")
    d_keys = scatter([d_keys[e] for e in range(outer)], "yh").reshape(2 * rows, 2 * inner)
    d_qkv = jnp.concatenate([d_query, d_keys.astype(bf16)], 1)
    two_rows = jnp.concatenate([attn_input[:rows], attn_input[2 * rows : 3 * rows]], 0)
    g_part = dot_nt(d_qkv, qkv_w)
    d_attn_input = pair_sum(scatter([g_part[:rows], g_part[rows:]], "yl"), "x")
    scale_one = inv_scale(inputs)
    input_grad = d_residual + norm_back(scale_one, inputs * scale_one, d_attn_input * gain_one)
    input_grad = input_grad.astype(bf16)

    ffn_sum = join(hold(dot_nt(hidden, down_w), d_rows))
    mixed = (residual + ffn_sum).astype(bf16)

    attn_grad = jnp.concatenate([dot_tn(two_rows, d_qkv), dot_tn(d_rows, attended)], 1)
    attn_grad = attn_grad.reshape(deep, 2, outer, 2, 2, part, 4 * inner)
    attn_grad = attn_grad.transpose(4, 2, 1, 0, 3, 5, 6)
    for axis, count in (("k", 2), ("yh", outer), ("zl", 2), ("zh", deep)):
        attn_grad = scatter([pick(attn_grad, axis, e) for e in range(count)], axis)
    attn_grad = place([pick(attn_grad, "yl"), fetch(pick(attn_grad, "yl", 1), "yl", 1)], "yl")
    attn_grad = attn_grad.reshape(2, part, 4, inner).transpose(2, 1, 0, 3).reshape(4, part, 2 * inner)
    weights = jnp.stack([w_query, w_key, w_value]).astype(f32)
    gain_one_part = jnp.sum(attn_grad[:3] * weights, axis=(0, 2)) / norm_one.astype(f32)
    grad_gains = jnp.stack([gain_one_part, gain_two_part])
    grad_gains = grad_gains + fetch(grad_gains, "x", 1)

    grad_table = jnp.einsum("hd,bd->hb", d_lines[:heads], indicator, precision="highest")
    for axis in ("k", "yh", "zl", "zh"):
        grad_table = jnp.sum(place(gather(grad_table, axis), axis), axis=0)
    grad_table = place(gather(grad_table, "yl"), "yl").reshape(heads_dev, buckets)
    return (
        mixed[None],
        input_grad[None],
        grad_gains[0],
        attn_grad[0],
        attn_grad[1],
        attn_grad[2],
        attn_grad[3].T,
        grad_table,
        grad_gains[1],
        grad_gate,
        grad_up,
        grad_down,
    )


def solution(mesh):
    depths, lines, halves = (mesh.shape[a] for a in ("fsdp", "ctx", "tp"))
    fine = Mesh(
        mesh.devices.reshape(depths // 2, 2, lines // 4, 2, 2, halves),
        ("zh", "zl", "yh", "yl", "k", "x"),
    )
    line = ("yh", "yl", "k")
    every = (*Z, *line)
    in_specs = (
        P(Z, line, None),
        P(Z, line, None),
        P(Z),
        P(every),
        P(every, "x"),
        P(every, "x"),
        P(every, "x"),
        P("x", every),
        P("x", None),
        P(every),
        P(every, "x"),
        P(every, "x"),
        P("x", every),
    )
    out_specs = (
        P(Z, line, None),
        P(Z, line, None),
        P(every),
        P(every, "x"),
        P(every, "x"),
        P(every, "x"),
        P("x", every),
        P("x", None),
        P(every),
        P(every, "x"),
        P(every, "x"),
        P("x", every),
    )
    return jax.shard_map(local, mesh=fine, in_specs=in_specs, out_specs=out_specs, check_vma=False)
```

```python
import functools

import jax
import jax.numpy as jnp
import numpy as np
from jax import lax
from jax.experimental import pallas as pl
from jax.experimental.pallas import tpu as pltpu
from jax.sharding import Mesh, PartitionSpec as P

epsilon = 1e-06
masked_value = -1e30
far_bounds = (12, 16, 23, 32, 46, 64, 91)
f32 = jnp.float32
bf16 = jnp.bfloat16
lane = 128
ffn_order = (2, 3, 0, 1, 4, 5)
attn_order = (4, 2, 1, 0, 3, 5)
at_k, at_yl, at_zl, at_zh, at_yh, at_prefix, at_lists = range(7)


def bucket_of(relative, buckets):
    offset = jnp.abs(relative)
    far = jnp.full(offset.shape, buckets // 4, jnp.int32)
    for threshold in far_bounds:
        far = far + (offset >= threshold).astype(jnp.int32)
    return jnp.where(offset < buckets // 4, offset, far) + buckets // 2 * (relative > 0).astype(
        jnp.int32
    )


def dot(left, right, dims=((1,), (0,))):
    return lax.dot_general(left, right, (dims, ((), ())), preferred_element_type=f32)


def dot_nt(left, right):
    return dot(left, right, ((1,), (1,)))


def dot_tn(left, right):
    return dot(left, right, ((0,), (0,)))


def fetch(value, axis, step):
    size = lax.axis_size(axis)
    return lax.ppermute(value, axis, [((i + step) % size, i) for i in range(size)])


def swap(value, axis):
    return fetch(value, axis, 1)


def gather(value, axis):
    return [value] + [fetch(value, axis, e) for e in range(1, lax.axis_size(axis))]


def send_sums(sends, axis):
    size = lax.axis_size(axis)
    return [fetch(sends[e - 1], axis, size - e) for e in range(1, size)]


def place(pieces, axis):
    size, here = len(pieces), lax.axis_index(axis)
    if size == 1:
        return pieces[0][None]
    if size == 2:
        first = here == 0
        return jnp.stack(
            [jnp.where(first, pieces[0], pieces[1]), jnp.where(first, pieces[1], pieces[0])]
        )
    stack = jnp.zeros((size, *pieces[0].shape), pieces[0].dtype)
    for e, piece in enumerate(pieces):
        stack = lax.dynamic_update_slice_in_dim(stack, piece[None], (here + e) % size, 0)
    return stack


def both(value, axis):
    return place(gather(value, axis), axis)


class Clock:
    def __init__(self, token):
        self.token = token

    def tick(self, *values):
        self.token, *values = lax.optimization_barrier((self.token, *values))
        return values


def runs_of(dims, order, inverse):
    index = np.arange(int(np.prod(dims))).reshape(dims).transpose(order).reshape(-1)
    if inverse:
        index = np.argsort(index)
    cuts = [0, *(np.flatnonzero(np.diff(index) != 1) + 1).tolist(), len(index)]
    return [(int(index[a]), int(index[a]) + b - a) for a, b in zip(cuts[:-1], cuts[1:])]


def reorder(value, dims, order, inverse=False):
    return jnp.concatenate([value[:, a:b] for a, b in runs_of(dims, order, inverse)], axis=1)


def inv_scale(values):
    return lax.rsqrt(jnp.mean(values * values, axis=-1, keepdims=True) + epsilon)


def norm_back(scale, normed, grad_normed):
    return scale * (grad_normed - normed * jnp.mean(grad_normed * normed, axis=-1, keepdims=True))


def aligned(index, size):
    return pl.ds(pl.multiple_of(index * size, size), size)


def call(body, name, here, arrays, outs, scratch=(), **static):
    space = pl.BlockSpec(memory_space=pltpu.VMEM)
    return pl.pallas_call(
        functools.partial(body, **static),
        out_shape=tuple(jax.ShapeDtypeStruct(shape, kind) for shape, kind in outs),
        in_specs=[pl.BlockSpec(memory_space=pltpu.SMEM)] + [space] * len(arrays),
        out_specs=tuple(space for _ in outs),
        scratch_shapes=scratch,
        name=name,
    )(here, *arrays)


def pack_attn_body(here, wq, wk, wv, wo, own, send):
    half = wq.shape[1] // 2
    mats = [wq[...], wk[...], wv[...], wo[...].astype(f32).T.astype(bf16)]
    low = jnp.concatenate([m[:, :half] for m in mats], axis=1)
    high = jnp.concatenate([m[:, half:] for m in mats], axis=1)

    @pl.when(here[at_yl] == 0)
    def _():
        own[...] = low
        send[...] = high

    @pl.when(here[at_yl] != 0)
    def _():
        own[...] = high
        send[...] = low


def pack_ffn_body(here, wg, wu, wd, own, send, room, *, chunks):
    hidden = wg.shape[1]
    whole = hidden // lane * lane
    room[:, :, whole:] = jnp.zeros((3, wg.shape[0], 4 * chunks * lane - whole), bf16)
    room[0, :, :hidden] = wg[...]
    room[1, :, :hidden] = wu[...]
    room[2, :, :hidden] = wd[...].astype(f32).T.astype(bf16)
    for out, core in ((own, here[at_k]), (send, 1 - here[at_k])):
        for h in range(2):
            for j in range(chunks):
                for m in range(3):
                    out[h, j, :, m * lane : (m + 1) * lane] = room[
                        m, :, aligned((2 * h + core) * chunks + j, lane)
                    ]


def place_ffn_body(here, own, got, near, other, *, chunks):
    k, zl = here[at_k], here[at_zl]
    for j in range(chunks):
        near[j, k] = own[zl, j]
        near[j, 1 - k] = got[zl, j]
        other[j, k] = own[1 - zl, j]
        other[j, 1 - k] = got[1 - zl, j]


def place_zl_body(here, near, got, *outs):
    zl = here[at_zl]
    for j, out in enumerate(outs):
        out[zl] = near[j]
        out[1 - zl] = got[j]


def rows_body(here, gain, cotangent, *refs, dims):
    *blocks, out, low_grad = refs
    rows = cotangent.shape[0]
    low_grad[...] = reorder(cotangent[...].astype(f32), dims, ffn_order).astype(bf16)
    for at, block in enumerate(blocks):
        values = block[...].astype(f32)
        values = values * inv_scale(values) * gain[...]
        out[at * rows : (at + 1) * rows] = reorder(values, dims, attn_order).astype(bf16)


def bias_block(line_ref, head, start, rows):
    line = line_ref[pl.ds(head, 1), pl.ds(pl.multiple_of(start, rows), 2 * rows)]
    spread = jnp.broadcast_to(line, (rows, 2 * rows))
    return pltpu.roll(spread, 0, 1, stride=1, stride_axis=0)[:, rows:]


def attend_body(
    here, inputs, w_own, w_other, lines, qkv, probs_out, attended, keep, send, *, sizes
):
    rows, heads, width, query_blocks, key_blocks, span = sizes
    prefix = here[at_prefix]
    inner = heads * width
    half = w_own.shape[0]
    places = [here[at_lists + i] for i in range(key_blocks)]
    mine, other = aligned(here[at_k], half), aligned(1 - here[at_k], half)
    qkv[...] = (
        dot(inputs[:, mine], w_own[:, : 3 * inner]) + dot(inputs[:, other], w_other[:, : 3 * inner])
    ).astype(bf16)
    for head in range(heads):
        lanes = slice(head * width, (head + 1) * width)
        keys = qkv[:, inner + head * width : inner + (head + 1) * width]
        values = qkv[:, 2 * inner + head * width : 2 * inner + (head + 1) * width]
        for at, block in enumerate(query_blocks):
            query_block = places[block]
            queries = qkv[block * rows : (block + 1) * rows, lanes]
            raw = dot_nt(queries, keys)
            query_pos = query_block * rows + lax.broadcasted_iota(jnp.int32, (rows, rows), 0)
            parts = []
            for key_at, key_block in enumerate(places):
                start = (key_block - query_block) * rows + span - rows
                key_pos = key_block * rows + lax.broadcasted_iota(jnp.int32, (rows, rows), 1)
                allowed = (key_pos <= query_pos) | (key_pos < prefix)
                biased = raw[:, key_at * rows : (key_at + 1) * rows] + bias_block(
                    lines, head, start, rows
                )
                parts.append(jnp.where(allowed, biased, masked_value))
            scores = jnp.concatenate(parts, axis=1)
            top = jnp.max(scores, axis=1, keepdims=True)
            powers = jnp.exp(scores - top)
            probs = powers / jnp.sum(powers, axis=1, keepdims=True)
            probs_out[head, at * rows : (at + 1) * rows, :] = probs
            attended[at * rows : (at + 1) * rows, lanes] = dot(probs.astype(bf16), values).astype(
                bf16
            )
    for lanes, weights in ((mine, w_own), (other, w_other)):
        out = dot_nt(attended[...], weights[:, 3 * inner :])
        keep[:, lanes] = out[:rows]
        send[:, lanes] = out[rows:].astype(bf16)


def norm_body(here, own, got, tokens, gain, residual, low, *, dims):
    total = own[...].astype(f32) + got[...].astype(f32)
    values = tokens[...].astype(f32) + reorder(total, dims, attn_order, True)
    residual[...] = values
    low[...] = reorder(values * inv_scale(values) * gain[...], dims, ffn_order).astype(bf16)


def tall(refs, lanes):
    return jnp.concatenate([ref[:, lanes] for ref in refs], axis=0)


def ffn_body(here, *refs, where):
    rows, grads, weights, (first_out, hidden_out) = refs[:4], refs[4:8], refs[8:-2], refs[-2:]
    size = weights[0].shape[0]
    first, d_hidden = None, None
    for at, w in enumerate(weights):
        lanes = aligned(here[where + at], size)
        first_part = dot(tall(rows, lanes), w[:, : 2 * lane])
        d_part = dot(tall(grads, lanes), w[:, 2 * lane :])
        first = first_part if first is None else first + first_part
        d_hidden = d_part if d_hidden is None else d_hidden + d_part
    gate, up = first[:, :lane], first[:, lane:]
    root = float(np.sqrt(2.0 / np.pi))
    square = gate * gate
    bend = jnp.tanh(root * gate * (1.0 + 0.044715 * square))
    half = 0.5 * (1.0 + bend)
    active = gate * half
    slope = half + 0.5 * gate * (1.0 - bend * bend) * (root * (1.0 + 3.0 * 0.044715 * square))
    hidden_out[...] = (active * up).astype(bf16)
    first_out[:, :lane] = (d_hidden * up * slope).astype(bf16)
    first_out[:, lane:] = (d_hidden * active).astype(bf16)


def back_body(here, *refs, where, chunks, lanes):
    lefts, weights, (keep, send) = refs[:chunks], refs[chunks:-2], refs[-2:]
    blocks = len(weights) // chunks
    size, rows = weights[0].shape[0], keep.shape[1]
    for at in range(blocks):
        total = None
        for j in range(chunks):
            part = dot_nt(lefts[j][...], weights[j * blocks + at][:, lanes])
            total = part if total is None else total + part
        here_lanes = aligned(here[where + at], size)
        for a in range(2):
            keep[a, :, here_lanes] = total[2 * a * rows : (2 * a + 1) * rows]
            send[a, :, here_lanes] = total[(2 * a + 1) * rows : (2 * a + 2) * rows].astype(bf16)


def ffn_grad_body(here, *refs, outer):
    rows, grads, (first, hidden, keep, send) = refs[:4], refs[4:8], refs[8:]
    size = keep.shape[1]
    for e in range(outer):
        yh = here[at_yh] + e
        yh = jnp.where(yh >= outer, yh - outer, yh) * 2
        for out, y in ((keep, yh + here[at_yl]), (send, yh + 1 - here[at_yl])):
            lanes = aligned(y, size)
            out[e, :, : 2 * lane] = dot_tn(tall(rows, lanes), first[...]).astype(out.dtype)
            out[e, :, 2 * lane :] = dot_tn(tall(grads, lanes), hidden[...]).astype(out.dtype)


def split_body(here, own, *refs, which):
    *got, keep, send = refs
    count = own.shape[0]
    for e in range(count):
        at = here[which] + e
        at = jnp.where(at >= count, at - count, at)
        total = own[at]
        for ref in got:
            total = total + ref[at].astype(f32)
        if e:
            send[e - 1] = total.astype(bf16)
        else:
            keep[...] = total


def split(here, which, own, got):
    shape = own.shape[1:]
    return call(
        split_body,
        "split",
        here,
        [own, *(g.reshape(own.shape) for g in got)],
        [(shape, f32), ((own.shape[0] - 1, *shape), bf16)],
        which=which,
    )


def ffn_split_body(here, *refs, chunks):
    done, core, other = refs[-3:]
    each = (len(refs) - 3) // chunks
    zl, k = here[at_zl], here[at_k]
    for j in range(chunks):
        own, *got = refs[j * each : (j + 1) * each]

        def total(depth, slice_):
            value = own[depth, slice_]
            for ref in got:
                value = value + ref[depth, slice_].astype(f32)
            return value

        done[j] = total(zl, k)
        core[j] = total(zl, 1 - k).astype(bf16)
        other[j, 0] = total(1 - zl, 0).astype(bf16)
        other[j, 1] = total(1 - zl, 1).astype(bf16)


def ffn_final_body(here, done, core, other, far, wg, wu, gain, grad_g, grad_u, grad_d, grad_gain, room):
    chunks, part, hidden = done.shape[0], done.shape[1], wg.shape[1]
    zl, k = here[at_zl], here[at_k]
    for j in range(chunks):
        for h, c, value in (
            (zl, k, done[j]),
            (1 - zl, k, other[j, k].astype(f32)),
            (zl, 1 - k, core[j].astype(f32)),
            (1 - zl, 1 - k, far[j, k].astype(f32)),
        ):
            for m in range(3):
                room[m, :, aligned((2 * h + c) * chunks + j, lane)] = value[
                    :, m * lane : (m + 1) * lane
                ]
    gate, up = room[0, :, :hidden], room[1, :, :hidden]
    grad_g[...] = gate
    grad_u[...] = up
    grad_d[...] = room[2].T[:hidden]
    sums = gate * wg[...].astype(f32) + up * wu[...].astype(f32)
    grad_gain[...] = jnp.sum(sums, axis=1, keepdims=True) / gain[...]


def pair_body(here, own, got, keep, send):
    keep[...] = own[0] + got[0].astype(f32)
    send[...] = (own[1] + got[1].astype(f32)).astype(bf16)


def residual_back_body(here, own, got, residual, cotangent, gain, d_residual, d_low, *, dims):
    total = own[...].astype(f32) + got[...].astype(f32)
    grad_normed = reorder(total, dims, ffn_order, True) * gain[...]
    values = residual[...]
    scale = inv_scale(values)
    back = cotangent[...].astype(f32) + norm_back(scale, values * scale, grad_normed)
    d_residual[...] = back
    d_low[...] = reorder(back, dims, attn_order).astype(bf16)


def attend_back_body(
    here, qkv, probs_in, d_own, d_far, w_own, w_other, d_query, d_keep, d_send, lines, d_att, *, sizes
):
    rows, heads, width, query_blocks, key_blocks, span = sizes
    inner = heads * width
    half = w_own.shape[0]
    places = [here[at_lists + i] for i in range(key_blocks)]
    mine, other = aligned(here[at_k], half), aligned(1 - here[at_k], half)
    d_rows = (d_own, d_far)
    d_att[...] = (
        dot(tall(d_rows, mine), w_own[:, 3 * inner :])
        + dot(tall(d_rows, other), w_other[:, 3 * inner :])
    ).astype(bf16)
    lines[...] = jnp.zeros_like(lines)
    up, down = (lax.broadcasted_iota(jnp.int32, (rows, rows), axis) for axis in (0, 1))
    flip = (up + down == rows - 1).astype(bf16)
    for head in range(heads):
        lanes = slice(head * width, (head + 1) * width)
        value_lanes = slice(inner + head * width, inner + (head + 1) * width)
        keys = qkv[:, inner + head * width : inner + (head + 1) * width]
        values = qkv[:, 2 * inner + head * width : 2 * inner + (head + 1) * width]
        d_key, d_value = None, None
        for at, block in enumerate(query_blocks):
            queries = qkv[block * rows : (block + 1) * rows, lanes]
            d_attended = d_att[at * rows : (at + 1) * rows, lanes]
            probs = probs_in[head, at * rows : (at + 1) * rows, :]
            d_probs = dot_nt(d_attended, values)
            delta = jnp.sum(probs * d_probs, axis=1, keepdims=True)
            d_scores = (probs * (d_probs - delta)).astype(bf16)
            d_query[at * rows : (at + 1) * rows, lanes] = dot(d_scores, keys).astype(bf16)
            key_part = dot_tn(d_scores, queries)
            value_part = dot_tn(probs.astype(bf16), d_attended)
            d_key = key_part if d_key is None else d_key + key_part
            d_value = value_part if d_value is None else d_value + value_part
            upward = dot(flip, d_scores)
            for key_at, key_block in enumerate(places):
                start = (key_block - places[block]) * rows + span - rows
                piece = upward[:, key_at * rows : (key_at + 1) * rows]
                padded = jnp.concatenate([piece, jnp.zeros_like(piece)], axis=1)
                turned = pltpu.roll(padded, 1, 1, stride=1, stride_axis=0)
                span_at = pl.ds(pl.multiple_of(start, rows), 2 * rows)
                lines[pl.ds(head, 1), span_at] += jnp.sum(turned, axis=0, keepdims=True)
        for key_at in range(key_blocks):
            from_, to = slice(key_at * rows, (key_at + 1) * rows), key_at // 2
            for out, parity in ((d_keep, 0), (d_send, 1)):
                if key_at % 2 == parity:
                    out[to, :, lanes] = d_key[from_].astype(out.dtype)
                    out[to, :, value_lanes] = d_value[from_].astype(out.dtype)


def attn_grad_body(
    here, inputs, d_query, d_keep, d_got, d_own, d_far, attended, w_own, w_other,
    g_keep, g_send, keep, send, d_qkv, *, sizes
):
    rows, heads, width, query_blocks, key_blocks, span = sizes
    inner = heads * width
    half = w_own.shape[0]
    mine, other = aligned(here[at_k], half), aligned(1 - here[at_k], half)
    d_qkv[:, :inner] = d_query[...]
    for at in range(2):
        d_qkv[at * rows : (at + 1) * rows, inner:] = (d_keep[at] + d_got[at].astype(f32)).astype(bf16)
    for lanes, weights, out in ((mine, w_own, keep), (other, w_other, send)):
        part = dot_nt(d_qkv[...], weights[:, : 3 * inner])
        g_keep[:, lanes] = part[:rows]
        g_send[:, lanes] = part[rows:].astype(bf16)
        two = jnp.concatenate([inputs[b * rows : (b + 1) * rows, lanes] for b in query_blocks], axis=0)
        out[:, : 3 * inner] = dot_tn(two, d_qkv[...]).astype(out.dtype)
        out[:, 3 * inner :] = dot_tn(tall((d_own, d_far), lanes), attended[...]).astype(out.dtype)


def input_grad_body(here, own, got, tokens, gain, d_residual, out, *, dims):
    total = own[...].astype(f32) + got[...].astype(f32)
    grad_normed = reorder(total, dims, attn_order, True) * gain[...]
    values = tokens[...].astype(f32)
    scale = inv_scale(values)
    out[...] = (d_residual[...] + norm_back(scale, values * scale, grad_normed)).astype(bf16)


def mixed_body(here, own, got, residual, out, *, dims):
    total = own[...].astype(f32) + got[...].astype(f32)
    out[...] = (residual[...] + reorder(total, dims, ffn_order, True)).astype(bf16)


def attn_final_body(here, own, got, wq, wk, wv, gain, gq, gk, gv, go, grad_gain):
    inner = own.shape[1] // 4

    def finish(low, high):
        grads = [
            jnp.concatenate([m[:, i * inner : (i + 1) * inner] for m in (low, high)], axis=1)
            for i in range(4)
        ]
        sums = 0.0
        for out, weights, grad in ((gq, wq, grads[0]), (gk, wk, grads[1]), (gv, wv, grads[2])):
            out[...] = grad
            sums = sums + jnp.sum(grad * weights[...].astype(f32), axis=1, keepdims=True)
        go[...] = grads[3].T
        grad_gain[...] = sums / gain[...]

    @pl.when(here[at_yl] == 0)
    def _():
        finish(own[...], got[...].astype(f32))

    @pl.when(here[at_yl] != 0)
    def _():
        finish(got[...].astype(f32), own[...])


def local(
    tokens,
    cotangent,
    prefix,
    norm_one,
    w_query,
    w_key,
    w_value,
    w_out,
    position_bias_matrix,
    norm_two,
    w_gate,
    w_up,
    w_down,
):
    tick = Clock(prefix).tick
    outer, deep = lax.axis_size("yh"), lax.axis_size("zh")
    rows, wide = tokens.shape[1:]
    part = w_query.shape[0]
    heads_dev, buckets = position_bias_matrix.shape
    heads = heads_dev // 2
    width = w_query.shape[1] // heads_dev
    inner = heads * width
    hidden_dev = w_gate.shape[1]
    chunks = -(-hidden_dev // (4 * lane))
    length = rows * outer * 4
    dims = (deep, 2, outer, 2, 2, part)
    half = wide // 2
    key_blocks = 4 * outer
    sizes = (rows, heads, width, (0, 2), key_blocks, length)

    split_deep = deep == 2 and (4 * part) % lane == 0
    deep_blocks = deep if split_deep else 1
    yh, yl, k, zl, zh = (lax.axis_index(a) for a in ("yh", "yl", "k", "zl", "zh"))
    relative = [(e, a) for a in range(2) for e in range(outer)]
    ys = [((yh + e) % outer) * 2 + (yl + a) % 2 for e, a in relative]
    where = at_lists + key_blocks
    here = [k, yl, zl, zh, yh, prefix[0]]
    here += [
        ((yh + e) % outer) * 4 + ((yl + a) % 2) * 2 + (k + b) % 2
        for e in range(outer)
        for a in range(2)
        for b in range(2)
    ]
    here += [y * deep_blocks + (zh + d) % deep_blocks for d in range(deep_blocks) for y in ys]
    here = jnp.stack([jnp.asarray(v, jnp.int32) for v in here])

    own, send = call(
        pack_attn_body,
        "pack_attn",
        here,
        [w_query, w_key, w_value, w_out],
        [((part, 4 * inner), bf16)] * 2,
    )
    own, send, gains, w_gate_in, w_up_in, w_down_in = tick(
        own, send, jnp.stack([norm_one, norm_two]), w_gate, w_up, w_down
    )
    pack = place([own, swap(send, "yl")], "yl")
    gains = both(both(gains, "zl"), "zh")
    pack, gains, w_gate_in, w_up_in, w_down_in, own_tokens = tick(
        pack, gains, w_gate_in, w_up_in, w_down_in, tokens[0]
    )

    own, send = call(
        pack_ffn_body,
        "pack_ffn",
        here,
        [w_gate_in, w_up_in, w_down_in],
        [((2, chunks, part, 3 * lane), bf16)] * 2,
        [pltpu.VMEM((3, part, 4 * chunks * lane), bf16)],
        chunks=chunks,
    )
    gains = both(both(gains, "yl"), "yh")
    far_tokens = swap(own_tokens, "yl")
    near, near_send = call(
        place_ffn_body,
        "place_ffn",
        here,
        [own, swap(send, "k")],
        [((chunks, 2, part, 3 * lane), bf16)] * 2,
        chunks=chunks,
    )
    pack, near, near_send, gains, far_tokens, own_tokens = tick(
        both(pack, "zh"), near, near_send, gains, far_tokens, own_tokens
    )

    gains = both(gains, "k")
    row_blocks = [p for pair in zip(gather(own_tokens, "yh"), gather(far_tokens, "yh")) for p in pair]
    row_blocks = [p for b in row_blocks for p in gather(b, "k")]
    near_got = swap(near_send, "zl")
    gains = gains.transpose(5, 3, 4, 1, 2, 0, 6).reshape(2, wide).astype(f32)
    gain_one, gain_two = gains[:1], gains[1:]
    attn_input, low_grad = call(
        rows_body,
        "rows",
        here,
        [gain_one, cotangent[0], *row_blocks],
        [((length, wide), bf16), ((rows, wide), bf16)],
        dims=dims,
    )
    table = jnp.where(yl == 0, position_bias_matrix[:heads], position_bias_matrix[heads:])
    distance = jnp.arange(2 * length, dtype=jnp.int32) - length
    indicator = (
        bucket_of(distance, buckets)[None] == jnp.arange(buckets, dtype=jnp.int32)[:, None]
    ).astype(f32)
    lines = jnp.einsum("hb,bd->hd", table.astype(f32), indicator, precision="highest")
    lines = jnp.pad(lines, ((0, 8 - heads), (0, 0)))
    nears = call(
        place_zl_body,
        "place_zl",
        here,
        [near, near_got],
        [((2, 2, part, 3 * lane), bf16)] * chunks,
    )
    pack, attn_input, low_grad, lines, *nears = tick(both(pack, "zl"), attn_input, low_grad, lines, *nears)

    def to_blocks(values):
        return [v.reshape(-1, 3 * lane) for v in values]

    def over_zh(near):
        pieces = gather(near, "zh")
        return pieces if split_deep else [None, place(pieces, "zh")]

    def over_y(value):
        return to_blocks([p for b in gather(value, "yl") for p in gather(b, "yh")])

    near_y = [None] * chunks
    far = [None] * chunks
    far_y = [None] * chunks
    early = split_deep
    pack = both(pack, "yh").reshape(half, 4 * inner)
    w_own, w_other = gather(pack, "k")
    far[0] = over_zh(nears[0])[1]
    for j in (0, 1):
        near_y[j] = over_y(nears[j]) if early else []
    qkv, probs, attended, out_keep, out_send = call(
        attend_body,
        "attend",
        here,
        [attn_input, w_own, w_other, lines],
        [
            ((length, 3 * inner), bf16),
            ((heads, 2 * rows, length), f32),
            ((2 * rows, inner), bf16),
            ((rows, wide), f32),
            ((rows, wide), bf16),
        ],
        sizes=sizes,
    )

    out_keep, out_send, nears[1], nears[2], far[0], low_grad, *flat = tick(
        out_keep, out_send, nears[1], nears[2], far[0], low_grad, *near_y[0], *near_y[1]
    )
    near_y[0], near_y[1] = flat[: len(flat) // 2], flat[len(flat) // 2 :]
    out_sum = (out_keep + swap(out_send, "yl").astype(f32)).astype(bf16)
    far[1] = over_zh(nears[1])[1]
    near_y[2] = over_y(nears[2]) if early else []
    far_grad = swap(low_grad, "zl")
    core_grad = swap(low_grad, "k")
    out_sum, nears[2], nears[3], far[0], far[1], far_grad, core_grad = tick(
        out_sum, nears[2], nears[3], far[0], far[1], far_grad, core_grad
    )
    far[2] = over_zh(nears[2])[1]
    near_y[3] = over_y(nears[3]) if early else []
    far_y[0] = over_y(far[0])
    farcore_grad = swap(far_grad, "k")
    residual, low_two = call(
        norm_body,
        "norm",
        here,
        [out_sum, swap(out_sum, "x"), tokens[0], gain_two],
        [((rows, wide), f32), ((rows, wide), bf16)],
        dims=dims,
    )
    low_two, nears[3], far[1], far[2], farcore_grad, *flat = tick(
        low_two, nears[3], far[1], far[2], farcore_grad, *near_y[2], *near_y[3], *far_y[0]
    )
    count = len(near_y[2])
    near_y[2], near_y[3], far_y[0] = flat[:count], flat[count : 2 * count], flat[2 * count :]
    far_two, core_two = swap(low_two, "zl"), swap(low_two, "k")
    far[3] = over_zh(nears[3])[1]
    far_y[1], far_y[2] = over_y(far[1]), over_y(far[2])
    count = len(far_y[1])
    far_two, core_two, far[3], *flat = tick(far_two, core_two, far[3], *far_y[1], *far_y[2])
    far_y[1], far_y[2] = flat[:count], flat[count:]
    far_y[3] = over_y(far[3])

    ffn_rows = [low_two, core_two, far_two, swap(far_two, "k")]
    grad_rows = [low_grad, core_grad, far_grad, farcore_grad]
    firsts, hiddens = [], []
    for j in range(chunks):
        first, hidden = call(
            ffn_body,
            "ffn",
            here,
            [*ffn_rows, *grad_rows, *near_y[j], *far_y[j]],
            [((4 * rows, 2 * lane), bf16), ((4 * rows, lane), bf16)],
            where=where,
        )
        firsts.append(first)
        hiddens.append(hidden)
    weights = [w for j in range(chunks) for w in (*near_y[j], *far_y[j])]

    def back(lefts, lanes):
        return call(
            back_body,
            "back",
            here,
            [*lefts, *weights],
            [((2, rows, wide), f32), ((2, rows, wide), bf16)],
            where=where,
            chunks=chunks,
            lanes=lanes,
        )

    def ffn_grad(j):
        return call(
            ffn_grad_body,
            "ffn_grad",
            here,
            [*ffn_rows, *grad_rows, firsts[j], hiddens[j]],
            [((outer, half // outer, 3 * lane), kind) for kind in (f32, bf16)],
            outer=outer,
        )

    def sum_y(grads):
        keep, send = grads
        got = [swap(send, "yl")]
        if outer > 1:
            total = keep + got[0].astype(f32)
            got = send_sums([total[e].astype(bf16) for e in range(1, outer)], "yh")
            keep = total[0]
        return split(here, at_zh, keep.reshape(deep, 4 * part, 3 * lane), got)

    def sum_zh(pieces):
        keep, send = pieces
        got = send_sums([send[e] for e in range(deep - 1)], "zh")
        return [v.reshape(2, 2, part, 3 * lane) for v in (keep, *got)]

    def pair(keep, got):
        shape = keep.shape[1:]
        return call(pair_body, "pair", here, [keep, got], [(shape, f32), (shape, bf16)])

    grads = [None] * chunks
    keep, send = back(firsts, slice(0, 2 * lane))
    send, keep = tick(send, keep)
    grads[0] = ffn_grad(0)
    core_keep, core_send = pair(keep, swap(send, "k"))
    core_keep, core_send, *grads[0] = tick(core_keep, core_send, *grads[0])
    core = (core_keep + swap(core_send, "zl").astype(f32)).astype(bf16)
    grads[1] = ffn_grad(1)
    sums = [None] * chunks
    sums[0] = sum_y(grads[0])
    core, *flat = tick(core, *sums[0], *grads[1])
    sums[0], grads[1] = flat[:2], flat[2:]
    grads[2] = ffn_grad(2)
    zh_sums = [None] * chunks
    zh_sums[0] = sum_zh(sums[0])
    sums[1] = sum_y(grads[1])
    d_residual, d_low = call(
        residual_back_body,
        "residual_back",
        here,
        [core, swap(core, "x"), residual, cotangent[0], gain_two],
        [((rows, wide), f32), ((rows, wide), bf16)],
        dims=dims,
    )
    d_low, *flat = tick(d_low, *sums[1], *grads[2], *zh_sums[0])
    sums[1], grads[2], zh_sums[0] = flat[:2], flat[2:4], flat[4:]
    d_far = swap(d_low, "yl")
    zh_sums[1] = sum_zh(sums[1])
    grads[3] = ffn_grad(3)
    mixed_keep, mixed_send = back(hiddens, slice(2 * lane, 3 * lane))
    d_low, d_far, mixed_keep, mixed_send, *flat = tick(
        d_low, d_far, mixed_keep, mixed_send, *grads[2], *grads[3], *zh_sums[1]
    )
    grads[2], grads[3], zh_sums[1] = flat[:2], flat[2:4], flat[4:]

    sums[2] = sum_y(grads[2])
    mixed_keep, mixed_send = pair(mixed_keep, swap(mixed_send, "k"))
    d_query, d_keep, d_send, d_lines = call(
        attend_back_body,
        "attend_back",
        here,
        [qkv, probs, d_low, d_far, w_own, w_other],
        [
            ((2 * rows, inner), bf16),
            ((2 * outer, rows, 2 * inner), f32),
            ((2 * outer, rows, 2 * inner), bf16),
            ((8, 2 * length), f32),
        ],
        [pltpu.VMEM((2 * rows, inner), bf16)],
        sizes=sizes,
    )
    d_query, d_keep, d_send, d_lines, mixed_keep, mixed_send, *flat = tick(
        d_query, d_keep, d_send, d_lines, mixed_keep, mixed_send, *sums[2], *grads[3]
    )
    sums[2], grads[3] = flat[:2], flat[2:]
    sums[3] = sum_y(grads[3])
    zh_sums[2] = sum_zh(sums[2])
    d_got = swap(d_send, "k")
    if outer > 1:
        total = (d_keep + d_got.astype(f32)).reshape(outer, 2, rows, 2 * inner)
        arrived = send_sums([total[e].astype(bf16) for e in range(1, outer)], "yh")
        d_keep, d_got = total[0], sum(a.astype(f32) for a in arrived)
    g_keep, g_send, keep, send = call(
        attn_grad_body,
        "attn_grad",
        here,
        [attn_input, d_query, d_keep, d_got, d_low, d_far, attended, w_own, w_other],
        [
            ((rows, wide), f32),
            ((rows, wide), bf16),
            ((half, 4 * inner), f32),
            ((half, 4 * inner), bf16),
        ],
        [pltpu.VMEM((2 * rows, 3 * inner), bf16)],
        sizes=sizes,
    )
    got = [swap(send, "k")]
    if outer > 1:
        total = (keep + got[0].astype(f32)).reshape(outer, -1, 4 * inner)
        pieces = [lax.dynamic_index_in_dim(total, (yh + e) % outer, 0, False) for e in range(outer)]
        keep, got = pieces[0], send_sums([p.astype(bf16) for p in pieces[1:]], "yh")
    keep, send = split(here, at_zl, keep.reshape(2, deep * 2 * part, 4 * inner), got)
    g_keep, g_send, keep, send, *flat = tick(g_keep, g_send, keep, send, *sums[3], *zh_sums[2])
    sums[3], zh_sums[2] = flat[:2], flat[2:]
    g_sum = (g_keep + swap(g_send, "yl").astype(f32)).astype(bf16)
    got = send_sums([send[0]], "zl")
    zh_sums[3] = sum_zh(sums[3])
    keep, send = split(here, at_zh, keep.reshape(deep, 2 * part, 4 * inner), got)
    done, core_send, other_send = call(
        ffn_split_body,
        "ffn_split",
        here,
        [v for each in zh_sums for v in each],
        [
            ((chunks, part, 3 * lane), f32),
            ((chunks, part, 3 * lane), bf16),
            ((chunks, 2, part, 3 * lane), bf16),
        ],
        chunks=chunks,
    )
    keep, send, g_sum, done, core_send, other_send = tick(
        keep, send, g_sum, done, core_send, other_send
    )
    got = send_sums([send[e] for e in range(deep - 1)], "zh")
    other = swap(other_send, "zl")
    core_got = swap(core_send, "k")
    far_got = swap(other, "k")
    mixed_half = (mixed_keep + swap(mixed_send, "zl").astype(f32)).astype(bf16)
    (input_grad,) = call(
        input_grad_body,
        "input_grad",
        here,
        [g_sum, swap(g_sum, "x"), tokens[0], gain_one, d_residual],
        [((rows, wide), bf16)],
        dims=dims,
    )
    keep, send = split(here, at_yl, keep.reshape(2, part, 4 * inner), got)
    keep, send, mixed_half, input_grad = tick(keep, send, mixed_half, input_grad)
    got = swap(send[0], "yl")
    grad_gate, grad_up, grad_down, gain_two_part = call(
        ffn_final_body,
        "ffn_final",
        here,
        [done, core_got, other, far_got, w_gate, w_up, norm_two.astype(f32)[:, None]],
        [
            ((part, hidden_dev), f32),
            ((part, hidden_dev), f32),
            ((hidden_dev, part), f32),
            ((part, 1), f32),
        ],
        [pltpu.VMEM((3, part, 4 * chunks * lane), f32)],
    )
    (mixed,) = call(
        mixed_body,
        "mixed",
        here,
        [mixed_half, swap(mixed_half, "x"), residual],
        [((rows, wide), bf16)],
        dims=dims,
    )
    grad_query, grad_key, grad_value, grad_out, gain_one_part = call(
        attn_final_body,
        "attn_final",
        here,
        [keep, got, w_query, w_key, w_value, norm_one.astype(f32)[:, None]],
        [((part, 2 * inner), f32)] * 3 + [((2 * inner, part), f32), ((part, 1), f32)],
    )
    grad_gains = jnp.concatenate([gain_one_part, gain_two_part], 1).T
    grad_gains = grad_gains + swap(grad_gains, "x")

    grad_table = jnp.einsum("hd,bd->hb", d_lines[:heads], indicator, precision="highest")
    for axis in ("k", "yh", "zl", "zh"):
        grad_table = jnp.sum(both(grad_table, axis), axis=0)
    grad_table = both(grad_table, "yl").reshape(heads_dev, buckets)
    return (
        mixed[None],
        input_grad[None],
        grad_gains[0],
        grad_query,
        grad_key,
        grad_value,
        grad_out,
        grad_table,
        grad_gains[1],
        grad_gate,
        grad_up,
        grad_down,
    )


def solution(mesh):
    depths, lines, halves = (mesh.shape[a] for a in ("fsdp", "ctx", "tp"))
    fine = Mesh(
        mesh.devices.reshape(depths // 2, 2, lines // 4, 2, 2, halves),
        ("zh", "zl", "yh", "yl", "k", "x"),
    )
    depth, line = ("zh", "zl"), ("yh", "yl", "k")
    every = (*depth, *line)
    in_specs = (
        P(depth, line, None),
        P(depth, line, None),
        P(depth),
        P(every),
        P(every, "x"),
        P(every, "x"),
        P(every, "x"),
        P("x", every),
        P("x", None),
        P(every),
        P(every, "x"),
        P(every, "x"),
        P("x", every),
    )
    out_specs = (
        P(depth, line, None),
        P(depth, line, None),
        P(every),
        P(every, "x"),
        P(every, "x"),
        P(every, "x"),
        P("x", every),
        P("x", None),
        P(every),
        P(every, "x"),
        P(every, "x"),
        P("x", every),
    )
    return jax.shard_map(local, mesh=fine, in_specs=in_specs, out_specs=out_specs, check_vma=False)
```

```python
import functools

import jax
import jax.numpy as jnp
import numpy as np
from jax import lax
from jax.experimental import pallas as pl
from jax.experimental.pallas import tpu as pltpu
from jax.sharding import Mesh, PartitionSpec as P

epsilon = 1e-06
masked_value = -1e30
far_bounds = (12, 16, 23, 32, 46, 64, 91)
f32 = jnp.float32
bf16 = jnp.bfloat16
lane = 128
ffn_order = (2, 3, 0, 1, 4, 5)
attn_order = (4, 2, 1, 0, 3, 5)
at_k, at_yl, at_zl, at_zh, at_yh, at_prefix, at_lists = range(7)


def bucket_of(relative, buckets):
    offset = jnp.abs(relative)
    far = jnp.full(offset.shape, buckets // 4, jnp.int32)
    for threshold in far_bounds:
        far = far + (offset >= threshold).astype(jnp.int32)
    return jnp.where(offset < buckets // 4, offset, far) + buckets // 2 * (relative > 0).astype(
        jnp.int32
    )


def dot(left, right, dims=((1,), (0,))):
    return lax.dot_general(left, right, (dims, ((), ())), preferred_element_type=f32)


def dot_nt(left, right):
    return dot(left, right, ((1,), (1,)))


def dot_tn(left, right):
    return dot(left, right, ((0,), (0,)))


def fetch(value, axis, step):
    size = lax.axis_size(axis)
    return lax.ppermute(value, axis, [((i + step) % size, i) for i in range(size)])


def swap(value, axis):
    return fetch(value, axis, 1)


def gather(value, axis):
    return [value] + [fetch(value, axis, e) for e in range(1, lax.axis_size(axis))]


def send_sums(sends, axis):
    size = lax.axis_size(axis)
    return [fetch(sends[e - 1], axis, size - e) for e in range(1, size)]


class Clock:
    def __init__(self, token):
        self.token = token

    def tick(self, *values):
        self.token, *values = lax.optimization_barrier((self.token, *values))
        return values


def runs_of(dims, order, inverse):
    index = np.arange(int(np.prod(dims))).reshape(dims).transpose(order).reshape(-1)
    if inverse:
        index = np.argsort(index)
    cuts = [0, *(np.flatnonzero(np.diff(index) != 1) + 1).tolist(), len(index)]
    return [(int(index[a]), int(index[a]) + b - a) for a, b in zip(cuts[:-1], cuts[1:])]


def reorder(value, dims, order, inverse=False):
    return jnp.concatenate([value[:, a:b] for a, b in runs_of(dims, order, inverse)], axis=1)


def inv_scale(values):
    return lax.rsqrt(jnp.mean(values * values, axis=-1, keepdims=True) + epsilon)


def norm_back(scale, normed, grad_normed):
    return scale * (grad_normed - normed * jnp.mean(grad_normed * normed, axis=-1, keepdims=True))


def aligned(index, size):
    return pl.ds(pl.multiple_of(index * size, size), size)


def call(body, name, here, arrays, outs, scratch=(), raw=0, **static):
    space = pl.BlockSpec(memory_space=pltpu.VMEM)
    spaces = [pl.BlockSpec(memory_space=pltpu.HBM)] * raw + [space] * (len(arrays) - raw)
    need = sum(int(np.prod(s.shape)) * jnp.dtype(s.dtype).itemsize for s in scratch[: len(scratch) - bool(raw)])
    need += (6 << 20) if static.get("dims", (lane,))[-1] >= 32 else (40 << 20)
    return pl.pallas_call(
        functools.partial(body, **static),
        out_shape=tuple(jax.ShapeDtypeStruct(shape, kind) for shape, kind in outs),
        in_specs=[pl.BlockSpec(memory_space=pltpu.SMEM)] + spaces,
        out_specs=tuple(space for _ in outs),
        scratch_shapes=scratch,
        compiler_params=pltpu.CompilerParams(vmem_limit_bytes=(56 << 20) if raw else need),
        cost_estimate=pl.CostEstimate(flops=2_000_000_000, bytes_accessed=8_000_000, transcendentals=0),
        name=name,
    )(here, *arrays)


def place_body(here, own, got, out, *, which):
    at = here[which]
    out[at] = own[...]
    out[1 - at] = got[...]


def pack_attn_body(here, wq, wk, wv, wo, one, two, own, send, mats, gains, sems):
    part, wide = mats.shape[1:]
    half = wide // 2
    copies = [
        pltpu.make_async_copy(ref, room, sems.at[i])
        for i, (ref, room) in enumerate(
            [*((ref, mats.at[i]) for i, ref in enumerate((wq, wk, wv, wo))), (one, gains.at[0]), (two, gains.at[1])]
        )
    ]
    for copy in copies:
        copy.start()
    for copy in copies:
        copy.wait()
    low = jnp.concatenate([mats[i, :, :half] for i in range(4)], axis=1)
    high = jnp.concatenate([mats[i, :, half:] for i in range(4)], axis=1)
    row = lax.broadcasted_iota(jnp.int32, (8, part), 0)
    first, second = (jnp.broadcast_to(gains[i].astype(f32), (8, part)) for i in range(2))
    head = jnp.where(row == 0, first, jnp.where(row == 1, second, 0.0)).astype(bf16)

    def write(out, mat):
        out[:8] = jnp.zeros((8, out.shape[1]), bf16)
        out[:8, :part] = head
        out[8:] = mat

    @pl.when(here[at_yl] == 0)
    def _():
        write(own, low)
        write(send, high)

    @pl.when(here[at_yl] != 0)
    def _():
        write(own, high)
        write(send, low)


def pack_ffn_body(here, wg, wu, wd, own, send, room, *, chunks):
    hidden = wg.shape[1]
    whole = hidden // lane * lane
    room[:, :, whole:] = jnp.zeros((3, wg.shape[0], 4 * chunks * lane - whole), bf16)
    room[0, :, :hidden] = wg[...]
    room[1, :, :hidden] = wu[...]
    room[2, :, :hidden] = wd[...]
    for out, core in ((own, here[at_k]), (send, 1 - here[at_k])):
        for h in range(2):
            for j in range(chunks):
                for m in range(3):
                    out[h, j, :, m * lane : (m + 1) * lane] = room[
                        m, :, aligned((2 * h + core) * chunks + j, lane)
                    ]


def place_ffn_body(here, own, got, near, first, rest, *, chunks):
    k, zl = here[at_k], here[at_zl]
    for j in range(chunks):
        near[j, k] = own[zl, j]
        near[j, 1 - k] = got[zl, j]
        out, at = (rest, j - 1) if j else (first, 0)
        out[at, k] = own[1 - zl, j]
        out[at, 1 - k] = got[1 - zl, j]


def place_first_body(here, near, got, out):
    zl = here[at_zl]
    out[zl] = near[0]
    out[1 - zl] = got[0]


def place_rest_body(here, near, rest, whole, *outs):
    zl = here[at_zl]
    j = 0
    for group in outs:
        for at in range(group.shape[0]):
            for out in (whole.at[j], group.at[at]):
                out[zl] = near[j + 1]
                out[1 - zl] = rest[j]
            j += 1


def buckets_row(span, buckets):
    return bucket_of(lax.broadcasted_iota(jnp.int32, (1, 2 * span), 1) - span, buckets)


def rows_body(here, table, *refs, dims, heads):
    *blocks, out, grads_out, lines = refs
    grads, blocks = blocks[:4], blocks[4:]
    rows = grads[0].shape[0]
    for at, block in enumerate(blocks):
        values = block[...].astype(f32)
        out[at * rows : (at + 1) * rows] = reorder(values * inv_scale(values), dims, attn_order)
    for at, block in enumerate(grads):
        low = reorder(block[...].astype(f32), dims, ffn_order)
        grads_out[at * rows : (at + 1) * rows] = low.astype(bf16)
    buckets = table.shape[1]
    values = table[...].astype(f32)
    mine = jnp.where(here[at_yl] == 0, values[:heads], values[heads:])
    row = buckets_row(lines.shape[1] // 2, buckets)
    line = jnp.zeros((heads, lines.shape[1]), f32)
    for b in range(buckets):
        line = line + jnp.where(row == b, mine[:, b : b + 1], 0.0)
    lines[...] = jnp.zeros_like(lines)
    lines[:heads] = line


def bias_block(line_ref, head, start, rows):
    line = line_ref[pl.ds(head, 1), pl.ds(pl.multiple_of(start, rows), 2 * rows)]
    spread = jnp.broadcast_to(line, (rows, 2 * rows))
    return pltpu.roll(spread, 0, 1, stride=1, stride_axis=0)[:, rows:]


def attend_body(
    here, normed, pack_own, pack_other, lines,
    qkv, probs_out, attended, keep, send, inputs, w_own, w_other, gains, *, sizes, dims
):
    rows, heads, width, query_blocks, key_blocks, span = sizes
    prefix = here[at_prefix]
    inner = heads * width
    half = w_own.shape[0]
    part = dims[-1]
    gain_parts = []
    for pack, weights in ((pack_own, w_own), (pack_other, w_other)):
        for at in range(half // part):
            weights[at * part : (at + 1) * part] = pack[at, 8:]
        gain_parts.append(
            [
                jnp.concatenate([pack[at, i : i + 1, :part].astype(f32) for at in range(half // part)], axis=1)
                for i in range(2)
            ]
        )
    for i in range(2):
        low, high = gain_parts[0][i], gain_parts[1][i]
        gain = jnp.where(
            here[at_k] == 0,
            jnp.concatenate([low, high], axis=1),
            jnp.concatenate([high, low], axis=1),
        )
        if i == 0:
            inputs[...] = (normed[...] * gain).astype(bf16)
        gains[i : i + 1] = reorder(gain, dims, attn_order, True)
    places = [here[at_lists + i] for i in range(key_blocks)]
    mine, other = aligned(here[at_k], half), aligned(1 - here[at_k], half)
    qkv[...] = (
        dot(inputs[:, mine], w_own[:, : 3 * inner]) + dot(inputs[:, other], w_other[:, : 3 * inner])
    ).astype(bf16)
    for head in range(heads):
        lanes = slice(head * width, (head + 1) * width)
        keys = qkv[:, inner + head * width : inner + (head + 1) * width]
        values = qkv[:, 2 * inner + head * width : 2 * inner + (head + 1) * width]
        for at, block in enumerate(query_blocks):
            query_block = places[block]
            queries = qkv[block * rows : (block + 1) * rows, lanes]
            raw = dot_nt(queries, keys)
            query_pos = query_block * rows + lax.broadcasted_iota(jnp.int32, (rows, rows), 0)
            parts = []
            for key_at, key_block in enumerate(places):
                start = (key_block - query_block) * rows + span - rows
                key_pos = key_block * rows + lax.broadcasted_iota(jnp.int32, (rows, rows), 1)
                allowed = (key_pos <= query_pos) | (key_pos < prefix)
                biased = raw[:, key_at * rows : (key_at + 1) * rows] + bias_block(
                    lines, head, start, rows
                )
                parts.append(jnp.where(allowed, biased, masked_value))
            scores = jnp.concatenate(parts, axis=1)
            top = jnp.max(scores, axis=1, keepdims=True)
            powers = jnp.exp(scores - top)
            probs = powers / jnp.sum(powers, axis=1, keepdims=True)
            probs_out[head, at * rows : (at + 1) * rows, :] = probs
            attended[at * rows : (at + 1) * rows, lanes] = dot(probs.astype(bf16), values).astype(
                bf16
            )
    for lanes, weights in ((mine, w_own), (other, w_other)):
        out = dot_nt(attended[...], weights[:, 3 * inner :])
        keep[:, lanes] = out[:rows]
        send[:, lanes] = out[rows:].astype(bf16)


def norm_body(here, own, got, tokens, gains, residual, low, *, dims):
    total = own[...].astype(f32) + got[...].astype(f32)
    values = tokens[...].astype(f32) + reorder(total, dims, attn_order, True)
    residual[...] = values
    low[...] = reorder(values * inv_scale(values) * gains[1:2], dims, ffn_order).astype(bf16)


def tall(refs, lanes):
    return jnp.concatenate([ref[:, lanes] for ref in refs], axis=0)


def ffn_body(here, *refs, where, picks):
    rows, grads, weights, (first_out, hidden_out) = refs[:4], refs[4], refs[5:-2], refs[-2:]
    weights = [w if at is None else w.at[at] for at, w in zip(picks, weights)]
    size = weights[0].shape[0]
    first, d_hidden = None, None
    for at, w in enumerate(weights):
        lanes = aligned(here[where + at], size)
        first_part = dot(tall(rows, lanes), w[:, : 2 * lane])
        d_part = dot(grads[:, lanes], w[:, 2 * lane :])
        first = first_part if first is None else first + first_part
        d_hidden = d_part if d_hidden is None else d_hidden + d_part
    gate, up = first[:, :lane], first[:, lane:]
    root = float(np.sqrt(2.0 / np.pi))
    square = gate * gate
    bend = jnp.tanh(root * gate * (1.0 + 0.044715 * square))
    half = 0.5 * (1.0 + bend)
    active = gate * half
    slope = half + 0.5 * gate * (1.0 - bend * bend) * (root * (1.0 + 3.0 * 0.044715 * square))
    hidden_out[...] = (active * up).astype(bf16)
    first_out[:, :lane] = (d_hidden * up * slope).astype(bf16)
    first_out[:, lane:] = (d_hidden * active).astype(bf16)


def back_body(here, *refs, where, chunks, picks, lanes):
    lefts, weights, (keep, send) = refs[:chunks], refs[chunks:-2], refs[-2:]
    weights = [w if at is None else w.at[at] for at, w in zip(picks, weights)]
    blocks = len(weights) // chunks
    rows = keep.shape[1]
    for at in range(blocks):
        total = None
        for j in range(chunks):
            w = weights[j * blocks + at]
            part = dot_nt(lefts[j][...], w[:, lanes])
            total = part if total is None else total + part
        here_lanes = aligned(here[where + at], w.shape[0])
        for a in range(2):
            keep[a, :, here_lanes] = total[2 * a * rows : (2 * a + 1) * rows]
            send[a, :, here_lanes] = total[(2 * a + 1) * rows : (2 * a + 2) * rows].astype(bf16)


def ffn_grad_body(here, *refs, outer):
    rows, grads, (first, hidden, keep, send) = refs[:4], refs[4], refs[5:]
    size = keep.shape[1]
    for e in range(outer):
        yh = here[at_yh] + e
        yh = jnp.where(yh >= outer, yh - outer, yh) * 2
        for out, y in ((keep, yh + here[at_yl]), (send, yh + 1 - here[at_yl])):
            lanes = aligned(y, size)
            out[e, :, : 2 * lane] = dot_tn(tall(rows, lanes), first[...]).astype(out.dtype)
            out[e, :, 2 * lane :] = dot_tn(grads[:, lanes], hidden[...]).astype(out.dtype)


def split_body(here, own, *refs, which):
    *got, keep, send = refs
    count = own.shape[0]
    for e in range(count):
        at = here[which] + e
        at = jnp.where(at >= count, at - count, at)
        total = own[at]
        for ref in got:
            total = total + ref[at].astype(f32)
        if e:
            send[e - 1] = total.astype(bf16)
        else:
            keep[...] = total


def split(here, which, own, got):
    shape = own.shape[1:]
    return call(
        split_body,
        "split",
        here,
        [own, *(g.reshape(own.shape) for g in got)],
        [(shape, f32), ((own.shape[0] - 1, *shape), bf16)],
        which=which,
    )


def ffn_split_body(here, *refs, chunks):
    done, core, other = refs[-3:]
    each = (len(refs) - 3) // chunks
    zl, k = here[at_zl], here[at_k]
    for j in range(chunks):
        own, *got = refs[j * each : (j + 1) * each]

        def total(depth, slice_):
            value = own[depth, slice_]
            for ref in got:
                value = value + ref[depth, slice_].astype(f32)
            return value

        done[j] = total(zl, k)
        core[j] = total(zl, 1 - k).astype(bf16)
        other[j, 0] = total(1 - zl, 0).astype(bf16)
        other[j, 1] = total(1 - zl, 1).astype(bf16)


def sum_row(values):
    sums = jnp.sum(values, axis=1, keepdims=True)
    return jnp.broadcast_to(sums, (values.shape[0], lane)).T[0:1]


def ffn_final_body(here, *refs, groups):
    parts, rest = refs[: 4 * groups], refs[4 * groups :]
    wg, wu, gain, first_row, grad_g, grad_u, grad_d, grad_gain, room = rest
    hidden = wg.shape[1]
    chunks = room.shape[2] // (4 * lane)
    zl, k = here[at_zl], here[at_k]
    j = 0
    for group in range(groups):
        done, other, core, far = parts[4 * group : 4 * group + 4]
        for at in range(done.shape[0]):
            for h, c, value in (
                (zl, k, done[at]),
                (1 - zl, k, other[at, k].astype(f32)),
                (zl, 1 - k, core[at].astype(f32)),
                (1 - zl, 1 - k, far[at, k].astype(f32)),
            ):
                for m in range(3):
                    room[m, :, aligned((2 * h + c) * chunks + j, lane)] = value[
                        :, m * lane : (m + 1) * lane
                    ]
            j += 1
    gate, up = room[0, :, :hidden], room[1, :, :hidden]
    grad_g[...] = gate
    grad_u[...] = up
    grad_d[...] = room[2, :, :hidden]
    sums = gate * wg[...].astype(f32) + up * wu[...].astype(f32)
    grad_gain[0:1] = first_row[...]
    grad_gain[1:2] = sum_row(sums) / gain[...].astype(f32)


def pair_body(here, own, got, keep, send):
    keep[...] = own[0] + got[0].astype(f32)
    send[...] = (own[1] + got[1].astype(f32)).astype(bf16)


def residual_back_body(here, own, got, residual, cotangent, gains, d_residual, d_low, *, dims):
    total = own[...].astype(f32) + got[...].astype(f32)
    grad_normed = reorder(total, dims, ffn_order, True) * gains[1:2]
    values = residual[...]
    scale = inv_scale(values)
    back = cotangent[...].astype(f32) + norm_back(scale, values * scale, grad_normed)
    d_residual[...] = back
    d_low[...] = reorder(back, dims, attn_order).astype(bf16)


def attend_back_body(
    here, qkv, probs_in, d_own, d_far, w_own, w_other,
    d_query, d_keep, d_send, table, lines, d_att, *, sizes, buckets
):
    rows, heads, width, query_blocks, key_blocks, span = sizes
    inner = heads * width
    half = w_own.shape[0]
    places = [here[at_lists + i] for i in range(key_blocks)]
    mine, other = aligned(here[at_k], half), aligned(1 - here[at_k], half)
    d_rows = (d_own, d_far)
    d_att[...] = (
        dot(tall(d_rows, mine), w_own[:, 3 * inner :])
        + dot(tall(d_rows, other), w_other[:, 3 * inner :])
    ).astype(bf16)
    lines[...] = jnp.zeros_like(lines)
    up, down = (lax.broadcasted_iota(jnp.int32, (rows, rows), axis) for axis in (0, 1))
    flip = (up + down == rows - 1).astype(bf16)
    for head in range(heads):
        lanes = slice(head * width, (head + 1) * width)
        value_lanes = slice(inner + head * width, inner + (head + 1) * width)
        keys = qkv[:, inner + head * width : inner + (head + 1) * width]
        values = qkv[:, 2 * inner + head * width : 2 * inner + (head + 1) * width]
        d_key, d_value = None, None
        for at, block in enumerate(query_blocks):
            queries = qkv[block * rows : (block + 1) * rows, lanes]
            d_attended = d_att[at * rows : (at + 1) * rows, lanes]
            probs = probs_in[head, at * rows : (at + 1) * rows, :]
            d_probs = dot_nt(d_attended, values)
            delta = jnp.sum(probs * d_probs, axis=1, keepdims=True)
            d_scores = (probs * (d_probs - delta)).astype(bf16)
            d_query[at * rows : (at + 1) * rows, lanes] = dot(d_scores, keys).astype(bf16)
            key_part = dot_tn(d_scores, queries)
            value_part = dot_tn(probs.astype(bf16), d_attended)
            d_key = key_part if d_key is None else d_key + key_part
            d_value = value_part if d_value is None else d_value + value_part
            upward = dot(flip, d_scores)
            for key_at, key_block in enumerate(places):
                start = (key_block - places[block]) * rows + span - rows
                piece = upward[:, key_at * rows : (key_at + 1) * rows]
                padded = jnp.concatenate([piece, jnp.zeros_like(piece)], axis=1)
                turned = pltpu.roll(padded, 1, 1, stride=1, stride_axis=0)
                span_at = pl.ds(pl.multiple_of(start, rows), 2 * rows)
                lines[pl.ds(head, 1), span_at] += jnp.sum(turned, axis=0, keepdims=True)
        for key_at in range(key_blocks):
            from_, to = slice(key_at * rows, (key_at + 1) * rows), key_at // 2
            for out, parity in ((d_keep, 0), (d_send, 1)):
                if key_at % 2 == parity:
                    out[to, :, lanes] = d_key[from_].astype(out.dtype)
                    out[to, :, value_lanes] = d_value[from_].astype(out.dtype)
    row = buckets_row(span, buckets)
    column = lax.broadcasted_iota(jnp.int32, table.shape, 1)
    total = jnp.zeros(table.shape, f32)
    for b in range(buckets):
        one = jnp.sum(jnp.where(row == b, lines[...], 0.0), axis=1, keepdims=True)
        total = jnp.where(column == b, one, total)
    table[...] = total


def attn_grad_body(
    here, inputs, d_query, d_keep, d_got, d_own, d_far, attended, w_own, w_other,
    g_keep, g_send, keep, send, d_qkv, *, sizes
):
    rows, heads, width, query_blocks, key_blocks, span = sizes
    inner = heads * width
    half = w_own.shape[0]
    mine, other = aligned(here[at_k], half), aligned(1 - here[at_k], half)
    d_qkv[:, :inner] = d_query[...]
    for at in range(2):
        d_qkv[at * rows : (at + 1) * rows, inner:] = (d_keep[at] + d_got[at].astype(f32)).astype(bf16)
    for lanes, weights, out in ((mine, w_own, keep), (other, w_other, send)):
        part = dot_nt(d_qkv[...], weights[:, : 3 * inner])
        g_keep[:, lanes] = part[:rows]
        g_send[:, lanes] = part[rows:].astype(bf16)
        two = jnp.concatenate([inputs[b * rows : (b + 1) * rows, lanes] for b in query_blocks], axis=0)
        out[:, : 3 * inner] = dot_tn(two, d_qkv[...]).astype(out.dtype)
        out[:, 3 * inner :] = dot_tn(tall((d_own, d_far), lanes), attended[...]).astype(out.dtype)


def input_grad_body(here, own, got, tokens, gains, d_residual, out, *, dims):
    total = own[...].astype(f32) + got[...].astype(f32)
    grad_normed = reorder(total, dims, attn_order, True) * gains[0:1]
    values = tokens[...].astype(f32)
    scale = inv_scale(values)
    out[...] = (d_residual[...] + norm_back(scale, values * scale, grad_normed)).astype(bf16)


def mixed_body(here, own, got, residual, out, *, dims):
    total = own[...].astype(f32) + got[...].astype(f32)
    out[...] = (residual[...] + reorder(total, dims, ffn_order, True)).astype(bf16)


def attn_final_body(here, own, got, wq, wk, wv, gain, gq, gk, gv, go, grad_gain):
    inner = own.shape[1] // 4

    def finish(low, high):
        grads = [
            jnp.concatenate([m[:, i * inner : (i + 1) * inner] for m in (low, high)], axis=1)
            for i in range(4)
        ]
        sums = 0.0
        for out, weights, grad in ((gq, wq, grads[0]), (gk, wk, grads[1]), (gv, wv, grads[2])):
            out[...] = grad
            sums = sums + grad * weights[...].astype(f32)
        go[...] = grads[3]
        grad_gain[...] = sum_row(sums) / gain[...].astype(f32)

    @pl.when(here[at_yl] == 0)
    def _():
        finish(own[...], got[...].astype(f32))

    @pl.when(here[at_yl] != 0)
    def _():
        finish(got[...].astype(f32), own[...])


def local(
    tokens,
    cotangent,
    prefix,
    norm_one,
    w_query,
    w_key,
    w_value,
    w_out,
    position_bias_matrix,
    norm_two,
    w_gate,
    w_up,
    w_down,
):
    outer, deep = lax.axis_size("yh"), lax.axis_size("zh")
    rows, wide = tokens.shape[1:]
    part = w_query.shape[0]
    heads_dev, buckets = position_bias_matrix.shape
    heads = heads_dev // 2
    width = w_query.shape[1] // heads_dev
    inner = heads * width
    hidden_dev = w_gate.shape[1]
    chunks = -(-hidden_dev // (4 * lane))
    length = rows * outer * 4
    dims = (deep, 2, outer, 2, 2, part)
    half = wide // 2
    key_blocks = 4 * outer
    sizes = (rows, heads, width, (0, 2), key_blocks, length)

    split_deep = deep == 2 and (4 * part) % lane == 0
    deep_blocks = deep if split_deep else 1
    yh, yl, k, zl, zh = (lax.axis_index(a) for a in ("yh", "yl", "k", "zl", "zh"))
    relative = [(e, a) for a in range(2) for e in range(outer)]
    ys = [((yh + e) % outer) * 2 + (yl + a) % 2 for e, a in relative]
    where = at_lists + key_blocks
    here = [k, yl, zl, zh, yh, prefix[0]]
    here += [
        ((yh + e) % outer) * 4 + ((yl + a) % 2) * 2 + (k + b) % 2
        for e in range(outer)
        for a in range(2)
        for b in range(2)
    ]
    here += [y * deep_blocks + (zh + d) % deep_blocks for d in range(deep_blocks) for y in ys]
    here = jnp.stack([jnp.asarray(v, jnp.int32) for v in here])
    tick = Clock(here).tick
    which = {"k": at_k, "yl": at_yl, "zl": at_zl, "zh": at_zh, "yh": at_yh}

    def kernel(body, name, arrays, outs, scratch=(), **static):
        return call(body, name, here, arrays, outs, scratch, **static)

    def place(pieces, axis):
        size, shape = len(pieces), pieces[0].shape
        if size == 1:
            return pieces[0][None]
        if size == 2:
            outs = [((2, *shape), pieces[0].dtype)]
            return kernel(place_body, "place", pieces, outs, which=which[axis])[0]
        stack = jnp.zeros((size, *shape), pieces[0].dtype)
        for e, piece in enumerate(pieces):
            at = (lax.axis_index(axis) + e) % size
            stack = lax.dynamic_update_slice_in_dim(stack, piece[None], at, 0)
        return stack

    def both(value, axis):
        return place(gather(value, axis), axis)

    tall_part = 8 + part
    own, send = kernel(
        pack_attn_body,
        "pack_attn",
        [w_query, w_key, w_value, w_out.T, norm_one[None], norm_two[None]],
        [((tall_part, 4 * inner), bf16)] * 2,
        [
            pltpu.VMEM((4, part, 2 * inner), bf16),
            pltpu.VMEM((2, 1, part), bf16),
            pltpu.SemaphoreType.DMA((6,)),
        ],
        raw=6,
    )
    own, send, own_grad, *ffn_in = tick(own, send, cotangent[0], w_gate, w_up, w_down.T)
    pack_got = swap(send, "yl")
    far_grad = swap(own_grad, "zl")
    ffn_own, ffn_send = kernel(
        pack_ffn_body,
        "pack_ffn",
        ffn_in,
        [((2, chunks, part, 3 * lane), bf16)] * 2,
        [pltpu.VMEM((3, part, 4 * chunks * lane), bf16)],
        chunks=chunks,
    )
    pack = place([own, pack_got], "yl")

    pack, ffn_own, ffn_send, own_tokens = tick(pack, ffn_own, ffn_send, tokens[0])
    pack_all = gather(pack, "zh")
    far_tokens = swap(own_tokens, "yl")
    near, near_first, near_rest = kernel(
        place_ffn_body,
        "place_ffn",
        [ffn_own, swap(ffn_send, "k")],
        [((n, 2, part, 3 * lane), bf16) for n in (chunks, 1, chunks - 1)],
        chunks=chunks,
    )
    pack = place(pack_all, "zh")

    pack, near, near_first, near_rest, far_tokens, own_tokens, far_grad, own_grad = tick(
        pack, near, near_first, near_rest, far_tokens, own_tokens, far_grad, own_grad
    )
    pack_all = gather(pack, "zl")
    first_got = swap(near_first, "zl")
    row_blocks = [p for pair in zip(gather(own_tokens, "yh"), gather(far_tokens, "yh")) for p in pair]
    row_blocks = [p for b in row_blocks for p in gather(b, "k")]
    grad_blocks = [p for b in (own_grad, far_grad) for p in gather(b, "k")]
    normed, grad_rows, lines = kernel(
        rows_body,
        "rows",
        [position_bias_matrix, *grad_blocks, *row_blocks],
        [((length, wide), f32), ((4 * rows, wide), bf16), ((8, 2 * length), f32)],
        dims=dims,
        heads=heads,
    )
    pack = place(pack_all, "zl")
    (near_zero,) = kernel(
        place_first_body, "place_first", [near, first_got], [((2, 2, part, 3 * lane), bf16)]
    )

    pack, near, near_zero, first_got, near_rest, normed, grad_rows, lines = tick(
        pack, near, near_zero, first_got, near_rest, normed, grad_rows, lines
    )
    pack = both(pack, "yh").reshape(half // part, tall_part, 4 * inner)
    pack_own, pack_other = gather(pack, "k")
    rest_got = swap(near_rest, "zl")

    groups = [[0], list(range(1, chunks - 1)), [chunks - 1]]

    def over_zh(value):
        pieces = gather(value, "zh")
        if split_deep:
            return pieces[1]
        return place(pieces, "zh").swapaxes(0, 1)

    def over_y(value):
        value = value.reshape(value.shape[0], -1, 3 * lane)
        return [p for b in gather(value, "yl") for p in gather(b, "yh")]

    far, far_y = [None] * 3, [None] * 3
    near_zero = near_zero[None]
    far[0] = over_zh(near_zero)
    zero_y = over_y(near_zero) if split_deep else []
    qkv, probs, attended, out_keep, out_send, attn_input, w_own, w_other, gains = kernel(
        attend_body,
        "attend",
        [normed, pack_own, pack_other, lines],
        [
            ((length, 3 * inner), bf16),
            ((heads, 2 * rows, length), f32),
            ((2 * rows, inner), bf16),
            ((rows, wide), f32),
            ((rows, wide), bf16),
            ((length, wide), bf16),
            ((half, 4 * inner), bf16),
            ((half, 4 * inner), bf16),
            ((2, wide), f32),
        ],
        sizes=sizes,
        dims=dims,
    )

    out_keep, out_send = tick(out_keep, out_send)
    out_got = swap(out_send, "yl")
    near, rest_got, far[0], *zero_y = tick(near, rest_got, far[0], *zero_y)
    shape = (2, 2, part, 3 * lane)
    whole, *nears = kernel(
        place_rest_body,
        "place_rest",
        [near, rest_got],
        [((chunks - 1, *shape), bf16)] + [((len(g), *shape), bf16) for g in groups[1:]],
    )
    out_keep, whole, *nears = tick(out_keep, whole, *nears)
    far[1] = over_zh(nears[0])
    rest_y = over_y(whole) if split_deep else []
    out_sum = (out_keep + out_got.astype(f32)).astype(bf16)

    out_sum, far[0] = tick(out_sum, far[0])
    out_other = swap(out_sum, "x")
    residual, low_two = kernel(
        norm_body,
        "norm",
        [out_sum, out_other, tokens[0], gains],
        [((rows, wide), f32), ((rows, wide), bf16)],
        dims=dims,
    )

    low_two, far[0], nears[1], *rest_y = tick(low_two, far[0], nears[1], *rest_y)
    far_two, core_two = swap(low_two, "zl"), swap(low_two, "k")
    far_y[0] = over_y(far[0])
    core_two, far[1], nears[1] = tick(core_two, far[1], nears[1])
    far[2] = over_zh(nears[1])
    far_y[1] = over_y(far[1])

    far_two, core_two, *far_y[0] = tick(far_two, core_two, *far_y[0])
    farcore_two = swap(far_two, "k")
    ffn_rows = [low_two, core_two, far_two, farcore_two]

    def weights_of(j):
        g = next(g for g, group in enumerate(groups) if j in group)
        at = j - groups[g][0]
        near_blocks = []
        if split_deep:
            own, others, near_at = (near_zero, zero_y, 0) if j == 0 else (whole, rest_y, j - 1)
            own = own.reshape(own.shape[0], -1, 3 * lane)
            near_blocks = [(v, near_at) for v in (own, *others[1:])]
        return near_blocks + [(v, at) for v in far_y[g]]

    def ffn(j):
        weights = weights_of(j)
        return kernel(
            ffn_body,
            "ffn",
            [*ffn_rows, grad_rows, *(w for w, _ in weights)],
            [((4 * rows, 2 * lane), bf16), ((4 * rows, lane), bf16)],
            where=where,
            picks=tuple(at for _, at in weights),
        )

    def back(lefts, lanes):
        weights = [w for j in range(chunks) for w in weights_of(j)]
        return kernel(
            back_body,
            "back",
            [*lefts, *(w for w, _ in weights)],
            [((2, rows, wide), f32), ((2, rows, wide), bf16)],
            where=where,
            chunks=chunks,
            picks=tuple(at for _, at in weights),
            lanes=lanes,
        )

    def ffn_grad(first, hidden):
        return kernel(
            ffn_grad_body,
            "ffn_grad",
            [*ffn_rows, grad_rows, first, hidden],
            [((outer, half // outer, 3 * lane), kind) for kind in (f32, bf16)],
            outer=outer,
        )

    def sum_y(keep, got):
        got = [got]
        if outer > 1:
            total = keep + got[0].astype(f32)
            got = send_sums([total[e].astype(bf16) for e in range(1, outer)], "yh")
            keep = total[0]
        return split(here, at_zh, keep.reshape(deep, 4 * part, 3 * lane), got)

    def sum_zh(keep, send):
        got = send_sums([send[e] for e in range(deep - 1)], "zh")
        return [v.reshape(2, 2, part, 3 * lane) for v in (keep, *got)]

    def pair(keep, got):
        shape = keep.shape[1:]
        return kernel(pair_body, "pair", [keep, got], [(shape, f32), (shape, bf16)])

    def ffn_split(group):
        count = len(group)
        return kernel(
            ffn_split_body,
            "ffn_split",
            [v for each in group for v in each],
            [
                ((count, part, 3 * lane), f32),
                ((count, part, 3 * lane), bf16),
                ((count, 2, part, 3 * lane), bf16),
            ],
            chunks=count,
        )

    first_0, hidden_0 = ffn(0)

    far[2], first_0, hidden_0 = tick(far[2], first_0, hidden_0)
    far_y[2] = over_y(far[2])
    grads = [None] * chunks
    grad_got, sums, zh_sums = [None] * chunks, [None] * chunks, [None] * chunks
    grads[0] = ffn_grad(first_0, hidden_0)
    firsts, hiddens = [first_0], [hidden_0]
    for j in range(1, chunks):
        first, hidden = ffn(j)
        firsts.append(first)
        hiddens.append(hidden)
    keep, send = back(firsts, slice(0, 2 * lane))

    keep, send, *flat = tick(keep, send, *grads[0], *firsts[1:], *hiddens)
    grads[0], firsts, hiddens = flat[:2], [None, *flat[2:5]], flat[5:]
    core_got = swap(send, "k")
    grad_got[0] = swap(grads[0][1], "yl")
    grads[1] = ffn_grad(firsts[1], hiddens[1])
    core_keep, core_send = pair(keep, core_got)

    core_keep, core_send, *flat = tick(core_keep, core_send, *grads[1], *firsts[2:], *hiddens)
    grads[1], firsts, hiddens = flat[:2], [None, None, *flat[2:4]], flat[4:]
    core_got = swap(core_send, "zl")
    grad_got[1] = swap(grads[1][1], "yl")
    grads[2] = ffn_grad(firsts[2], hiddens[2])
    grads[3] = ffn_grad(firsts[3], hiddens[3])
    mixed_keep, mixed_send = back(hiddens, slice(2 * lane, 3 * lane))
    grad_keep, mixed_keep, *flat = tick(grads[0][0], mixed_keep, mixed_send, *grads[2], *grads[3])
    mixed_send, grads[2], grads[3] = flat[0], flat[1:3], flat[3:]
    sums[0] = sum_y(grad_keep, grad_got[0])
    core = (core_keep + core_got.astype(f32)).astype(bf16)

    core, mixed_keep, mixed_send, *flat = tick(
        core, mixed_keep, mixed_send, *sums[0], *grads[2], *grads[3]
    )
    sums[0], grads[2], grads[3] = flat[:2], flat[2:4], flat[4:]
    core_other = swap(core, "x")
    zh_sums[0] = sum_zh(*sums[0])
    sums[1] = sum_y(grads[1][0], grad_got[1])
    d_residual, d_low = kernel(
        residual_back_body,
        "residual_back",
        [core, core_other, residual, cotangent[0], gains],
        [((rows, wide), f32), ((rows, wide), bf16)],
        dims=dims,
    )

    d_low, mixed_send, *flat = tick(d_low, mixed_send, *sums[1], *grads[2])
    sums[1], grads[2] = flat[:2], flat[2:]
    d_far = swap(d_low, "yl")
    grad_got[2] = swap(grads[2][1], "yl")
    zh_sums[1] = sum_zh(*sums[1])
    mixed_got = swap(mixed_send, "k")
    mixed_keep, mixed_got, *zh_sums[0] = tick(mixed_keep, mixed_got, *zh_sums[0])
    mixed_keep, mixed_send = pair(mixed_keep, mixed_got)

    d_far, mixed_keep, mixed_send = tick(d_far, mixed_keep, mixed_send)
    mixed_got = swap(mixed_send, "zl")
    d_query, d_keep, d_send, grad_table = kernel(
        attend_back_body,
        "attend_back",
        [qkv, probs, d_low, d_far, w_own, w_other],
        [
            ((2 * rows, inner), bf16),
            ((2 * outer, rows, 2 * inner), f32),
            ((2 * outer, rows, 2 * inner), bf16),
            ((8, lane), f32),
        ],
        [pltpu.VMEM((8, 2 * length), f32), pltpu.VMEM((2 * rows, inner), bf16)],
        sizes=sizes,
        buckets=buckets,
    )

    def table_sum(value, axis):
        if lax.axis_size(axis) == 2:
            return value + swap(value, axis)
        return jnp.sum(both(value, axis), axis=0)

    d_query, d_keep, d_send, grad_table, *zh_sums[1] = tick(
        d_query, d_keep, d_send, grad_table, *zh_sums[1]
    )
    done_a = ffn_split(zh_sums[: chunks // 2])
    d_got = swap(d_send, "k")
    grad_table = table_sum(grad_table, "k")
    if outer > 1:
        grad_table = table_sum(grad_table, "yh")
        total = (d_keep + d_got.astype(f32)).reshape(outer, 2, rows, 2 * inner)
        arrived = send_sums([total[e].astype(bf16) for e in range(1, outer)], "yh")
        d_keep, d_got = total[0], sum(a.astype(f32) for a in arrived)
    g_keep, g_send, keep, send = kernel(
        attn_grad_body,
        "attn_grad",
        [attn_input, d_query, d_keep, d_got, d_low, d_far, attended, w_own, w_other],
        [
            ((rows, wide), f32),
            ((rows, wide), bf16),
            ((half, 4 * inner), f32),
            ((half, 4 * inner), bf16),
        ],
        [pltpu.VMEM((2 * rows, 3 * inner), bf16)],
        sizes=sizes,
    )

    g_keep, g_send, keep, send, grad_table, *flat = tick(
        g_keep, g_send, keep, send, grad_table, grad_got[2], *done_a
    )
    grad_got[2], done_a = flat[0], flat[1:]
    got = [swap(send, "k")]
    g_got = swap(g_send, "yl")
    grad_table = table_sum(grad_table, "zl")

    def spread(done):
        other = swap(done[2], "zl")
        return [done[0], other, swap(done[1], "k"), swap(other, "k")]

    if outer > 1:
        total = (keep + got[0].astype(f32)).reshape(outer, -1, 4 * inner)
        pieces = [lax.dynamic_index_in_dim(total, (yh + e) % outer, 0, False) for e in range(outer)]
        keep, got = pieces[0], send_sums([p.astype(bf16) for p in pieces[1:]], "yh")
    sums[2] = sum_y(grads[2][0], grad_got[2])
    keep, send = split(here, at_zl, keep.reshape(2, deep * 2 * part, 4 * inner), got)

    keep, send, mixed_got, grad_table, *flat = tick(
        keep, send, mixed_got, grad_table, *sums[2], *grads[3]
    )
    sums[2], grads[3] = flat[:2], flat[2:4]
    got = send_sums([send[0]], "zl")
    grad_got[3] = swap(grads[3][1], "yl")
    zh_sums[2] = sum_zh(*sums[2])
    grad_table = table_sum(grad_table, "zh")
    mixed_half = (mixed_keep + mixed_got.astype(f32)).astype(bf16)
    g_sum = (g_keep + g_got.astype(f32)).astype(bf16)
    keep, send = split(here, at_zh, keep.reshape(deep, 2 * part, 4 * inner), got)

    keep, send, g_sum, mixed_half, grad_table, *done_a = tick(
        keep, send, g_sum, mixed_half, grad_table, *done_a
    )
    got = send_sums([send[e] for e in range(deep - 1)], "zh")
    g_other = swap(g_sum, "x")
    mixed_other = swap(mixed_half, "x")

    sums[3] = sum_y(grads[3][0], grad_got[3])
    grad_table = both(grad_table, "yl")
    (mixed,) = kernel(
        mixed_body, "mixed", [mixed_half, mixed_other, residual], [((rows, wide), bf16)], dims=dims
    )
    mixed, *flat = tick(mixed, *sums[3], *done_a)
    sums[3], done_a = flat[:2], flat[2:]
    zh_sums[3] = sum_zh(*sums[3])
    group_a = spread(done_a)
    (input_grad,) = kernel(
        input_grad_body,
        "input_grad",
        [g_sum, g_other, tokens[0], gains, d_residual],
        [((rows, wide), bf16)],
        dims=dims,
    )
    keep, send = split(here, at_yl, keep.reshape(2, part, 4 * inner), got)

    keep, send, grad_table = tick(keep, send, grad_table)
    got = swap(send[0], "yl")
    keep, input_grad = tick(keep, input_grad)
    group_b = spread(ffn_split(zh_sums[chunks // 2 :]))
    grad_query, grad_key, grad_value, grad_out, gain_row = kernel(
        attn_final_body,
        "attn_final",
        [keep, got, w_query, w_key, w_value, norm_one[None]],
        [((part, 2 * inner), f32)] * 4 + [((1, part), f32)],
    )
    grad_gate, grad_up, grad_down, grad_gains = kernel(
        ffn_final_body,
        "ffn_final",
        [*group_a, *group_b, w_gate, w_up, norm_two[None], gain_row],
        [((part, hidden_dev), f32)] * 3 + [((2, part), f32)],
        [pltpu.VMEM((3, part, 4 * chunks * lane), f32)],
        groups=2,
    )
    grad_gains = grad_gains + swap(grad_gains, "x")
    return (
        mixed[None],
        input_grad[None],
        grad_gains[0],
        grad_query,
        grad_key,
        grad_value,
        grad_out.T,
        grad_table[:, :heads, :buckets].reshape(heads_dev, buckets),
        grad_gains[1],
        grad_gate,
        grad_up,
        grad_down.T,
    )


def solution(mesh):
    depths, lines, halves = (mesh.shape[a] for a in ("fsdp", "ctx", "tp"))
    fine = Mesh(
        mesh.devices.reshape(depths // 2, 2, lines // 4, 2, 2, halves),
        ("zh", "zl", "yh", "yl", "k", "x"),
    )
    depth, line = ("zh", "zl"), ("yh", "yl", "k")
    every = (*depth, *line)
    in_specs = (
        P(depth, line, None),
        P(depth, line, None),
        P(depth),
        P(every),
        P(every, "x"),
        P(every, "x"),
        P(every, "x"),
        P("x", every),
        P("x", None),
        P(every),
        P(every, "x"),
        P(every, "x"),
        P("x", every),
    )
    out_specs = (
        P(depth, line, None),
        P(depth, line, None),
        P(every),
        P(every, "x"),
        P(every, "x"),
        P(every, "x"),
        P("x", every),
        P("x", None),
        P(every),
        P(every, "x"),
        P(every, "x"),
        P("x", every),
    )
    return jax.shard_map(local, mesh=fine, in_specs=in_specs, out_specs=out_specs, check_vma=False)
```

```python
import functools

import jax
import jax.numpy as jnp
import numpy as np
from jax import lax
from jax.experimental import pallas as pl
from jax.experimental.pallas import tpu as pltpu
from jax.sharding import Mesh, PartitionSpec as P

epsilon = 1e-06
masked_value = -1e30
far_bounds = (12, 16, 23, 32, 46, 64, 91)
f32 = jnp.float32
bf16 = jnp.bfloat16
lane = 128
ffn_order = (2, 3, 0, 1, 4, 5)
attn_order = (4, 2, 1, 0, 3, 5)
at_k, at_yl, at_zl, at_zh, at_yh, at_prefix, at_lists = range(7)


def bucket_of(relative, buckets):
    offset = jnp.abs(relative)
    far = jnp.full(offset.shape, buckets // 4, jnp.int32)
    for threshold in far_bounds:
        far = far + (offset >= threshold).astype(jnp.int32)
    return jnp.where(offset < buckets // 4, offset, far) + buckets // 2 * (relative > 0).astype(
        jnp.int32
    )


def dot(left, right, dims=((1,), (0,))):
    return lax.dot_general(left, right, (dims, ((), ())), preferred_element_type=f32)


def dot_nt(left, right):
    return dot(left, right, ((1,), (1,)))


def dot_tn(left, right):
    return dot(left, right, ((0,), (0,)))


def fetch(value, axis, step):
    size = lax.axis_size(axis)
    return lax.ppermute(value, axis, [((i + step) % size, i) for i in range(size)])


def swap(value, axis):
    return fetch(value, axis, 1)


def gather(value, axis):
    return [value] + [fetch(value, axis, e) for e in range(1, lax.axis_size(axis))]


def send_sums(sends, axis):
    size = lax.axis_size(axis)
    return [fetch(sends[e - 1], axis, size - e) for e in range(1, size)]


class Clock:
    def __init__(self, token):
        self.token = token

    def tick(self, *values):
        self.token, *values = lax.optimization_barrier((self.token, *values))
        return values


def runs_of(dims, order, inverse):
    index = np.arange(int(np.prod(dims))).reshape(dims).transpose(order).reshape(-1)
    if inverse:
        index = np.argsort(index)
    cuts = [0, *(np.flatnonzero(np.diff(index) != 1) + 1).tolist(), len(index)]
    return [(int(index[a]), int(index[a]) + b - a) for a, b in zip(cuts[:-1], cuts[1:])]


def reorder(value, dims, order, inverse=False):
    return jnp.concatenate([value[:, a:b] for a, b in runs_of(dims, order, inverse)], axis=1)


def inv_scale(values):
    return lax.rsqrt(jnp.mean(values * values, axis=-1, keepdims=True) + epsilon)


def norm_back(scale, normed, grad_normed):
    return scale * (grad_normed - normed * jnp.mean(grad_normed * normed, axis=-1, keepdims=True))


def aligned(index, size):
    return pl.ds(pl.multiple_of(index * size, size), size)


def call(body, name, here, arrays, outs, scratch=(), raw=0, **static):
    space = pl.BlockSpec(memory_space=pltpu.VMEM)
    spaces = [pl.BlockSpec(memory_space=pltpu.HBM)] * raw + [space] * (len(arrays) - raw)
    need = sum(int(np.prod(s.shape)) * jnp.dtype(s.dtype).itemsize for s in scratch[: len(scratch) - bool(raw)])
    need += (6 << 20) if static.get("dims", (lane,))[-1] >= 32 else (40 << 20)
    return pl.pallas_call(
        functools.partial(body, **static),
        out_shape=tuple(jax.ShapeDtypeStruct(shape, kind) for shape, kind in outs),
        in_specs=[pl.BlockSpec(memory_space=pltpu.SMEM)] + spaces,
        out_specs=tuple(space for _ in outs),
        scratch_shapes=scratch,
        compiler_params=pltpu.CompilerParams(vmem_limit_bytes=(56 << 20) if raw else need),
        cost_estimate=pl.CostEstimate(flops=2_000_000_000, bytes_accessed=8_000_000, transcendentals=0),
        name=name,
    )(here, *arrays)


def place_body(here, own, got, out, *, which):
    at = here[which]
    out[at] = own[...]
    out[1 - at] = got[...]


def pack_attn_body(here, wq, wk, wv, wo, one, two, own, send, mats, gains, sems):
    part, wide = mats.shape[1:]
    half = wide // 2
    copies = [
        pltpu.make_async_copy(ref, room, sems.at[i])
        for i, (ref, room) in enumerate(
            [*((ref, mats.at[i]) for i, ref in enumerate((wq, wk, wv, wo))), (one, gains.at[0]), (two, gains.at[1])]
        )
    ]
    for copy in copies:
        copy.start()
    for copy in copies:
        copy.wait()
    low = jnp.concatenate([mats[i, :, :half] for i in range(4)], axis=1)
    high = jnp.concatenate([mats[i, :, half:] for i in range(4)], axis=1)
    row = lax.broadcasted_iota(jnp.int32, (8, part), 0)
    first, second = (jnp.broadcast_to(gains[i].astype(f32), (8, part)) for i in range(2))
    head = jnp.where(row == 0, first, jnp.where(row == 1, second, 0.0)).astype(bf16)

    def write(out, mat):
        out[:8] = jnp.zeros((8, out.shape[1]), bf16)
        out[:8, :part] = head
        out[8:] = mat

    @pl.when(here[at_yl] == 0)
    def _():
        write(own, low)
        write(send, high)

    @pl.when(here[at_yl] != 0)
    def _():
        write(own, high)
        write(send, low)


def pack_ffn_body(here, wg, wu, wd, own, send, room, *, chunks):
    hidden = wg.shape[1]
    whole = hidden // lane * lane
    room[:, :, whole:] = jnp.zeros((3, wg.shape[0], 4 * chunks * lane - whole), bf16)
    room[0, :, :hidden] = wg[...]
    room[1, :, :hidden] = wu[...]
    room[2, :, :hidden] = wd[...]
    for out, core in ((own, here[at_k]), (send, 1 - here[at_k])):
        for h in range(2):
            for j in range(chunks):
                for m in range(3):
                    out[h, j, :, m * lane : (m + 1) * lane] = room[
                        m, :, aligned((2 * h + core) * chunks + j, lane)
                    ]


def place_ffn_body(here, own, got, near, first, rest, *, chunks):
    k, zl = here[at_k], here[at_zl]
    for j in range(chunks):
        near[j, k] = own[zl, j]
        near[j, 1 - k] = got[zl, j]
        out, at = (rest, j - 1) if j else (first, 0)
        out[at, k] = own[1 - zl, j]
        out[at, 1 - k] = got[1 - zl, j]


def place_first_body(here, near, got, out):
    zl = here[at_zl]
    out[zl] = near[0]
    out[1 - zl] = got[0]


def place_rest_body(here, near, rest, whole, *outs):
    zl = here[at_zl]
    j = 0
    for group in outs:
        for at in range(group.shape[0]):
            for out in (whole.at[j], group.at[at]):
                out[zl] = near[j + 1]
                out[1 - zl] = rest[j]
            j += 1


def buckets_row(span, buckets):
    return bucket_of(lax.broadcasted_iota(jnp.int32, (1, 2 * span), 1) - span, buckets)


def rows_body(here, table, *refs, dims, heads):
    *blocks, out, grads_out, lines = refs
    grads, blocks = blocks[:4], blocks[4:]
    rows = grads[0].shape[0]
    for at, block in enumerate(blocks):
        values = block[...].astype(f32)
        out[at * rows : (at + 1) * rows] = reorder(values * inv_scale(values), dims, attn_order)
    for at, block in enumerate(grads):
        low = reorder(block[...].astype(f32), dims, ffn_order)
        grads_out[at * rows : (at + 1) * rows] = low.astype(bf16)
    buckets = table.shape[1]
    values = table[...].astype(f32)
    mine = jnp.where(here[at_yl] == 0, values[:heads], values[heads:])
    row = buckets_row(lines.shape[1] // 2, buckets)
    line = jnp.zeros((heads, lines.shape[1]), f32)
    for b in range(buckets):
        line = line + jnp.where(row == b, mine[:, b : b + 1], 0.0)
    lines[...] = jnp.zeros_like(lines)
    lines[:heads] = line


def bias_block(line_ref, head, start, rows):
    line = line_ref[pl.ds(head, 1), pl.ds(pl.multiple_of(start, rows), 2 * rows)]
    spread = jnp.broadcast_to(line, (rows, 2 * rows))
    return pltpu.roll(spread, 0, 1, stride=1, stride_axis=0)[:, rows:]


def attend_body(
    here, normed, pack_own, pack_other, lines,
    qkv, probs_out, attended, keep, send, inputs, w_own, w_other, gains, *, sizes, dims
):
    rows, heads, width, query_blocks, key_blocks, span = sizes
    prefix = here[at_prefix]
    inner = heads * width
    half = w_own.shape[0]
    part = dims[-1]
    gain_parts = []
    for pack, weights in ((pack_own, w_own), (pack_other, w_other)):
        for at in range(half // part):
            weights[at * part : (at + 1) * part] = pack[at, 8:]
        gain_parts.append(
            [
                jnp.concatenate([pack[at, i : i + 1, :part].astype(f32) for at in range(half // part)], axis=1)
                for i in range(2)
            ]
        )
    for i in range(2):
        low, high = gain_parts[0][i], gain_parts[1][i]
        gain = jnp.where(
            here[at_k] == 0,
            jnp.concatenate([low, high], axis=1),
            jnp.concatenate([high, low], axis=1),
        )
        if i == 0:
            inputs[...] = (normed[...] * gain).astype(bf16)
        gains[i : i + 1] = reorder(gain, dims, attn_order, True)
    places = [here[at_lists + i] for i in range(key_blocks)]
    mine, other = aligned(here[at_k], half), aligned(1 - here[at_k], half)
    qkv[...] = (
        dot(inputs[:, mine], w_own[:, : 3 * inner]) + dot(inputs[:, other], w_other[:, : 3 * inner])
    ).astype(bf16)
    for head in range(heads):
        lanes = slice(head * width, (head + 1) * width)
        keys = qkv[:, inner + head * width : inner + (head + 1) * width]
        values = qkv[:, 2 * inner + head * width : 2 * inner + (head + 1) * width]
        for at, block in enumerate(query_blocks):
            query_block = places[block]
            queries = qkv[block * rows : (block + 1) * rows, lanes]
            raw = dot_nt(queries, keys)
            query_pos = query_block * rows + lax.broadcasted_iota(jnp.int32, (rows, rows), 0)
            parts = []
            for key_at, key_block in enumerate(places):
                start = (key_block - query_block) * rows + span - rows
                key_pos = key_block * rows + lax.broadcasted_iota(jnp.int32, (rows, rows), 1)
                allowed = (key_pos <= query_pos) | (key_pos < prefix)
                biased = raw[:, key_at * rows : (key_at + 1) * rows] + bias_block(
                    lines, head, start, rows
                )
                parts.append(jnp.where(allowed, biased, masked_value))
            scores = jnp.concatenate(parts, axis=1)
            top = jnp.max(scores, axis=1, keepdims=True)
            powers = jnp.exp(scores - top)
            probs = powers / jnp.sum(powers, axis=1, keepdims=True)
            probs_out[head, at * rows : (at + 1) * rows, :] = probs
            attended[at * rows : (at + 1) * rows, lanes] = dot(probs.astype(bf16), values).astype(
                bf16
            )
    for lanes, weights in ((mine, w_own), (other, w_other)):
        out = dot_nt(attended[...], weights[:, 3 * inner :])
        keep[:, lanes] = out[:rows]
        send[:, lanes] = out[rows:].astype(bf16)


def norm_body(here, own, got, tokens, gains, residual, low, *, dims):
    total = own[...].astype(f32) + got[...].astype(f32)
    values = tokens[...].astype(f32) + reorder(total, dims, attn_order, True)
    residual[...] = values
    low[...] = reorder(values * inv_scale(values) * gains[1:2], dims, ffn_order).astype(bf16)


def tall(refs, lanes):
    return jnp.concatenate([ref[:, lanes] for ref in refs], axis=0)


def ffn_body(here, *refs, where, picks):
    rows, grads, weights, (first_out, hidden_out) = refs[:4], refs[4], refs[5:-2], refs[-2:]
    weights = [w if at is None else w.at[at] for at, w in zip(picks, weights)]
    size = weights[0].shape[0]
    first, d_hidden = None, None
    for at, w in enumerate(weights):
        lanes = aligned(here[where + at], size)
        first_part = dot(tall(rows, lanes), w[:, : 2 * lane])
        d_part = dot(grads[:, lanes], w[:, 2 * lane :])
        first = first_part if first is None else first + first_part
        d_hidden = d_part if d_hidden is None else d_hidden + d_part
    gate, up = first[:, :lane], first[:, lane:]
    root = float(np.sqrt(2.0 / np.pi))
    square = gate * gate
    bend = jnp.tanh(root * gate * (1.0 + 0.044715 * square))
    half = 0.5 * (1.0 + bend)
    active = gate * half
    slope = half + 0.5 * gate * (1.0 - bend * bend) * (root * (1.0 + 3.0 * 0.044715 * square))
    hidden_out[...] = (active * up).astype(bf16)
    first_out[:, :lane] = (d_hidden * up * slope).astype(bf16)
    first_out[:, lane:] = (d_hidden * active).astype(bf16)


def back_body(here, *refs, where, chunks, picks, lanes):
    lefts, weights, (keep, send) = refs[:chunks], refs[chunks:-2], refs[-2:]
    weights = [w if at is None else w.at[at] for at, w in zip(picks, weights)]
    blocks = len(weights) // chunks
    rows = keep.shape[1]
    for at in range(blocks):
        total = None
        for j in range(chunks):
            w = weights[j * blocks + at]
            part = dot_nt(lefts[j][...], w[:, lanes])
            total = part if total is None else total + part
        here_lanes = aligned(here[where + at], w.shape[0])
        for a in range(2):
            keep[a, :, here_lanes] = total[2 * a * rows : (2 * a + 1) * rows]
            send[a, :, here_lanes] = total[(2 * a + 1) * rows : (2 * a + 2) * rows].astype(bf16)


def ffn_grad_body(here, *refs, outer):
    rows, grads, (first, hidden, keep, send) = refs[:4], refs[4], refs[5:]
    size = keep.shape[1]
    for e in range(outer):
        yh = here[at_yh] + e
        yh = jnp.where(yh >= outer, yh - outer, yh) * 2
        for out, y in ((keep, yh + here[at_yl]), (send, yh + 1 - here[at_yl])):
            lanes = aligned(y, size)
            out[e, :, : 2 * lane] = dot_tn(tall(rows, lanes), first[...]).astype(out.dtype)
            out[e, :, 2 * lane :] = dot_tn(grads[:, lanes], hidden[...]).astype(out.dtype)


def table_parts(values):
    high = values.astype(bf16)
    return jnp.concatenate([high, (values - high.astype(f32)).astype(bf16)], axis=0)


def table_value(parts):
    half = parts.shape[0] // 2
    return parts[:half].astype(f32) + parts[half:].astype(f32)


def split_body(here, own, *refs, which, count, tail):
    *got, keep, send = refs
    size = keep.shape[0] - tail

    def piece(ref, at):
        if size % 8 == 0:
            return ref[aligned(at, size)]
        value = ref[:size]
        for i in range(1, count):
            value = jnp.where(at == i, ref[i * size : (i + 1) * size], value)
        return value

    for e in range(count):
        at = here[which] + e
        at = jnp.where(at >= count, at - count, at)
        total = piece(own, at)
        for ref in got:
            total = total + piece(ref, at).astype(f32)
        if e:
            send[e - 1, :size] = total.astype(bf16)
        else:
            keep[:size] = total
    if tail:
        total = own[count * size :]
        for ref in got:
            total = total + table_value(ref[count * size :])
        parts = table_parts(total)
        keep[size:] = table_value(parts)
        for e in range(count - 1):
            send[e, size:] = parts


def split(here, which, count, own, got, tail=0):
    size = (own.shape[0] - tail // 2) // count
    return call(
        split_body,
        "split",
        here,
        [own, *got],
        [((size + tail // 2, own.shape[1]), f32), ((count - 1, size + tail, own.shape[1]), bf16)],
        which=which,
        count=count,
        tail=tail // 2,
    )


def ffn_split_body(here, *refs, chunks):
    done, core, other = refs[-3:]
    each = (len(refs) - 3) // chunks
    zl, k = here[at_zl], here[at_k]
    for j in range(chunks):
        own, *got = refs[j * each : (j + 1) * each]

        def total(depth, slice_):
            value = own[depth, slice_]
            for ref in got:
                value = value + ref[depth, slice_].astype(f32)
            return value

        done[j] = total(zl, k)
        core[j] = total(zl, 1 - k).astype(bf16)
        other[j, 0] = total(1 - zl, 0).astype(bf16)
        other[j, 1] = total(1 - zl, 1).astype(bf16)


def sum_row(values):
    sums = jnp.sum(values, axis=1, keepdims=True)
    return jnp.broadcast_to(sums, (values.shape[0], lane)).T[0:1]


def ffn_final_body(here, *refs, groups):
    parts, rest = refs[: 4 * groups], refs[4 * groups :]
    wg, wu, gain, first_row, grad_g, grad_u, grad_d, grad_gain, room = rest
    hidden = wg.shape[1]
    chunks = room.shape[2] // (4 * lane)
    zl, k = here[at_zl], here[at_k]
    j = 0
    for group in range(groups):
        done, other, core, far = parts[4 * group : 4 * group + 4]
        for at in range(done.shape[0]):
            for h, c, value in (
                (zl, k, done[at]),
                (1 - zl, k, other[at, k].astype(f32)),
                (zl, 1 - k, core[at].astype(f32)),
                (1 - zl, 1 - k, far[at, k].astype(f32)),
            ):
                for m in range(3):
                    room[m, :, aligned((2 * h + c) * chunks + j, lane)] = value[
                        :, m * lane : (m + 1) * lane
                    ]
            j += 1
    gate, up = room[0, :, :hidden], room[1, :, :hidden]
    grad_g[...] = gate
    grad_u[...] = up
    grad_d[...] = room[2, :, :hidden]
    sums = gate * wg[...].astype(f32) + up * wu[...].astype(f32)
    grad_gain[0:1] = first_row[...]
    grad_gain[1:2] = sum_row(sums) / gain[...].astype(f32)


def pair_body(here, own, got, keep, send):
    keep[...] = own[0] + got[0].astype(f32)
    send[...] = (own[1] + got[1].astype(f32)).astype(bf16)


def residual_back_body(here, own, got, residual, cotangent, gains, d_residual, d_low, *, dims):
    total = own[...].astype(f32) + got[...].astype(f32)
    grad_normed = reorder(total, dims, ffn_order, True) * gains[1:2]
    values = residual[...]
    scale = inv_scale(values)
    back = cotangent[...].astype(f32) + norm_back(scale, values * scale, grad_normed)
    d_residual[...] = back
    d_low[...] = reorder(back, dims, attn_order).astype(bf16)


def attend_back_body(
    here, qkv, probs_in, d_own, d_far, w_own, w_other,
    d_query, d_keep, d_send, table, lines, d_att, *, sizes, buckets
):
    rows, heads, width, query_blocks, key_blocks, span = sizes
    inner = heads * width
    half = w_own.shape[0]
    places = [here[at_lists + i] for i in range(key_blocks)]
    mine, other = aligned(here[at_k], half), aligned(1 - here[at_k], half)
    d_rows = (d_own, d_far)
    d_att[...] = (
        dot(tall(d_rows, mine), w_own[:, 3 * inner :])
        + dot(tall(d_rows, other), w_other[:, 3 * inner :])
    ).astype(bf16)
    lines[...] = jnp.zeros_like(lines)
    up, down = (lax.broadcasted_iota(jnp.int32, (rows, rows), axis) for axis in (0, 1))
    flip = (up + down == rows - 1).astype(bf16)
    for head in range(heads):
        lanes = slice(head * width, (head + 1) * width)
        value_lanes = slice(inner + head * width, inner + (head + 1) * width)
        keys = qkv[:, inner + head * width : inner + (head + 1) * width]
        values = qkv[:, 2 * inner + head * width : 2 * inner + (head + 1) * width]
        d_key, d_value = None, None
        for at, block in enumerate(query_blocks):
            queries = qkv[block * rows : (block + 1) * rows, lanes]
            d_attended = d_att[at * rows : (at + 1) * rows, lanes]
            probs = probs_in[head, at * rows : (at + 1) * rows, :]
            d_probs = dot_nt(d_attended, values)
            delta = jnp.sum(probs * d_probs, axis=1, keepdims=True)
            d_scores = (probs * (d_probs - delta)).astype(bf16)
            d_query[at * rows : (at + 1) * rows, lanes] = dot(d_scores, keys).astype(bf16)
            key_part = dot_tn(d_scores, queries)
            value_part = dot_tn(probs.astype(bf16), d_attended)
            d_key = key_part if d_key is None else d_key + key_part
            d_value = value_part if d_value is None else d_value + value_part
            upward = dot(flip, d_scores)
            for key_at, key_block in enumerate(places):
                start = (key_block - places[block]) * rows + span - rows
                piece = upward[:, key_at * rows : (key_at + 1) * rows]
                padded = jnp.concatenate([piece, jnp.zeros_like(piece)], axis=1)
                turned = pltpu.roll(padded, 1, 1, stride=1, stride_axis=0)
                span_at = pl.ds(pl.multiple_of(start, rows), 2 * rows)
                lines[pl.ds(head, 1), span_at] += jnp.sum(turned, axis=0, keepdims=True)
        for key_at in range(key_blocks):
            from_, to = slice(key_at * rows, (key_at + 1) * rows), key_at // 2
            for out, parity in ((d_keep, 0), (d_send, 1)):
                if key_at % 2 == parity:
                    out[to, :, lanes] = d_key[from_].astype(out.dtype)
                    out[to, :, value_lanes] = d_value[from_].astype(out.dtype)
    row = buckets_row(span, buckets)
    column = lax.broadcasted_iota(jnp.int32, table.shape, 1)
    total = jnp.zeros(table.shape, f32)
    for b in range(buckets):
        one = jnp.sum(jnp.where(row == b, lines[...], 0.0), axis=1, keepdims=True)
        total = jnp.where(column == b, one, total)
    table[...] = total


def attn_grad_body(
    here, inputs, d_query, d_keep, d_got, d_own, d_far, attended, w_own, w_other, table,
    g_keep, g_send, keep, send, d_qkv, *, sizes
):
    rows, heads, width, query_blocks, key_blocks, span = sizes
    inner = heads * width
    half = w_own.shape[0]
    mine, other = aligned(here[at_k], half), aligned(1 - here[at_k], half)
    d_qkv[:, :inner] = d_query[...]
    for at in range(2):
        d_qkv[at * rows : (at + 1) * rows, inner:] = (d_keep[at] + d_got[at].astype(f32)).astype(bf16)
    for lanes, weights, out in ((mine, w_own, keep), (other, w_other, send)):
        part = dot_nt(d_qkv[...], weights[:, : 3 * inner])
        g_keep[:, lanes] = part[:rows]
        g_send[:, lanes] = part[rows:].astype(bf16)
        two = jnp.concatenate([inputs[b * rows : (b + 1) * rows, lanes] for b in query_blocks], axis=0)
        out[:half, : 3 * inner] = dot_tn(two, d_qkv[...]).astype(out.dtype)
        out[:half, 3 * inner :] = dot_tn(tall((d_own, d_far), lanes), attended[...]).astype(out.dtype)
    parts = table_parts(table[...])
    keep[half:] = jnp.zeros((keep.shape[0] - half, keep.shape[1]), f32)
    send[half:] = jnp.zeros((send.shape[0] - half, send.shape[1]), bf16)
    keep[half:, :lane] = table_value(parts)
    send[half:, :lane] = parts


def input_grad_body(here, own, got, tokens, gains, d_residual, out, *, dims):
    total = own[...].astype(f32) + got[...].astype(f32)
    grad_normed = reorder(total, dims, attn_order, True) * gains[0:1]
    values = tokens[...].astype(f32)
    scale = inv_scale(values)
    out[...] = (d_residual[...] + norm_back(scale, values * scale, grad_normed)).astype(bf16)


def mixed_body(here, own, got, residual, out, *, dims):
    total = own[...].astype(f32) + got[...].astype(f32)
    out[...] = (residual[...] + reorder(total, dims, ffn_order, True)).astype(bf16)


def attn_final_body(here, own, got, wq, wk, wv, gain, gq, gk, gv, go, grad_gain, table, *, heads):
    part, inner = gq.shape[0], own.shape[1] // 4

    def finish(low, high, low_table, high_table):
        grads = [
            jnp.concatenate([m[:, i * inner : (i + 1) * inner] for m in (low, high)], axis=1)
            for i in range(4)
        ]
        sums = 0.0
        for out, weights, grad in ((gq, wq, grads[0]), (gk, wk, grads[1]), (gv, wv, grads[2])):
            out[...] = grad
            sums = sums + grad * weights[...].astype(f32)
        go[...] = grads[3]
        grad_gain[...] = sum_row(sums) / gain[...].astype(f32)
        table[...] = jnp.concatenate([low_table[:heads], high_table[:heads]], axis=0)

    values = own[:part], got[:part].astype(f32)
    tables = own[part:, :lane], table_value(got[part:, :lane])

    @pl.when(here[at_yl] == 0)
    def _():
        finish(*values, *tables)

    @pl.when(here[at_yl] != 0)
    def _():
        finish(*values[::-1], *tables[::-1])


def local(
    tokens,
    cotangent,
    prefix,
    norm_one,
    w_query,
    w_key,
    w_value,
    w_out,
    position_bias_matrix,
    norm_two,
    w_gate,
    w_up,
    w_down,
):
    outer, deep = lax.axis_size("yh"), lax.axis_size("zh")
    rows, wide = tokens.shape[1:]
    part = w_query.shape[0]
    heads_dev, buckets = position_bias_matrix.shape
    heads = heads_dev // 2
    width = w_query.shape[1] // heads_dev
    inner = heads * width
    hidden_dev = w_gate.shape[1]
    chunks = -(-hidden_dev // (4 * lane))
    length = rows * outer * 4
    dims = (deep, 2, outer, 2, 2, part)
    half = wide // 2
    key_blocks = 4 * outer
    sizes = (rows, heads, width, (0, 2), key_blocks, length)

    tail = 16
    split_deep = deep == 2 and (4 * part) % lane == 0
    deep_blocks = deep if split_deep else 1
    yh, yl, k, zl, zh = (lax.axis_index(a) for a in ("yh", "yl", "k", "zl", "zh"))
    relative = [(e, a) for a in range(2) for e in range(outer)]
    ys = [((yh + e) % outer) * 2 + (yl + a) % 2 for e, a in relative]
    where = at_lists + key_blocks
    here = [k, yl, zl, zh, yh, prefix[0]]
    here += [
        ((yh + e) % outer) * 4 + ((yl + a) % 2) * 2 + (k + b) % 2
        for e in range(outer)
        for a in range(2)
        for b in range(2)
    ]
    here += [y * deep_blocks + (zh + d) % deep_blocks for d in range(deep_blocks) for y in ys]
    here = jnp.stack([jnp.asarray(v, jnp.int32) for v in here])
    tick = Clock(here).tick
    which = {"k": at_k, "yl": at_yl, "zl": at_zl, "zh": at_zh, "yh": at_yh}

    def kernel(body, name, arrays, outs, scratch=(), **static):
        return call(body, name, here, arrays, outs, scratch, **static)

    def place(pieces, axis):
        size, shape = len(pieces), pieces[0].shape
        if size == 1:
            return pieces[0][None]
        if size == 2:
            outs = [((2, *shape), pieces[0].dtype)]
            return kernel(place_body, "place", pieces, outs, which=which[axis])[0]
        stack = jnp.zeros((size, *shape), pieces[0].dtype)
        for e, piece in enumerate(pieces):
            at = (lax.axis_index(axis) + e) % size
            stack = lax.dynamic_update_slice_in_dim(stack, piece[None], at, 0)
        return stack

    def both(value, axis):
        return place(gather(value, axis), axis)

    tall_part = 8 + part
    own, send = kernel(
        pack_attn_body,
        "pack_attn",
        [w_query, w_key, w_value, w_out.T, norm_one[None], norm_two[None]],
        [((tall_part, 4 * inner), bf16)] * 2,
        [
            pltpu.VMEM((4, part, 2 * inner), bf16),
            pltpu.VMEM((2, 1, part), bf16),
            pltpu.SemaphoreType.DMA((6,)),
        ],
        raw=6,
    )
    own, send, own_grad, *ffn_in = tick(own, send, cotangent[0], w_gate, w_up, w_down.T)
    pack_got = swap(send, "yl")
    far_grad = swap(own_grad, "zl")
    ffn_own, ffn_send = kernel(
        pack_ffn_body,
        "pack_ffn",
        ffn_in,
        [((2, chunks, part, 3 * lane), bf16)] * 2,
        [pltpu.VMEM((3, part, 4 * chunks * lane), bf16)],
        chunks=chunks,
    )
    pack = place([own, pack_got], "yl")

    pack, ffn_own, ffn_send, own_tokens = tick(pack, ffn_own, ffn_send, tokens[0])
    pack_all = gather(pack, "zh")
    far_tokens = swap(own_tokens, "yl")
    near, near_first, near_rest = kernel(
        place_ffn_body,
        "place_ffn",
        [ffn_own, swap(ffn_send, "k")],
        [((n, 2, part, 3 * lane), bf16) for n in (chunks, 1, chunks - 1)],
        chunks=chunks,
    )
    pack = place(pack_all, "zh")

    pack, near, near_first, near_rest, far_tokens, own_tokens, far_grad, own_grad = tick(
        pack, near, near_first, near_rest, far_tokens, own_tokens, far_grad, own_grad
    )
    pack_all = gather(pack, "zl")
    first_got = swap(near_first, "zl")
    row_blocks = [p for pair in zip(gather(own_tokens, "yh"), gather(far_tokens, "yh")) for p in pair]
    row_blocks = [p for b in row_blocks for p in gather(b, "k")]
    grad_blocks = [p for b in (own_grad, far_grad) for p in gather(b, "k")]
    normed, grad_rows, lines = kernel(
        rows_body,
        "rows",
        [position_bias_matrix, *grad_blocks, *row_blocks],
        [((length, wide), f32), ((4 * rows, wide), bf16), ((8, 2 * length), f32)],
        dims=dims,
        heads=heads,
    )
    pack = place(pack_all, "zl")
    (near_zero,) = kernel(
        place_first_body, "place_first", [near, first_got], [((2, 2, part, 3 * lane), bf16)]
    )

    pack, near, near_zero, first_got, near_rest, normed, grad_rows, lines = tick(
        pack, near, near_zero, first_got, near_rest, normed, grad_rows, lines
    )
    pack = both(pack, "yh").reshape(half // part, tall_part, 4 * inner)
    pack_own, pack_other = gather(pack, "k")
    rest_got = swap(near_rest, "zl")

    groups = [[0], list(range(1, chunks - 1)), [chunks - 1]]

    def over_zh(value):
        pieces = gather(value, "zh")
        if split_deep:
            return pieces[1]
        return place(pieces, "zh").swapaxes(0, 1)

    def over_y(value):
        value = value.reshape(value.shape[0], -1, 3 * lane)
        return [p for b in gather(value, "yl") for p in gather(b, "yh")]

    far, far_y = [None] * 3, [None] * 3
    near_zero = near_zero[None]
    far[0] = over_zh(near_zero)
    zero_y = over_y(near_zero) if split_deep else []
    qkv, probs, attended, out_keep, out_send, attn_input, w_own, w_other, gains = kernel(
        attend_body,
        "attend",
        [normed, pack_own, pack_other, lines],
        [
            ((length, 3 * inner), bf16),
            ((heads, 2 * rows, length), f32),
            ((2 * rows, inner), bf16),
            ((rows, wide), f32),
            ((rows, wide), bf16),
            ((length, wide), bf16),
            ((half, 4 * inner), bf16),
            ((half, 4 * inner), bf16),
            ((2, wide), f32),
        ],
        sizes=sizes,
        dims=dims,
    )

    out_keep, out_send = tick(out_keep, out_send)
    out_got = swap(out_send, "yl")
    near, rest_got, far[0], *zero_y = tick(near, rest_got, far[0], *zero_y)
    shape = (2, 2, part, 3 * lane)
    whole, *nears = kernel(
        place_rest_body,
        "place_rest",
        [near, rest_got],
        [((chunks - 1, *shape), bf16)] + [((len(g), *shape), bf16) for g in groups[1:]],
    )
    out_keep, whole, *nears = tick(out_keep, whole, *nears)
    far[1] = over_zh(nears[0])
    rest_y = over_y(whole) if split_deep else []
    out_sum = (out_keep + out_got.astype(f32)).astype(bf16)

    out_sum, far[0] = tick(out_sum, far[0])
    out_other = swap(out_sum, "x")
    residual, low_two = kernel(
        norm_body,
        "norm",
        [out_sum, out_other, tokens[0], gains],
        [((rows, wide), f32), ((rows, wide), bf16)],
        dims=dims,
    )

    low_two, far[0], nears[1] = tick(low_two, far[0], nears[1])
    far_two, core_two = swap(low_two, "zl"), swap(low_two, "k")
    far_y[0] = over_y(far[0])
    core_two, far[1], nears[1], *rest_y = tick(core_two, far[1], nears[1], *rest_y)
    far[2] = over_zh(nears[1])
    far_y[1] = over_y(far[1])


    def weights_of(j):
        g = next(g for g, group in enumerate(groups) if j in group)
        at = j - groups[g][0]
        near_blocks = []
        if split_deep:
            own, others, near_at = (near_zero, zero_y, 0) if j == 0 else (whole, rest_y, j - 1)
            own = own.reshape(own.shape[0], -1, 3 * lane)
            near_blocks = [(v, near_at) for v in (own, *others[1:])]
        return near_blocks + [(v, at) for v in far_y[g]]

    def ffn(j):
        weights = weights_of(j)
        return kernel(
            ffn_body,
            "ffn",
            [*ffn_rows, grad_rows, *(w for w, _ in weights)],
            [((4 * rows, 2 * lane), bf16), ((4 * rows, lane), bf16)],
            where=where,
            picks=tuple(at for _, at in weights),
        )

    def back(lefts, lanes):
        weights = [w for j in range(chunks) for w in weights_of(j)]
        return kernel(
            back_body,
            "back",
            [*lefts, *(w for w, _ in weights)],
            [((2, rows, wide), f32), ((2, rows, wide), bf16)],
            where=where,
            chunks=chunks,
            picks=tuple(at for _, at in weights),
            lanes=lanes,
        )

    def ffn_grad(first, hidden):
        return kernel(
            ffn_grad_body,
            "ffn_grad",
            [*ffn_rows, grad_rows, first, hidden],
            [((outer, half // outer, 3 * lane), kind) for kind in (f32, bf16)],
            outer=outer,
        )

    def sum_y(keep, got):
        got = [got]
        if outer > 1:
            total = keep + got[0].astype(f32)
            got = send_sums([total[e].astype(bf16) for e in range(1, outer)], "yh")
            keep = total[0]
        flat = [v.reshape(deep * 4 * part, 3 * lane) for v in (keep, *got)]
        return split(here, at_zh, deep, flat[0], flat[1:])

    def sum_zh(keep, send):
        got = send_sums([send[e] for e in range(deep - 1)], "zh")
        return [v.reshape(2, 2, part, 3 * lane) for v in (keep, *got)]

    def pair(keep, got):
        shape = keep.shape[1:]
        return kernel(pair_body, "pair", [keep, got], [(shape, f32), (shape, bf16)])

    def ffn_split(group):
        count = len(group)
        return kernel(
            ffn_split_body,
            "ffn_split",
            [v for each in group for v in each],
            [
                ((count, part, 3 * lane), f32),
                ((count, part, 3 * lane), bf16),
                ((count, 2, part, 3 * lane), bf16),
            ],
            chunks=count,
        )

    far[2], far_two, core_two, *far_y[0] = tick(far[2], far_two, core_two, *far_y[0])
    far_y[2] = over_y(far[2])
    farcore_two = swap(far_two, "k")
    ffn_rows = [low_two, core_two, far_two, farcore_two]
    first_0, hidden_0 = ffn(0)
    grads = [None] * chunks
    grad_got, sums, zh_sums = [None] * chunks, [None] * chunks, [None] * chunks
    firsts, hiddens = [first_0], [hidden_0]
    for j in range(1, chunks):
        if j == chunks - 1:
            grads[0] = ffn_grad(firsts[0], hiddens[0])
            low_two, *flat = tick(low_two, *firsts, *hiddens, *grads[0])
            firsts, hiddens, grads[0] = flat[:j], flat[j : 2 * j], flat[2 * j :]
        elif j == 1:
            low_two, *flat = tick(low_two, *firsts, *hiddens)
            firsts, hiddens = flat[:1], flat[1:]
        ffn_rows[0] = low_two
        first, hidden = ffn(j)
        firsts.append(first)
        hiddens.append(hidden)
    keep, send = back(firsts, slice(0, 2 * lane))

    keep, send, *flat = tick(keep, send, *grads[0], *firsts[1:], *hiddens)
    grads[0], firsts, hiddens = flat[:2], [None, *flat[2:5]], flat[5:]
    core_got = swap(send, "k")
    grad_got[0] = swap(grads[0][1], "yl")
    grads[1] = ffn_grad(firsts[1], hiddens[1])
    core_keep, core_send = pair(keep, core_got)

    core_keep, core_send, *flat = tick(core_keep, core_send, *grads[1], *firsts[2:], *hiddens)
    grads[1], firsts, hiddens = flat[:2], [None, None, *flat[2:4]], flat[4:]
    core_got = swap(core_send, "zl")
    grad_got[1] = swap(grads[1][1], "yl")
    mixed_keep, mixed_send = back(hiddens, slice(2 * lane, 3 * lane))
    mixed_keep, mixed_send, *flat = tick(mixed_keep, mixed_send, *firsts[2:], *hiddens)
    firsts, hiddens = [None, None, *flat[:2]], flat[2:]
    mixed_got = swap(mixed_send, "k")
    grads[2] = ffn_grad(firsts[2], hiddens[2])
    grads[3] = ffn_grad(firsts[3], hiddens[3])
    mixed_keep, mixed_got, *flat = tick(mixed_keep, mixed_got, grads[0][0], *grads[2], *grads[3])
    grad_keep, grads[2], grads[3] = flat[0], flat[1:3], flat[3:]
    mixed_keep, mixed_send = pair(mixed_keep, mixed_got)
    sums[0] = sum_y(grad_keep, grad_got[0])
    core = (core_keep + core_got.astype(f32)).astype(bf16)

    core, mixed_keep, mixed_send, grad_keep, *flat = tick(
        core, mixed_keep, mixed_send, grads[1][0], *sums[0], *grads[2], *grads[3]
    )
    sums[0], grads[2], grads[3] = flat[:2], flat[2:4], flat[4:]
    core_other = swap(core, "x")
    zh_sums[0] = sum_zh(*sums[0])
    mixed_got = swap(mixed_send, "zl")
    sums[1] = sum_y(grad_keep, grad_got[1])
    d_residual, d_low = kernel(
        residual_back_body,
        "residual_back",
        [core, core_other, residual, cotangent[0], gains],
        [((rows, wide), f32), ((rows, wide), bf16)],
        dims=dims,
    )

    d_low, *flat = tick(d_low, *sums[1], *grads[2], *zh_sums[0])
    sums[1], grads[2], zh_sums[0] = flat[:2], flat[2:4], flat[4:]
    d_far = swap(d_low, "yl")
    grad_got[2] = swap(grads[2][1], "yl")
    zh_sums[1] = sum_zh(*sums[1])

    d_far, mixed_keep, mixed_got = tick(d_far, mixed_keep, mixed_got)
    mixed_half = (mixed_keep + mixed_got.astype(f32)).astype(bf16)
    mixed_other = swap(mixed_half, "x")
    d_query, d_keep, d_send, grad_table = kernel(
        attend_back_body,
        "attend_back",
        [qkv, probs, d_low, d_far, w_own, w_other],
        [
            ((2 * rows, inner), bf16),
            ((2 * outer, rows, 2 * inner), f32),
            ((2 * outer, rows, 2 * inner), bf16),
            ((8, lane), f32),
        ],
        [pltpu.VMEM((8, 2 * length), f32), pltpu.VMEM((2 * rows, inner), bf16)],
        sizes=sizes,
        buckets=buckets,
    )

    d_query, d_keep, d_send, grad_table, *zh_sums[1] = tick(
        d_query, d_keep, d_send, grad_table, *zh_sums[1]
    )
    d_got = swap(d_send, "k")
    if outer > 1:
        total = (d_keep + d_got.astype(f32)).reshape(outer, 2, rows, 2 * inner)
        arrived = send_sums([total[e].astype(bf16) for e in range(1, outer)], "yh")
        d_keep, d_got = total[0], sum(a.astype(f32) for a in arrived)
    g_keep, g_send, keep, send = kernel(
        attn_grad_body,
        "attn_grad",
        [attn_input, d_query, d_keep, d_got, d_low, d_far, attended, w_own, w_other, grad_table],
        [
            ((rows, wide), f32),
            ((rows, wide), bf16),
            ((half + tail // 2, 4 * inner), f32),
            ((half + tail, 4 * inner), bf16),
        ],
        [pltpu.VMEM((2 * rows, 3 * inner), bf16)],
        sizes=sizes,
    )

    g_keep, g_send, keep, send, grad_got[2], *grads[3] = tick(
        g_keep, g_send, keep, send, grad_got[2], *grads[3]
    )
    got = [swap(send, "k")]
    grad_got[3] = swap(grads[3][1], "yl")
    done_a = ffn_split(zh_sums[: chunks // 2])
    keep, grad_keep = tick(keep, grads[2][0])
    if outer > 1:
        keep, send = split(here, at_yh, outer, keep, got, tail)
        got = send_sums([send[e] for e in range(outer - 1)], "yh")
    sums[2] = sum_y(grad_keep, grad_got[2])
    keep, send = split(here, at_zl, 2, keep, got, tail)

    def spread(done):
        other = swap(done[2], "zl")
        return [done[0], other, swap(done[1], "k")]

    def over_cores(group):
        return [*group, swap(group[1], "k")]

    keep, send, g_keep, g_send, residual, *flat = tick(
        keep, send, g_keep, g_send, residual, *sums[2], *done_a
    )
    sums[2], done_a = flat[:2], flat[2:]
    got = send_sums([send[0]], "zl")
    zh_sums[2] = sum_zh(*sums[2])
    group_a = spread(done_a)
    g_got = swap(g_send, "yl")
    (mixed,) = kernel(
        mixed_body, "mixed", [mixed_half, mixed_other, residual], [((rows, wide), bf16)], dims=dims
    )
    keep, send = split(here, at_zh, deep, keep, got, tail)

    keep, send, mixed, grad_keep, *flat = tick(
        keep, send, mixed, grads[3][0], *zh_sums[2], *group_a[:2]
    )
    zh_sums[2], group_a[:2] = flat[:deep], flat[deep:]
    got = send_sums([send[e] for e in range(deep - 1)], "zh")
    sums[3] = sum_y(grad_keep, grad_got[3])
    zh_sums[3] = sum_zh(*sums[3])
    keep, send = split(here, at_yl, 2, keep, got, tail)

    keep, send, g_keep, g_got = tick(keep, send, g_keep, g_got)
    got = swap(send[0], "yl")
    got, zh_sums[3][0] = tick(got, zh_sums[3][0])
    g_sum = (g_keep + g_got.astype(f32)).astype(bf16)
    g_other = swap(g_sum, "x")
    group_a = over_cores(group_a)
    group_b = over_cores(spread(ffn_split(zh_sums[chunks // 2 :])))
    grad_query, grad_key, grad_value, grad_out, gain_row, grad_table = kernel(
        attn_final_body,
        "attn_final",
        [keep, got, w_query, w_key, w_value, norm_one[None]],
        [((part, 2 * inner), f32)] * 4 + [((1, part), f32), ((heads_dev, lane), f32)],
        heads=heads,
    )
    (input_grad,) = kernel(
        input_grad_body,
        "input_grad",
        [g_sum, g_other, tokens[0], gains, d_residual],
        [((rows, wide), bf16)],
        dims=dims,
    )
    gain_row, input_grad = tick(gain_row, input_grad)
    grad_gate, grad_up, grad_down, grad_gains = kernel(
        ffn_final_body,
        "ffn_final",
        [*group_a, *group_b, w_gate, w_up, norm_two[None], gain_row],
        [((part, hidden_dev), f32)] * 3 + [((2, part), f32)],
        [pltpu.VMEM((3, part, 4 * chunks * lane), f32)],
        groups=2,
    )
    grad_gains = grad_gains + swap(grad_gains, "x")
    return (
        mixed[None],
        input_grad[None],
        grad_gains[0],
        grad_query,
        grad_key,
        grad_value,
        grad_out.T,
        grad_table[:, :buckets],
        grad_gains[1],
        grad_gate,
        grad_up,
        grad_down.T,
    )


def solution(mesh):
    depths, lines, halves = (mesh.shape[a] for a in ("fsdp", "ctx", "tp"))
    fine = Mesh(
        mesh.devices.reshape(depths // 2, 2, lines // 4, 2, 2, halves),
        ("zh", "zl", "yh", "yl", "k", "x"),
    )
    depth, line = ("zh", "zl"), ("yh", "yl", "k")
    every = (*depth, *line)
    in_specs = (
        P(depth, line, None),
        P(depth, line, None),
        P(depth),
        P(every),
        P(every, "x"),
        P(every, "x"),
        P(every, "x"),
        P("x", every),
        P("x", None),
        P(every),
        P(every, "x"),
        P(every, "x"),
        P("x", every),
    )
    out_specs = (
        P(depth, line, None),
        P(depth, line, None),
        P(every),
        P(every, "x"),
        P(every, "x"),
        P(every, "x"),
        P("x", every),
        P("x", None),
        P(every),
        P(every, "x"),
        P(every, "x"),
        P("x", every),
    )
    return jax.shard_map(local, mesh=fine, in_specs=in_specs, out_specs=out_specs, check_vma=False)
```

```python
import functools

import jax
import jax.numpy as jnp
import numpy as np
from jax import lax
from jax.experimental import pallas as pl
from jax.experimental.pallas import tpu as pltpu
from jax.sharding import Mesh, PartitionSpec as P

epsilon = 1e-06
masked_value = -1e30
far_bounds = (12, 16, 23, 32, 46, 64, 91)
f32 = jnp.float32
bf16 = jnp.bfloat16
lane = 128
ffn_order = (2, 3, 0, 1, 4, 5)
attn_order = (4, 2, 1, 0, 3, 5)
at_k, at_yl, at_zl, at_zh, at_yh, at_prefix, at_lists = range(7)


def bucket_of(relative, buckets):
    offset = jnp.abs(relative)
    far = jnp.full(offset.shape, buckets // 4, jnp.int32)
    for threshold in far_bounds:
        far = far + (offset >= threshold).astype(jnp.int32)
    return jnp.where(offset < buckets // 4, offset, far) + buckets // 2 * (relative > 0).astype(
        jnp.int32
    )


def dot(left, right, dims=((1,), (0,))):
    return lax.dot_general(left, right, (dims, ((), ())), preferred_element_type=f32)


def dot_nt(left, right):
    return dot(left, right, ((1,), (1,)))


def dot_tn(left, right):
    return dot(left, right, ((0,), (0,)))


def fetch(value, axis, step):
    size = lax.axis_size(axis)
    return lax.ppermute(value, axis, [((i + step) % size, i) for i in range(size)])


def swap(value, axis):
    return fetch(value, axis, 1)


def gather(value, axis):
    return [value] + [fetch(value, axis, e) for e in range(1, lax.axis_size(axis))]


def send_sums(sends, axis):
    size = lax.axis_size(axis)
    return [fetch(sends[e - 1], axis, size - e) for e in range(1, size)]


class Clock:
    def __init__(self, token):
        self.token = token

    def tick(self, *values):
        self.token, *values = lax.optimization_barrier((self.token, *values))
        return values


def runs_of(dims, order, inverse):
    index = np.arange(int(np.prod(dims))).reshape(dims).transpose(order).reshape(-1)
    if inverse:
        index = np.argsort(index)
    cuts = [0, *(np.flatnonzero(np.diff(index) != 1) + 1).tolist(), len(index)]
    return [(int(index[a]), int(index[a]) + b - a) for a, b in zip(cuts[:-1], cuts[1:])]


def reorder(value, dims, order, inverse=False):
    return jnp.concatenate([value[:, a:b] for a, b in runs_of(dims, order, inverse)], axis=1)


def inv_scale(values):
    return lax.rsqrt(jnp.mean(values * values, axis=-1, keepdims=True) + epsilon)


def norm_back(scale, normed, grad_normed):
    return scale * (grad_normed - normed * jnp.mean(grad_normed * normed, axis=-1, keepdims=True))


def aligned(index, size):
    return pl.ds(pl.multiple_of(index * size, size), size)


def call(body, name, here, arrays, outs, scratch=(), raw=0, **static):
    space = pl.BlockSpec(memory_space=pltpu.VMEM)
    spaces = [pl.BlockSpec(memory_space=pltpu.HBM)] * raw + [space] * (len(arrays) - raw)
    need = sum(int(np.prod(s.shape)) * jnp.dtype(s.dtype).itemsize for s in scratch[: len(scratch) - bool(raw)])
    need += (6 << 20) if static.get("dims", (lane,))[-1] >= 32 else (40 << 20)
    return pl.pallas_call(
        functools.partial(body, **static),
        out_shape=tuple(jax.ShapeDtypeStruct(shape, kind) for shape, kind in outs),
        in_specs=[pl.BlockSpec(memory_space=pltpu.SMEM)] + spaces,
        out_specs=tuple(space for _ in outs),
        scratch_shapes=scratch,
        compiler_params=pltpu.CompilerParams(vmem_limit_bytes=(56 << 20) if raw else need),
        cost_estimate=pl.CostEstimate(flops=2_000_000_000, bytes_accessed=8_000_000, transcendentals=0),
        name=name,
    )(here, *arrays)


def place_body(here, own, got, out, *, which):
    at = here[which]
    out[at] = own[...]
    out[1 - at] = got[...]


def pack_attn_body(here, wq, wk, wv, wo, one, two, own, send, mats, gains, sems):
    part, wide = mats.shape[1:]
    half = wide // 2
    copies = [
        pltpu.make_async_copy(ref, room, sems.at[i])
        for i, (ref, room) in enumerate(
            [*((ref, mats.at[i]) for i, ref in enumerate((wq, wk, wv, wo))), (one, gains.at[0]), (two, gains.at[1])]
        )
    ]
    for copy in copies:
        copy.start()
    for copy in copies:
        copy.wait()
    low = jnp.concatenate([mats[i, :, :half] for i in range(4)], axis=1)
    high = jnp.concatenate([mats[i, :, half:] for i in range(4)], axis=1)
    row = lax.broadcasted_iota(jnp.int32, (8, part), 0)
    first, second = (jnp.broadcast_to(gains[i].astype(f32), (8, part)) for i in range(2))
    head = jnp.where(row == 0, first, jnp.where(row == 1, second, 0.0)).astype(bf16)

    def write(out, mat):
        out[:8] = jnp.zeros((8, out.shape[1]), bf16)
        out[:8, :part] = head
        out[8:] = mat

    @pl.when(here[at_yl] == 0)
    def _():
        write(own, low)
        write(send, high)

    @pl.when(here[at_yl] != 0)
    def _():
        write(own, high)
        write(send, low)


def pack_ffn_body(here, wg, wu, wd, own, send, room, *, chunks):
    hidden = wg.shape[1]
    whole = hidden // lane * lane
    room[:, :, whole:] = jnp.zeros((3, wg.shape[0], 4 * chunks * lane - whole), bf16)
    room[0, :, :hidden] = wg[...]
    room[1, :, :hidden] = wu[...]
    room[2, :, :hidden] = wd[...]
    for out, core in ((own, here[at_k]), (send, 1 - here[at_k])):
        for h in range(2):
            for j in range(chunks):
                for m in range(3):
                    out[h, j, :, m * lane : (m + 1) * lane] = room[
                        m, :, aligned((2 * h + core) * chunks + j, lane)
                    ]


def place_ffn_body(here, own, got, near, first, rest, *, chunks):
    k, zl = here[at_k], here[at_zl]
    for j in range(chunks):
        near[j, k] = own[zl, j]
        near[j, 1 - k] = got[zl, j]
        out, at = (rest, j - 1) if j else (first, 0)
        out[at, k] = own[1 - zl, j]
        out[at, 1 - k] = got[1 - zl, j]


def place_first_body(here, near, got, out):
    zl = here[at_zl]
    out[zl] = near[0]
    out[1 - zl] = got[0]


def place_rest_body(here, near, rest, whole, *outs):
    zl = here[at_zl]
    j = 0
    for group in outs:
        for at in range(group.shape[0]):
            for out in (whole.at[j], group.at[at]):
                out[zl] = near[j + 1]
                out[1 - zl] = rest[j]
            j += 1


def buckets_row(span, buckets):
    return bucket_of(lax.broadcasted_iota(jnp.int32, (1, 2 * span), 1) - span, buckets)


def rows_body(here, table, *refs, dims, heads):
    *blocks, out, grads_out, lines = refs
    grads, blocks = blocks[:4], blocks[4:]
    rows = grads[0].shape[0]
    for at, block in enumerate(blocks):
        values = block[...].astype(f32)
        out[at * rows : (at + 1) * rows] = reorder(values * inv_scale(values), dims, attn_order)
    for at, block in enumerate(grads):
        low = reorder(block[...].astype(f32), dims, ffn_order)
        grads_out[at * rows : (at + 1) * rows] = low.astype(bf16)
    buckets = table.shape[1]
    values = table[...].astype(f32)
    mine = jnp.where(here[at_yl] == 0, values[:heads], values[heads:])
    row = buckets_row(lines.shape[1] // 2, buckets)
    line = jnp.zeros((heads, lines.shape[1]), f32)
    for b in range(buckets):
        line = line + jnp.where(row == b, mine[:, b : b + 1], 0.0)
    lines[...] = jnp.zeros_like(lines)
    lines[:heads] = line


def bias_block(line_ref, head, start, rows):
    line = line_ref[pl.ds(head, 1), pl.ds(pl.multiple_of(start, rows), 2 * rows)]
    spread = jnp.broadcast_to(line, (rows, 2 * rows))
    return pltpu.roll(spread, 0, 1, stride=1, stride_axis=0)[:, rows:]


def attend_body(
    here, normed, pack_own, pack_other, lines,
    qkv, probs_out, attended, keep, send, inputs, w_own, w_other, gains, *, sizes, dims
):
    rows, heads, width, query_blocks, key_blocks, span = sizes
    prefix = here[at_prefix]
    inner = heads * width
    half = w_own.shape[0]
    part = dims[-1]
    gain_parts = []
    for pack, weights in ((pack_own, w_own), (pack_other, w_other)):
        for at in range(half // part):
            weights[at * part : (at + 1) * part] = pack[at, 8:]
        gain_parts.append(
            [
                jnp.concatenate([pack[at, i : i + 1, :part].astype(f32) for at in range(half // part)], axis=1)
                for i in range(2)
            ]
        )
    for i in range(2):
        low, high = gain_parts[0][i], gain_parts[1][i]
        gain = jnp.where(
            here[at_k] == 0,
            jnp.concatenate([low, high], axis=1),
            jnp.concatenate([high, low], axis=1),
        )
        if i == 0:
            inputs[...] = (normed[...] * gain).astype(bf16)
        gains[i : i + 1] = reorder(gain, dims, attn_order, True)
    places = [here[at_lists + i] for i in range(key_blocks)]
    mine, other = aligned(here[at_k], half), aligned(1 - here[at_k], half)
    qkv[...] = (
        dot(inputs[:, mine], w_own[:, : 3 * inner]) + dot(inputs[:, other], w_other[:, : 3 * inner])
    ).astype(bf16)
    for head in range(heads):
        lanes = slice(head * width, (head + 1) * width)
        keys = qkv[:, inner + head * width : inner + (head + 1) * width]
        values = qkv[:, 2 * inner + head * width : 2 * inner + (head + 1) * width]
        for at, block in enumerate(query_blocks):
            query_block = places[block]
            queries = qkv[block * rows : (block + 1) * rows, lanes]
            raw = dot_nt(queries, keys)
            query_pos = query_block * rows + lax.broadcasted_iota(jnp.int32, (rows, rows), 0)
            parts = []
            for key_at, key_block in enumerate(places):
                start = (key_block - query_block) * rows + span - rows
                key_pos = key_block * rows + lax.broadcasted_iota(jnp.int32, (rows, rows), 1)
                allowed = (key_pos <= query_pos) | (key_pos < prefix)
                biased = raw[:, key_at * rows : (key_at + 1) * rows] + bias_block(
                    lines, head, start, rows
                )
                parts.append(jnp.where(allowed, biased, masked_value))
            scores = jnp.concatenate(parts, axis=1)
            top = jnp.max(scores, axis=1, keepdims=True)
            powers = jnp.exp(scores - top)
            probs = powers / jnp.sum(powers, axis=1, keepdims=True)
            probs_out[head, at * rows : (at + 1) * rows, :] = probs
            attended[at * rows : (at + 1) * rows, lanes] = dot(probs.astype(bf16), values).astype(
                bf16
            )
    for lanes, weights in ((mine, w_own), (other, w_other)):
        out = dot_nt(attended[...], weights[:, 3 * inner :])
        keep[:, lanes] = out[:rows]
        send[:, lanes] = out[rows:].astype(bf16)


def norm_body(here, own, got, tokens, gains, residual, low, *, dims):
    total = own[...].astype(f32) + got[...].astype(f32)
    values = tokens[...].astype(f32) + reorder(total, dims, attn_order, True)
    residual[...] = values
    low[...] = reorder(values * inv_scale(values) * gains[1:2], dims, ffn_order).astype(bf16)


def tall(refs, lanes):
    return jnp.concatenate([ref[:, lanes] for ref in refs], axis=0)


def ffn_body(here, *refs, where, picks):
    rows, grads, weights, (first_out, hidden_out) = refs[:4], refs[4], refs[5:-2], refs[-2:]
    weights = [w if at is None else w.at[at] for at, w in zip(picks, weights)]
    size = weights[0].shape[0]
    first, d_hidden = None, None
    for at, w in enumerate(weights):
        lanes = aligned(here[where + at], size)
        first_part = dot(tall(rows, lanes), w[:, : 2 * lane])
        d_part = dot(grads[:, lanes], w[:, 2 * lane :])
        first = first_part if first is None else first + first_part
        d_hidden = d_part if d_hidden is None else d_hidden + d_part
    gate, up = first[:, :lane], first[:, lane:]
    root = float(np.sqrt(2.0 / np.pi))
    square = gate * gate
    bend = jnp.tanh(root * gate * (1.0 + 0.044715 * square))
    half = 0.5 * (1.0 + bend)
    active = gate * half
    slope = half + 0.5 * gate * (1.0 - bend * bend) * (root * (1.0 + 3.0 * 0.044715 * square))
    hidden_out[...] = (active * up).astype(bf16)
    first_out[:, :lane] = (d_hidden * up * slope).astype(bf16)
    first_out[:, lane:] = (d_hidden * active).astype(bf16)


def back_body(here, *refs, where, chunks, picks, lanes):
    lefts, weights, (keep, send) = refs[:chunks], refs[chunks:-2], refs[-2:]
    weights = [w if at is None else w.at[at] for at, w in zip(picks, weights)]
    blocks = len(weights) // chunks
    rows = keep.shape[1]
    for at in range(blocks):
        total = None
        for j in range(chunks):
            w = weights[j * blocks + at]
            part = dot_nt(lefts[j][...], w[:, lanes])
            total = part if total is None else total + part
        here_lanes = aligned(here[where + at], w.shape[0])
        for a in range(2):
            keep[a, :, here_lanes] = total[2 * a * rows : (2 * a + 1) * rows]
            send[a, :, here_lanes] = total[(2 * a + 1) * rows : (2 * a + 2) * rows].astype(bf16)


def ffn_grad_body(here, *refs, outer):
    rows, grads, (first, hidden, keep, send) = refs[:4], refs[4], refs[5:]
    size = keep.shape[1]
    for e in range(outer):
        yh = here[at_yh] + e
        yh = jnp.where(yh >= outer, yh - outer, yh) * 2
        for out, y in ((keep, yh + here[at_yl]), (send, yh + 1 - here[at_yl])):
            lanes = aligned(y, size)
            out[e, :, : 2 * lane] = dot_tn(tall(rows, lanes), first[...]).astype(out.dtype)
            out[e, :, 2 * lane :] = dot_tn(grads[:, lanes], hidden[...]).astype(out.dtype)


def table_parts(values):
    high = values.astype(bf16)
    return jnp.concatenate([high, (values - high.astype(f32)).astype(bf16)], axis=0)


def table_value(parts):
    half = parts.shape[0] // 2
    return parts[:half].astype(f32) + parts[half:].astype(f32)


def split_body(here, own, *refs, which, count, tail):
    *got, keep, send = refs
    size = keep.shape[0] - tail

    def piece(ref, at):
        if size % 8 == 0:
            return ref[aligned(at, size)]
        value = ref[:size]
        for i in range(1, count):
            value = jnp.where(at == i, ref[i * size : (i + 1) * size], value)
        return value

    for e in range(count):
        at = here[which] + e
        at = jnp.where(at >= count, at - count, at)
        total = piece(own, at)
        for ref in got:
            total = total + piece(ref, at).astype(f32)
        if e:
            send[e - 1, :size] = total.astype(bf16)
        else:
            keep[:size] = total
    if tail:
        total = own[count * size :]
        for ref in got:
            total = total + table_value(ref[count * size :])
        parts = table_parts(total)
        keep[size:] = table_value(parts)
        for e in range(count - 1):
            send[e, size:] = parts


def split(here, which, count, own, got, tail=0):
    size = (own.shape[0] - tail // 2) // count
    return call(
        split_body,
        "split",
        here,
        [own, *got],
        [((size + tail // 2, own.shape[1]), f32), ((max(count - 1, 1), size + tail, own.shape[1]), bf16)],
        which=which,
        count=count,
        tail=tail // 2,
    )


def ffn_split_body(here, *refs, chunks):
    done, core, other = refs[-3:]
    each = (len(refs) - 3) // chunks
    zl, k = here[at_zl], here[at_k]
    for j in range(chunks):
        own, *got = refs[j * each : (j + 1) * each]

        def total(depth, slice_):
            value = own[depth, slice_]
            for ref in got:
                value = value + ref[depth, slice_].astype(f32)
            return value

        done[j] = total(zl, k)
        core[j] = total(zl, 1 - k).astype(bf16)
        other[j, 0] = total(1 - zl, 0).astype(bf16)
        other[j, 1] = total(1 - zl, 1).astype(bf16)


def last_y_body(here, own, got, keep, send):
    zl = here[at_zl]
    for h in range(keep.shape[0]):
        keep[h] = own[h, zl] + got[h, zl].astype(f32)
        send[h] = (own[h, 1 - zl] + got[h, 1 - zl].astype(f32)).astype(bf16)


def ahead(here, which, count, e):
    at = here[which] + e
    return jnp.where(at >= count, at - count, at)


def last_z_body(here, own, got, send):
    count = own.shape[0]
    for e in range(1, count):
        at = ahead(here, at_zh, count, e)
        send[e - 1, 0] = own[at].astype(bf16)
        send[e - 1, 1] = got[at]


def last_body(here, own, got, *refs):
    *arrived, done, core, other = refs
    part = done.shape[1]
    zh, k = here[at_zh], here[at_k]
    mine, theirs = own[zh], got[zh].astype(f32)
    for ref in arrived:
        mine = mine + ref[0].astype(f32)
        theirs = theirs + ref[1].astype(f32)
    low, high = mine[:part], mine[part:]
    done[0] = jnp.where(k == 0, low, high)
    core[0] = jnp.where(k == 0, high, low).astype(bf16)
    other[0, 0] = theirs[:part].astype(bf16)
    other[0, 1] = theirs[part:].astype(bf16)


def sum_row(values):
    sums = jnp.sum(values, axis=1, keepdims=True)
    return jnp.broadcast_to(sums, (values.shape[0], lane)).T[0:1]


def ffn_final_body(here, *refs, groups):
    parts, rest = refs[: 4 * groups], refs[4 * groups :]
    wg, wu, gain, first_row, grad_g, grad_u, grad_d, grad_gain, room = rest
    hidden = wg.shape[1]
    chunks = room.shape[2] // (4 * lane)
    zl, k = here[at_zl], here[at_k]
    j = 0
    for group in range(groups):
        done, other, core, far = parts[4 * group : 4 * group + 4]
        for at in range(done.shape[0]):
            for h, c, value in (
                (zl, k, done[at]),
                (1 - zl, k, other[at, k].astype(f32)),
                (zl, 1 - k, core[at].astype(f32)),
                (1 - zl, 1 - k, far[at, k].astype(f32)),
            ):
                for m in range(3):
                    room[m, :, aligned((2 * h + c) * chunks + j, lane)] = value[
                        :, m * lane : (m + 1) * lane
                    ]
            j += 1
    gate, up = room[0, :, :hidden], room[1, :, :hidden]
    grad_g[...] = gate
    grad_u[...] = up
    grad_d[...] = room[2, :, :hidden]
    sums = gate * wg[...].astype(f32) + up * wu[...].astype(f32)
    grad_gain[0:1] = first_row[...]
    grad_gain[1:2] = sum_row(sums) / gain[...].astype(f32)


def pair_body(here, own, got, keep, send):
    keep[...] = own[0] + got[0].astype(f32)
    send[...] = (own[1] + got[1].astype(f32)).astype(bf16)


def residual_back_body(here, own, got, residual, cotangent, gains, d_residual, d_low, *, dims):
    total = own[...].astype(f32) + got[...].astype(f32)
    grad_normed = reorder(total, dims, ffn_order, True) * gains[1:2]
    values = residual[...]
    scale = inv_scale(values)
    back = cotangent[...].astype(f32) + norm_back(scale, values * scale, grad_normed)
    d_residual[...] = back
    d_low[...] = reorder(back, dims, attn_order).astype(bf16)


def attend_back_body(
    here, qkv, probs_in, d_own, d_far, w_own, w_other,
    d_query, d_keep, d_send, table, lines, d_att, *, sizes, buckets
):
    rows, heads, width, query_blocks, key_blocks, span = sizes
    inner = heads * width
    half = w_own.shape[0]
    places = [here[at_lists + i] for i in range(key_blocks)]
    mine, other = aligned(here[at_k], half), aligned(1 - here[at_k], half)
    d_rows = (d_own, d_far)
    d_att[...] = (
        dot(tall(d_rows, mine), w_own[:, 3 * inner :])
        + dot(tall(d_rows, other), w_other[:, 3 * inner :])
    ).astype(bf16)
    lines[...] = jnp.zeros_like(lines)
    up, down = (lax.broadcasted_iota(jnp.int32, (rows, rows), axis) for axis in (0, 1))
    flip = (up + down == rows - 1).astype(bf16)
    for head in range(heads):
        lanes = slice(head * width, (head + 1) * width)
        value_lanes = slice(inner + head * width, inner + (head + 1) * width)
        keys = qkv[:, inner + head * width : inner + (head + 1) * width]
        values = qkv[:, 2 * inner + head * width : 2 * inner + (head + 1) * width]
        d_key, d_value = None, None
        for at, block in enumerate(query_blocks):
            queries = qkv[block * rows : (block + 1) * rows, lanes]
            d_attended = d_att[at * rows : (at + 1) * rows, lanes]
            probs = probs_in[head, at * rows : (at + 1) * rows, :]
            d_probs = dot_nt(d_attended, values)
            delta = jnp.sum(probs * d_probs, axis=1, keepdims=True)
            d_scores = (probs * (d_probs - delta)).astype(bf16)
            d_query[at * rows : (at + 1) * rows, lanes] = dot(d_scores, keys).astype(bf16)
            key_part = dot_tn(d_scores, queries)
            value_part = dot_tn(probs.astype(bf16), d_attended)
            d_key = key_part if d_key is None else d_key + key_part
            d_value = value_part if d_value is None else d_value + value_part
            upward = dot(flip, d_scores)
            for key_at, key_block in enumerate(places):
                start = (key_block - places[block]) * rows + span - rows
                piece = upward[:, key_at * rows : (key_at + 1) * rows]
                padded = jnp.concatenate([piece, jnp.zeros_like(piece)], axis=1)
                turned = pltpu.roll(padded, 1, 1, stride=1, stride_axis=0)
                span_at = pl.ds(pl.multiple_of(start, rows), 2 * rows)
                lines[pl.ds(head, 1), span_at] += jnp.sum(turned, axis=0, keepdims=True)
        for key_at in range(key_blocks):
            from_, to = slice(key_at * rows, (key_at + 1) * rows), key_at // 2
            for out, parity in ((d_keep, 0), (d_send, 1)):
                if key_at % 2 == parity:
                    out[to, :, lanes] = d_key[from_].astype(out.dtype)
                    out[to, :, value_lanes] = d_value[from_].astype(out.dtype)
    row = buckets_row(span, buckets)
    column = lax.broadcasted_iota(jnp.int32, table.shape, 1)
    total = jnp.zeros(table.shape, f32)
    for b in range(buckets):
        one = jnp.sum(jnp.where(row == b, lines[...], 0.0), axis=1, keepdims=True)
        total = jnp.where(column == b, one, total)
    table[...] = total


def attn_grad_body(
    here, inputs, d_query, d_keep, d_got, d_own, d_far, attended, w_own, w_other, table,
    g_keep, g_send, keep, send, d_qkv, *, sizes
):
    rows, heads, width, query_blocks, key_blocks, span = sizes
    inner = heads * width
    half = w_own.shape[0]
    mine, other = aligned(here[at_k], half), aligned(1 - here[at_k], half)
    d_qkv[:, :inner] = d_query[...]
    for at in range(2):
        d_qkv[at * rows : (at + 1) * rows, inner:] = (d_keep[at] + d_got[at].astype(f32)).astype(bf16)
    for lanes, weights, out in ((mine, w_own, keep), (other, w_other, send)):
        part = dot_nt(d_qkv[...], weights[:, : 3 * inner])
        g_keep[:, lanes] = part[:rows]
        g_send[:, lanes] = part[rows:].astype(bf16)
        two = jnp.concatenate([inputs[b * rows : (b + 1) * rows, lanes] for b in query_blocks], axis=0)
        out[:half, : 3 * inner] = dot_tn(two, d_qkv[...]).astype(out.dtype)
        out[:half, 3 * inner :] = dot_tn(tall((d_own, d_far), lanes), attended[...]).astype(out.dtype)
    parts = table_parts(table[...])
    keep[half:] = jnp.zeros((keep.shape[0] - half, keep.shape[1]), f32)
    send[half:] = jnp.zeros((send.shape[0] - half, send.shape[1]), bf16)
    keep[half:, :lane] = table_value(parts)
    send[half:, :lane] = parts


def input_grad_body(here, own, got, tokens, gains, d_residual, out, *, dims):
    total = own[...].astype(f32) + got[...].astype(f32)
    grad_normed = reorder(total, dims, attn_order, True) * gains[0:1]
    values = tokens[...].astype(f32)
    scale = inv_scale(values)
    out[...] = (d_residual[...] + norm_back(scale, values * scale, grad_normed)).astype(bf16)


def mixed_body(here, own, got, residual, out, *, dims):
    total = own[...].astype(f32) + got[...].astype(f32)
    out[...] = (residual[...] + reorder(total, dims, ffn_order, True)).astype(bf16)


def attn_final_body(here, own, got, wq, wk, wv, gain, gq, gk, gv, go, grad_gain, table, *, heads):
    part, inner = gq.shape[0], own.shape[1] // 4

    def finish(low, high, low_table, high_table):
        grads = [
            jnp.concatenate([m[:, i * inner : (i + 1) * inner] for m in (low, high)], axis=1)
            for i in range(4)
        ]
        sums = 0.0
        for out, weights, grad in ((gq, wq, grads[0]), (gk, wk, grads[1]), (gv, wv, grads[2])):
            out[...] = grad
            sums = sums + grad * weights[...].astype(f32)
        go[...] = grads[3]
        grad_gain[...] = sum_row(sums) / gain[...].astype(f32)
        table[...] = jnp.concatenate([low_table[:heads], high_table[:heads]], axis=0)

    values = own[:part], got[:part].astype(f32)
    tables = own[part:, :lane], table_value(got[part:, :lane])

    @pl.when(here[at_yl] == 0)
    def _():
        finish(*values, *tables)

    @pl.when(here[at_yl] != 0)
    def _():
        finish(*values[::-1], *tables[::-1])


def local(
    tokens,
    cotangent,
    prefix,
    norm_one,
    w_query,
    w_key,
    w_value,
    w_out,
    position_bias_matrix,
    norm_two,
    w_gate,
    w_up,
    w_down,
):
    outer, deep = lax.axis_size("yh"), lax.axis_size("zh")
    rows, wide = tokens.shape[1:]
    part = w_query.shape[0]
    heads_dev, buckets = position_bias_matrix.shape
    heads = heads_dev // 2
    width = w_query.shape[1] // heads_dev
    inner = heads * width
    hidden_dev = w_gate.shape[1]
    chunks = -(-hidden_dev // (4 * lane))
    length = rows * outer * 4
    dims = (deep, 2, outer, 2, 2, part)
    half = wide // 2
    key_blocks = 4 * outer
    sizes = (rows, heads, width, (0, 2), key_blocks, length)

    tail = 16
    split_deep = deep == 2 and (4 * part) % lane == 0
    deep_blocks = deep if split_deep else 1
    yh, yl, k, zl, zh = (lax.axis_index(a) for a in ("yh", "yl", "k", "zl", "zh"))
    relative = [(e, a) for a in range(2) for e in range(outer)]
    ys = [((yh + e) % outer) * 2 + (yl + a) % 2 for e, a in relative]
    where = at_lists + key_blocks
    here = [k, yl, zl, zh, yh, prefix[0]]
    here += [
        ((yh + e) % outer) * 4 + ((yl + a) % 2) * 2 + (k + b) % 2
        for e in range(outer)
        for a in range(2)
        for b in range(2)
    ]
    here += [y * deep_blocks + (zh + d) % deep_blocks for d in range(deep_blocks) for y in ys]
    here = jnp.stack([jnp.asarray(v, jnp.int32) for v in here])
    tick = Clock(here).tick
    which = {"k": at_k, "yl": at_yl, "zl": at_zl, "zh": at_zh, "yh": at_yh}

    def kernel(body, name, arrays, outs, scratch=(), **static):
        return call(body, name, here, arrays, outs, scratch, **static)

    def place(pieces, axis):
        size, shape = len(pieces), pieces[0].shape
        if size == 1:
            return pieces[0][None]
        if size == 2:
            outs = [((2, *shape), pieces[0].dtype)]
            return kernel(place_body, "place", pieces, outs, which=which[axis])[0]
        stack = jnp.zeros((size, *shape), pieces[0].dtype)
        for e, piece in enumerate(pieces):
            at = (lax.axis_index(axis) + e) % size
            stack = lax.dynamic_update_slice_in_dim(stack, piece[None], at, 0)
        return stack

    def both(value, axis):
        return place(gather(value, axis), axis)

    tall_part = 8 + part
    own, send = kernel(
        pack_attn_body,
        "pack_attn",
        [w_query, w_key, w_value, w_out.T, norm_one[None], norm_two[None]],
        [((tall_part, 4 * inner), bf16)] * 2,
        [
            pltpu.VMEM((4, part, 2 * inner), bf16),
            pltpu.VMEM((2, 1, part), bf16),
            pltpu.SemaphoreType.DMA((6,)),
        ],
        raw=6,
    )
    own, send, own_grad, *ffn_in = tick(own, send, cotangent[0], w_gate, w_up, w_down.T)
    pack_got = swap(send, "yl")
    far_grad = swap(own_grad, "zl")
    ffn_own, ffn_send = kernel(
        pack_ffn_body,
        "pack_ffn",
        ffn_in,
        [((2, chunks, part, 3 * lane), bf16)] * 2,
        [pltpu.VMEM((3, part, 4 * chunks * lane), bf16)],
        chunks=chunks,
    )
    pack = place([own, pack_got], "yl")

    pack, ffn_own, ffn_send, own_tokens = tick(pack, ffn_own, ffn_send, tokens[0])
    pack_all = gather(pack, "zh")
    far_tokens = swap(own_tokens, "yl")
    near, near_first, near_rest = kernel(
        place_ffn_body,
        "place_ffn",
        [ffn_own, swap(ffn_send, "k")],
        [((n, 2, part, 3 * lane), bf16) for n in (chunks, 1, chunks - 1)],
        chunks=chunks,
    )
    pack = place(pack_all, "zh")

    pack, near, near_first, near_rest, far_tokens, own_tokens, far_grad, own_grad = tick(
        pack, near, near_first, near_rest, far_tokens, own_tokens, far_grad, own_grad
    )
    pack_all = gather(pack, "zl")
    first_got = swap(near_first, "zl")
    row_blocks = [p for pair in zip(gather(own_tokens, "yh"), gather(far_tokens, "yh")) for p in pair]
    row_blocks = [p for b in row_blocks for p in gather(b, "k")]
    grad_blocks = [p for b in (own_grad, far_grad) for p in gather(b, "k")]
    normed, grad_rows, lines = kernel(
        rows_body,
        "rows",
        [position_bias_matrix, *grad_blocks, *row_blocks],
        [((length, wide), f32), ((4 * rows, wide), bf16), ((8, 2 * length), f32)],
        dims=dims,
        heads=heads,
    )
    pack = place(pack_all, "zl")
    (near_zero,) = kernel(
        place_first_body, "place_first", [near, first_got], [((2, 2, part, 3 * lane), bf16)]
    )

    pack, near, near_zero, first_got, near_rest, normed, grad_rows, lines = tick(
        pack, near, near_zero, first_got, near_rest, normed, grad_rows, lines
    )
    pack = both(pack, "yh").reshape(half // part, tall_part, 4 * inner)
    pack_own, pack_other = gather(pack, "k")
    rest_got = swap(near_rest, "zl")

    groups = [[0], list(range(1, chunks - 1)), [chunks - 1]]

    def over_zh(value):
        pieces = gather(value, "zh")
        if split_deep:
            return pieces[1]
        return place(pieces, "zh").swapaxes(0, 1)

    def over_y(value):
        value = value.reshape(value.shape[0], -1, 3 * lane)
        return [p for b in gather(value, "yl") for p in gather(b, "yh")]

    far, far_y = [None] * 3, [None] * 3
    near_zero = near_zero[None]
    far[0] = over_zh(near_zero)
    zero_y = over_y(near_zero) if split_deep else []
    qkv, probs, attended, out_keep, out_send, attn_input, w_own, w_other, gains = kernel(
        attend_body,
        "attend",
        [normed, pack_own, pack_other, lines],
        [
            ((length, 3 * inner), bf16),
            ((heads, 2 * rows, length), f32),
            ((2 * rows, inner), bf16),
            ((rows, wide), f32),
            ((rows, wide), bf16),
            ((length, wide), bf16),
            ((half, 4 * inner), bf16),
            ((half, 4 * inner), bf16),
            ((2, wide), f32),
        ],
        sizes=sizes,
        dims=dims,
    )

    out_keep, out_send = tick(out_keep, out_send)
    out_got = swap(out_send, "yl")
    near, rest_got, far[0], *zero_y = tick(near, rest_got, far[0], *zero_y)
    shape = (2, 2, part, 3 * lane)
    whole, *nears = kernel(
        place_rest_body,
        "place_rest",
        [near, rest_got],
        [((chunks - 1, *shape), bf16)] + [((len(g), *shape), bf16) for g in groups[1:]],
    )
    out_keep, whole, *nears = tick(out_keep, whole, *nears)
    far[1] = over_zh(nears[0])
    rest_y = over_y(whole) if split_deep else []
    out_sum = (out_keep + out_got.astype(f32)).astype(bf16)

    out_sum, far[0] = tick(out_sum, far[0])
    out_other = swap(out_sum, "x")
    residual, low_two = kernel(
        norm_body,
        "norm",
        [out_sum, out_other, tokens[0], gains],
        [((rows, wide), f32), ((rows, wide), bf16)],
        dims=dims,
    )

    low_two, far[0], nears[1] = tick(low_two, far[0], nears[1])
    far_two, core_two = swap(low_two, "zl"), swap(low_two, "k")
    far_y[0] = over_y(far[0])
    core_two, far[1], nears[1], *rest_y = tick(core_two, far[1], nears[1], *rest_y)
    far[2] = over_zh(nears[1])
    far_y[1] = over_y(far[1])


    def weights_of(j):
        g = next(g for g, group in enumerate(groups) if j in group)
        at = j - groups[g][0]
        near_blocks = []
        if split_deep:
            own, others, near_at = (near_zero, zero_y, 0) if j == 0 else (whole, rest_y, j - 1)
            own = own.reshape(own.shape[0], -1, 3 * lane)
            near_blocks = [(v, near_at) for v in (own, *others[1:])]
        return near_blocks + [(v, at) for v in far_y[g]]

    def ffn(j):
        weights = weights_of(j)
        return kernel(
            ffn_body,
            "ffn",
            [*ffn_rows, grad_rows, *(w for w, _ in weights)],
            [((4 * rows, 2 * lane), bf16), ((4 * rows, lane), bf16)],
            where=where,
            picks=tuple(at for _, at in weights),
        )

    def back(lefts, lanes):
        weights = [w for j in range(chunks) for w in weights_of(j)]
        return kernel(
            back_body,
            "back",
            [*lefts, *(w for w, _ in weights)],
            [((2, rows, wide), f32), ((2, rows, wide), bf16)],
            where=where,
            chunks=chunks,
            picks=tuple(at for _, at in weights),
            lanes=lanes,
        )

    def ffn_grad(first, hidden):
        return kernel(
            ffn_grad_body,
            "ffn_grad",
            [*ffn_rows, grad_rows, first, hidden],
            [((outer, half // outer, 3 * lane), kind) for kind in (f32, bf16)],
            outer=outer,
        )

    def sum_yh(keep, got):
        if outer == 1:
            return keep, [got]
        total = keep + got.astype(f32)
        return total[0], send_sums([total[e].astype(bf16) for e in range(1, outer)], "yh")

    def sum_y(keep, got):
        keep, got = sum_yh(keep, got)
        flat = [v.reshape(deep * 4 * part, 3 * lane) for v in (keep, *got)]
        return split(here, at_zh, deep, flat[0], flat[1:])

    def sum_y_last(keep, got):
        keep, got = sum_yh(keep, got)
        shape = (deep, 2, 2 * part, 3 * lane)
        return kernel(
            last_y_body,
            "last_y",
            [keep.reshape(shape), sum(g.astype(f32) for g in got).reshape(shape) if outer > 1 else got[0].reshape(shape)],
            [((deep, *shape[2:]), f32), ((deep, *shape[2:]), bf16)],
        )

    def sum_zh(keep, send):
        got = send_sums([send[e] for e in range(deep - 1)], "zh")
        return [v.reshape(2, 2, part, 3 * lane) for v in (keep, *got)]

    def pair(keep, got):
        shape = keep.shape[1:]
        return kernel(pair_body, "pair", [keep, got], [(shape, f32), (shape, bf16)])

    def ffn_split(group):
        count = len(group)
        return kernel(
            ffn_split_body,
            "ffn_split",
            [v for each in group for v in each],
            [
                ((count, part, 3 * lane), f32),
                ((count, part, 3 * lane), bf16),
                ((count, 2, part, 3 * lane), bf16),
            ],
            chunks=count,
        )

    far[2], far_two, core_two, *far_y[0] = tick(far[2], far_two, core_two, *far_y[0])
    far_y[2] = over_y(far[2])
    farcore_two = swap(far_two, "k")
    ffn_rows = [low_two, core_two, far_two, farcore_two]
    first_0, hidden_0 = ffn(0)
    grads = [None] * chunks
    grad_got, sums, zh_sums = [None] * chunks, [None] * chunks, [None] * chunks
    firsts, hiddens = [first_0], [hidden_0]
    for j in range(1, chunks):
        if j == chunks - 1:
            grads[0] = ffn_grad(firsts[0], hiddens[0])
            low_two, *flat = tick(low_two, *firsts, *hiddens, *grads[0])
            firsts, hiddens, grads[0] = flat[:j], flat[j : 2 * j], flat[2 * j :]
        elif j == 1:
            low_two, *flat = tick(low_two, *firsts, *hiddens)
            firsts, hiddens = flat[:1], flat[1:]
        ffn_rows[0] = low_two
        first, hidden = ffn(j)
        firsts.append(first)
        hiddens.append(hidden)
    keep, send = back(firsts, slice(0, 2 * lane))

    keep, send, *flat = tick(keep, send, *grads[0], *firsts[1:], *hiddens)
    grads[0], firsts, hiddens = flat[:2], [None, *flat[2:5]], flat[5:]
    core_got = swap(send, "k")
    grad_got[0] = swap(grads[0][1], "yl")
    grads[1] = ffn_grad(firsts[1], hiddens[1])
    core_keep, core_send = pair(keep, core_got)

    core_keep, core_send, *flat = tick(core_keep, core_send, *grads[1], *firsts[2:], *hiddens)
    grads[1], firsts, hiddens = flat[:2], [None, None, *flat[2:4]], flat[4:]
    core_got = swap(core_send, "zl")
    grad_got[1] = swap(grads[1][1], "yl")
    mixed_keep, mixed_send = back(hiddens, slice(2 * lane, 3 * lane))
    mixed_keep, mixed_send, *flat = tick(mixed_keep, mixed_send, *firsts[2:], *hiddens)
    firsts, hiddens = [None, None, *flat[:2]], flat[2:]
    mixed_got = swap(mixed_send, "k")
    grads[2] = ffn_grad(firsts[2], hiddens[2])
    grads[3] = ffn_grad(firsts[3], hiddens[3])
    mixed_keep, mixed_got, *flat = tick(mixed_keep, mixed_got, grads[0][0], *grads[2], *grads[3])
    grad_keep, grads[2], grads[3] = flat[0], flat[1:3], flat[3:]
    mixed_keep, mixed_send = pair(mixed_keep, mixed_got)
    sums[0] = sum_y(grad_keep, grad_got[0])
    core = (core_keep + core_got.astype(f32)).astype(bf16)

    core, mixed_keep, mixed_send, grad_keep, *flat = tick(
        core, mixed_keep, mixed_send, grads[1][0], *sums[0], *grads[2], *grads[3]
    )
    sums[0], grads[2], grads[3] = flat[:2], flat[2:4], flat[4:]
    core_other = swap(core, "x")
    zh_sums[0] = sum_zh(*sums[0])
    mixed_got = swap(mixed_send, "zl")
    sums[1] = sum_y(grad_keep, grad_got[1])
    d_residual, d_low = kernel(
        residual_back_body,
        "residual_back",
        [core, core_other, residual, cotangent[0], gains],
        [((rows, wide), f32), ((rows, wide), bf16)],
        dims=dims,
    )

    d_low, *flat = tick(d_low, *sums[1], *grads[2], *zh_sums[0])
    sums[1], grads[2], zh_sums[0] = flat[:2], flat[2:4], flat[4:]
    d_far = swap(d_low, "yl")
    grad_got[2] = swap(grads[2][1], "yl")
    zh_sums[1] = sum_zh(*sums[1])

    d_far, mixed_keep, mixed_got = tick(d_far, mixed_keep, mixed_got)
    mixed_half = (mixed_keep + mixed_got.astype(f32)).astype(bf16)
    mixed_other = swap(mixed_half, "x")
    d_query, d_keep, d_send, grad_table = kernel(
        attend_back_body,
        "attend_back",
        [qkv, probs, d_low, d_far, w_own, w_other],
        [
            ((2 * rows, inner), bf16),
            ((2 * outer, rows, 2 * inner), f32),
            ((2 * outer, rows, 2 * inner), bf16),
            ((8, lane), f32),
        ],
        [pltpu.VMEM((8, 2 * length), f32), pltpu.VMEM((2 * rows, inner), bf16)],
        sizes=sizes,
        buckets=buckets,
    )

    d_query, d_keep, d_send, grad_table, *zh_sums[1] = tick(
        d_query, d_keep, d_send, grad_table, *zh_sums[1]
    )
    d_got = swap(d_send, "k")
    if outer > 1:
        total = (d_keep + d_got.astype(f32)).reshape(outer, 2, rows, 2 * inner)
        arrived = send_sums([total[e].astype(bf16) for e in range(1, outer)], "yh")
        d_keep, d_got = total[0], sum(a.astype(f32) for a in arrived)
    g_keep, g_send, keep, send = kernel(
        attn_grad_body,
        "attn_grad",
        [attn_input, d_query, d_keep, d_got, d_low, d_far, attended, w_own, w_other, grad_table],
        [
            ((rows, wide), f32),
            ((rows, wide), bf16),
            ((half + tail // 2, 4 * inner), f32),
            ((half + tail, 4 * inner), bf16),
        ],
        [pltpu.VMEM((2 * rows, 3 * inner), bf16)],
        sizes=sizes,
    )

    g_keep, g_send, keep, send, grad_got[2], *grads[3] = tick(
        g_keep, g_send, keep, send, grad_got[2], *grads[3]
    )
    got = [swap(send, "k")]
    grad_got[3] = swap(grads[3][1], "yl")
    keep, grad_keep = tick(keep, grads[2][0])
    if outer > 1:
        keep, send = split(here, at_yh, outer, keep, got, tail)
        got = send_sums([send[e] for e in range(outer - 1)], "yh")
    sums[2] = sum_y(grad_keep, grad_got[2])
    keep, send = split(here, at_zl, 2, keep, got, tail)

    keep, send, g_keep, g_send, residual, grad_keep, *sums[2] = tick(
        keep, send, g_keep, g_send, residual, grads[3][0], *sums[2]
    )
    got = send_sums([send[0]], "zl")
    zh_sums[2] = sum_zh(*sums[2])
    g_got = swap(g_send, "yl")
    last_keep, last_send = sum_y_last(grad_keep, grad_got[3])
    last_got = swap(last_send, "zl")
    residual, *zh_sums[2] = tick(residual, *zh_sums[2])
    (mixed,) = kernel(
        mixed_body, "mixed", [mixed_half, mixed_other, residual], [((rows, wide), bf16)], dims=dims
    )
    keep, send = split(here, at_zh, deep, keep, got, tail)

    keep, send, mixed, last_keep, *zh_sums[2] = tick(keep, send, mixed, last_keep, *zh_sums[2])
    got = send_sums([send[e] for e in range(deep - 1)], "zh")
    (last_send,) = kernel(
        last_z_body,
        "last_z",
        [last_keep, last_got],
        [((max(deep - 1, 1), 2, 2 * part, 3 * lane), bf16)],
    )
    last_sums = send_sums([last_send[e] for e in range(deep - 1)], "zh")
    done = ffn_split(zh_sums[:-1])
    other = swap(done[2], "zl")
    group_a = [done[0], other, swap(done[1], "k")]
    keep, send = split(here, at_yl, 2, keep, got, tail)

    keep, send, g_keep, g_got, last_keep = tick(keep, send, g_keep, g_got, last_keep)
    got = swap(send[0], "yl")
    group_a.append(swap(other, "k"))
    g_sum = (g_keep + g_got.astype(f32)).astype(bf16)
    g_other = swap(g_sum, "x")
    grad_query, grad_key, grad_value, grad_out, gain_row, grad_table = kernel(
        attn_final_body,
        "attn_final",
        [keep, got, w_query, w_key, w_value, norm_one[None]],
        [((part, 2 * inner), f32)] * 4 + [((1, part), f32), ((heads_dev, lane), f32)],
        heads=heads,
    )
    gain_row, last_keep = tick(gain_row, last_keep)
    done = kernel(
        last_body,
        "last",
        [last_keep, last_got, *last_sums],
        [
            ((1, part, 3 * lane), f32),
            ((1, part, 3 * lane), bf16),
            ((1, 2, part, 3 * lane), bf16),
        ],
    )
    group_b = [done[0], done[2], swap(done[1], "k"), swap(done[2], "k")]
    grad_gate, grad_up, grad_down, grad_gains = kernel(
        ffn_final_body,
        "ffn_final",
        [*group_a, *group_b, w_gate, w_up, norm_two[None], gain_row],
        [((part, hidden_dev), f32)] * 3 + [((2, part), f32)],
        [pltpu.VMEM((3, part, 4 * chunks * lane), f32)],
        groups=2,
    )
    grad_gains, d_residual = tick(grad_gains, d_residual)
    gains_got = swap(grad_gains, "x")
    (input_grad,) = kernel(
        input_grad_body,
        "input_grad",
        [g_sum, g_other, tokens[0], gains, d_residual],
        [((rows, wide), bf16)],
        dims=dims,
    )
    grad_gains = grad_gains + gains_got
    return (
        mixed[None],
        input_grad[None],
        grad_gains[0],
        grad_query,
        grad_key,
        grad_value,
        grad_out.T,
        grad_table[:, :buckets],
        grad_gains[1],
        grad_gate,
        grad_up,
        grad_down.T,
    )


def solution(mesh):
    depths, lines, halves = (mesh.shape[a] for a in ("fsdp", "ctx", "tp"))
    fine = Mesh(
        mesh.devices.reshape(depths // 2, 2, lines // 4, 2, 2, halves),
        ("zh", "zl", "yh", "yl", "k", "x"),
    )
    depth, line = ("zh", "zl"), ("yh", "yl", "k")
    every = (*depth, *line)
    in_specs = (
        P(depth, line, None),
        P(depth, line, None),
        P(depth),
        P(every),
        P(every, "x"),
        P(every, "x"),
        P(every, "x"),
        P("x", every),
        P("x", None),
        P(every),
        P(every, "x"),
        P(every, "x"),
        P("x", every),
    )
    out_specs = (
        P(depth, line, None),
        P(depth, line, None),
        P(every),
        P(every, "x"),
        P(every, "x"),
        P(every, "x"),
        P("x", every),
        P("x", None),
        P(every),
        P(every, "x"),
        P(every, "x"),
        P("x", every),
    )
    return jax.shard_map(local, mesh=fine, in_specs=in_specs, out_specs=out_specs, check_vma=False)
```

```python
import functools

import jax
import jax.numpy as jnp
import numpy as np
from jax import lax
from jax.experimental import pallas as pl
from jax.experimental.pallas import tpu as pltpu
from jax.sharding import Mesh, PartitionSpec as P

epsilon = 1e-06
masked_value = -1e30
far_bounds = (12, 16, 23, 32, 46, 64, 91)
f32 = jnp.float32
bf16 = jnp.bfloat16
lane = 128
ffn_order = (2, 3, 0, 1, 4, 5)
attn_order = (4, 2, 1, 0, 3, 5)
at_k, at_yl, at_zl, at_zh, at_yh, at_prefix, at_lists = range(7)


def bucket_of(relative, buckets):
    offset = jnp.abs(relative)
    far = jnp.full(offset.shape, buckets // 4, jnp.int32)
    for threshold in far_bounds:
        far = far + (offset >= threshold).astype(jnp.int32)
    return jnp.where(offset < buckets // 4, offset, far) + buckets // 2 * (relative > 0).astype(
        jnp.int32
    )


def dot(left, right, dims=((1,), (0,))):
    return lax.dot_general(left, right, (dims, ((), ())), preferred_element_type=f32)


def dot_nt(left, right):
    return dot(left, right, ((1,), (1,)))


def dot_tn(left, right):
    return dot(left, right, ((0,), (0,)))


def fetch(value, axis, step):
    size = lax.axis_size(axis)
    return lax.ppermute(value, axis, [((i + step) % size, i) for i in range(size)])


def swap(value, axis):
    return fetch(value, axis, 1)


def gather(value, axis):
    return [value] + [fetch(value, axis, e) for e in range(1, lax.axis_size(axis))]


def send_sums(sends, axis):
    size = lax.axis_size(axis)
    return [fetch(sends[e - 1], axis, size - e) for e in range(1, size)]


class Clock:
    def __init__(self, token):
        self.token = token

    def tick(self, *values):
        self.token, *values = lax.optimization_barrier((self.token, *values))
        return values


costs = {"attn_final": 200, "last_z": 40, "place": 200}


def runs_of(dims, order, inverse):
    index = np.arange(int(np.prod(dims))).reshape(dims).transpose(order).reshape(-1)
    if inverse:
        index = np.argsort(index)
    cuts = [0, *(np.flatnonzero(np.diff(index) != 1) + 1).tolist(), len(index)]
    return [(int(index[a]), int(index[a]) + b - a) for a, b in zip(cuts[:-1], cuts[1:])]


def reorder(value, dims, order, inverse=False):
    return jnp.concatenate([value[:, a:b] for a, b in runs_of(dims, order, inverse)], axis=1)


def inv_scale(values):
    return lax.rsqrt(jnp.mean(values * values, axis=-1, keepdims=True) + epsilon)


def norm_back(scale, normed, grad_normed):
    return scale * (grad_normed - normed * jnp.mean(grad_normed * normed, axis=-1, keepdims=True))


def aligned(index, size):
    return pl.ds(pl.multiple_of(index * size, size), size)


def call(body, name, here, arrays, outs, scratch=(), raw=0, **static):
    cost = costs.get(name, 100)
    space = pl.BlockSpec(memory_space=pltpu.VMEM)
    spaces = [pl.BlockSpec(memory_space=pltpu.HBM)] * raw + [space] * (len(arrays) - raw)
    need = sum(int(np.prod(s.shape)) * jnp.dtype(s.dtype).itemsize for s in scratch[: len(scratch) - bool(raw)])
    need += (6 << 20) if static.get("dims", (lane,))[-1] >= 32 else (40 << 20)
    return pl.pallas_call(
        functools.partial(body, **static),
        out_shape=tuple(jax.ShapeDtypeStruct(shape, kind) for shape, kind in outs),
        in_specs=[pl.BlockSpec(memory_space=pltpu.SMEM)] + spaces,
        out_specs=tuple(space for _ in outs),
        scratch_shapes=scratch,
        compiler_params=pltpu.CompilerParams(vmem_limit_bytes=(56 << 20) if raw else need),
        cost_estimate=pl.CostEstimate(
            flops=20_000_000 * cost, bytes_accessed=80_000 * cost, transcendentals=0
        ),
        name=name,
    )(here, *arrays)


def place_body(here, own, got, out, *, which):
    at = here[which]
    out[at] = own[...]
    out[1 - at] = got[...]


def pack_attn_body(here, wq, wk, wv, wo, one, two, own, send, mats, gains, sems):
    part, wide = mats.shape[1:]
    half = wide // 2
    copies = [
        pltpu.make_async_copy(ref, room, sems.at[i])
        for i, (ref, room) in enumerate(
            [*((ref, mats.at[i]) for i, ref in enumerate((wq, wk, wv, wo))), (one, gains.at[0]), (two, gains.at[1])]
        )
    ]
    for copy in copies:
        copy.start()
    for copy in copies:
        copy.wait()
    low = jnp.concatenate([mats[i, :, :half] for i in range(4)], axis=1)
    high = jnp.concatenate([mats[i, :, half:] for i in range(4)], axis=1)
    row = lax.broadcasted_iota(jnp.int32, (8, part), 0)
    first, second = (jnp.broadcast_to(gains[i].astype(f32), (8, part)) for i in range(2))
    head = jnp.where(row == 0, first, jnp.where(row == 1, second, 0.0)).astype(bf16)

    def write(out, mat):
        out[:8] = jnp.zeros((8, out.shape[1]), bf16)
        out[:8, :part] = head
        out[8:] = mat

    @pl.when(here[at_yl] == 0)
    def _():
        write(own, low)
        write(send, high)

    @pl.when(here[at_yl] != 0)
    def _():
        write(own, high)
        write(send, low)


def pack_ffn_body(here, wg, wu, wd, own, send, room, *, chunks):
    hidden = wg.shape[1]
    whole = hidden // lane * lane
    room[:, :, whole:] = jnp.zeros((3, wg.shape[0], 4 * chunks * lane - whole), bf16)
    room[0, :, :hidden] = wg[...]
    room[1, :, :hidden] = wu[...]
    room[2, :, :hidden] = wd[...]
    for out, core in ((own, here[at_k]), (send, 1 - here[at_k])):
        for h in range(2):
            for j in range(chunks):
                for m in range(3):
                    out[h, j, :, m * lane : (m + 1) * lane] = room[
                        m, :, aligned((2 * h + core) * chunks + j, lane)
                    ]


def place_ffn_body(here, own, got, near, first, rest, *, chunks):
    k, zl = here[at_k], here[at_zl]
    for j in range(chunks):
        near[j, k] = own[zl, j]
        near[j, 1 - k] = got[zl, j]
        out, at = (rest, j - 1) if j else (first, 0)
        out[at, k] = own[1 - zl, j]
        out[at, 1 - k] = got[1 - zl, j]


def place_first_body(here, near, got, out):
    zl = here[at_zl]
    out[zl] = near[0]
    out[1 - zl] = got[0]


def place_rest_body(here, near, rest, whole, *outs):
    zl = here[at_zl]
    j = 0
    for group in outs:
        for at in range(group.shape[0]):
            for out in (whole.at[j], group.at[at]):
                out[zl] = near[j + 1]
                out[1 - zl] = rest[j]
            j += 1


def buckets_row(span, buckets):
    return bucket_of(lax.broadcasted_iota(jnp.int32, (1, 2 * span), 1) - span, buckets)


def rows_body(here, table, *refs, dims, heads):
    *blocks, out, grads_out, lines = refs
    grads, blocks = blocks[:4], blocks[4:]
    rows = grads[0].shape[0]
    for at, block in enumerate(blocks):
        values = block[...].astype(f32)
        out[at * rows : (at + 1) * rows] = reorder(values * inv_scale(values), dims, attn_order)
    for at, block in enumerate(grads):
        low = reorder(block[...].astype(f32), dims, ffn_order)
        grads_out[at * rows : (at + 1) * rows] = low.astype(bf16)
    buckets = table.shape[1]
    values = table[...].astype(f32)
    mine = jnp.where(here[at_yl] == 0, values[:heads], values[heads:])
    row = buckets_row(lines.shape[1] // 2, buckets)
    line = jnp.zeros((heads, lines.shape[1]), f32)
    for b in range(buckets):
        line = line + jnp.where(row == b, mine[:, b : b + 1], 0.0)
    lines[...] = jnp.zeros_like(lines)
    lines[:heads] = line


def bias_block(line_ref, head, start, rows):
    line = line_ref[pl.ds(head, 1), pl.ds(pl.multiple_of(start, rows), 2 * rows)]
    spread = jnp.broadcast_to(line, (rows, 2 * rows))
    return pltpu.roll(spread, 0, 1, stride=1, stride_axis=0)[:, rows:]


def attend_body(
    here, normed, pack_own, pack_other, lines,
    qkv, probs_out, attended, keep, send, inputs, w_own, w_other, gains, *, sizes, dims
):
    rows, heads, width, query_blocks, key_blocks, span = sizes
    prefix = here[at_prefix]
    inner = heads * width
    half = w_own.shape[0]
    part = dims[-1]
    gain_parts = []
    for pack, weights in ((pack_own, w_own), (pack_other, w_other)):
        for at in range(half // part):
            weights[at * part : (at + 1) * part] = pack[at, 8:]
        gain_parts.append(
            [
                jnp.concatenate([pack[at, i : i + 1, :part].astype(f32) for at in range(half // part)], axis=1)
                for i in range(2)
            ]
        )
    for i in range(2):
        low, high = gain_parts[0][i], gain_parts[1][i]
        gain = jnp.where(
            here[at_k] == 0,
            jnp.concatenate([low, high], axis=1),
            jnp.concatenate([high, low], axis=1),
        )
        if i == 0:
            inputs[...] = (normed[...] * gain).astype(bf16)
        gains[i : i + 1] = reorder(gain, dims, attn_order, True)
    places = [here[at_lists + i] for i in range(key_blocks)]
    mine, other = aligned(here[at_k], half), aligned(1 - here[at_k], half)
    qkv[...] = (
        dot(inputs[:, mine], w_own[:, : 3 * inner]) + dot(inputs[:, other], w_other[:, : 3 * inner])
    ).astype(bf16)
    for head in range(heads):
        lanes = slice(head * width, (head + 1) * width)
        keys = qkv[:, inner + head * width : inner + (head + 1) * width]
        values = qkv[:, 2 * inner + head * width : 2 * inner + (head + 1) * width]
        for at, block in enumerate(query_blocks):
            query_block = places[block]
            queries = qkv[block * rows : (block + 1) * rows, lanes]
            raw = dot_nt(queries, keys)
            query_pos = query_block * rows + lax.broadcasted_iota(jnp.int32, (rows, rows), 0)
            parts = []
            for key_at, key_block in enumerate(places):
                start = (key_block - query_block) * rows + span - rows
                key_pos = key_block * rows + lax.broadcasted_iota(jnp.int32, (rows, rows), 1)
                allowed = (key_pos <= query_pos) | (key_pos < prefix)
                biased = raw[:, key_at * rows : (key_at + 1) * rows] + bias_block(
                    lines, head, start, rows
                )
                parts.append(jnp.where(allowed, biased, masked_value))
            scores = jnp.concatenate(parts, axis=1)
            top = jnp.max(scores, axis=1, keepdims=True)
            powers = jnp.exp(scores - top)
            probs = powers / jnp.sum(powers, axis=1, keepdims=True)
            probs_out[head, at * rows : (at + 1) * rows, :] = probs
            attended[at * rows : (at + 1) * rows, lanes] = dot(probs.astype(bf16), values).astype(
                bf16
            )
    for lanes, weights in ((mine, w_own), (other, w_other)):
        out = dot_nt(attended[...], weights[:, 3 * inner :])
        keep[:, lanes] = out[:rows]
        send[:, lanes] = out[rows:].astype(bf16)


def norm_body(here, own, got, tokens, gains, residual, low, *, dims):
    total = own[...].astype(f32) + got[...].astype(f32)
    values = tokens[...].astype(f32) + reorder(total, dims, attn_order, True)
    residual[...] = values
    low[...] = reorder(values * inv_scale(values) * gains[1:2], dims, ffn_order).astype(bf16)


def tall(refs, lanes):
    return jnp.concatenate([ref[:, lanes] for ref in refs], axis=0)


def ffn_body(here, *refs, where, picks):
    rows, grads, weights, (first_out, hidden_out) = refs[:4], refs[4], refs[5:-2], refs[-2:]
    weights = [w if at is None else w.at[at] for at, w in zip(picks, weights)]
    size = weights[0].shape[0]
    first, d_hidden = None, None
    for at, w in enumerate(weights):
        lanes = aligned(here[where + at], size)
        first_part = dot(tall(rows, lanes), w[:, : 2 * lane])
        d_part = dot(grads[:, lanes], w[:, 2 * lane :])
        first = first_part if first is None else first + first_part
        d_hidden = d_part if d_hidden is None else d_hidden + d_part
    gate, up = first[:, :lane], first[:, lane:]
    root = float(np.sqrt(2.0 / np.pi))
    square = gate * gate
    bend = jnp.tanh(root * gate * (1.0 + 0.044715 * square))
    half = 0.5 * (1.0 + bend)
    active = gate * half
    slope = half + 0.5 * gate * (1.0 - bend * bend) * (root * (1.0 + 3.0 * 0.044715 * square))
    hidden_out[...] = (active * up).astype(bf16)
    first_out[:, :lane] = (d_hidden * up * slope).astype(bf16)
    first_out[:, lane:] = (d_hidden * active).astype(bf16)


def back_body(here, *refs, where, chunks, picks, lanes):
    lefts, weights, (keep, send) = refs[:chunks], refs[chunks:-2], refs[-2:]
    weights = [w if at is None else w.at[at] for at, w in zip(picks, weights)]
    blocks = len(weights) // chunks
    rows = keep.shape[1]
    for at in range(blocks):
        total = None
        for j in range(chunks):
            w = weights[j * blocks + at]
            part = dot_nt(lefts[j][...], w[:, lanes])
            total = part if total is None else total + part
        here_lanes = aligned(here[where + at], w.shape[0])
        for a in range(2):
            keep[a, :, here_lanes] = total[2 * a * rows : (2 * a + 1) * rows]
            send[a, :, here_lanes] = total[(2 * a + 1) * rows : (2 * a + 2) * rows].astype(bf16)


def ffn_grad_body(here, *refs, outer):
    rows, grads, (first, hidden, keep, send) = refs[:4], refs[4], refs[5:]
    size = keep.shape[1]
    for e in range(outer):
        yh = here[at_yh] + e
        yh = jnp.where(yh >= outer, yh - outer, yh) * 2
        for out, y in ((keep, yh + here[at_yl]), (send, yh + 1 - here[at_yl])):
            lanes = aligned(y, size)
            out[e, :, : 2 * lane] = dot_tn(tall(rows, lanes), first[...]).astype(out.dtype)
            out[e, :, 2 * lane :] = dot_tn(grads[:, lanes], hidden[...]).astype(out.dtype)


def table_parts(values):
    high = values.astype(bf16)
    return jnp.concatenate([high, (values - high.astype(f32)).astype(bf16)], axis=0)


def table_value(parts):
    half = parts.shape[0] // 2
    return parts[:half].astype(f32) + parts[half:].astype(f32)


def split_body(here, own, *refs, which, count, tail):
    *got, keep, send = refs
    size = keep.shape[0] - tail

    def piece(ref, at):
        if size % 8 == 0:
            return ref[aligned(at, size)]
        value = ref[:size]
        for i in range(1, count):
            value = jnp.where(at == i, ref[i * size : (i + 1) * size], value)
        return value

    for e in range(count):
        at = here[which] + e
        at = jnp.where(at >= count, at - count, at)
        total = piece(own, at)
        for ref in got:
            total = total + piece(ref, at).astype(f32)
        if e:
            send[e - 1, :size] = total.astype(bf16)
        else:
            keep[:size] = total
    if tail:
        total = own[count * size :]
        for ref in got:
            total = total + table_value(ref[count * size :])
        parts = table_parts(total)
        keep[size:] = table_value(parts)
        for e in range(count - 1):
            send[e, size:] = parts


def split(here, which, count, own, got, tail=0):
    size = (own.shape[0] - tail // 2) // count
    return call(
        split_body,
        "split",
        here,
        [own, *got],
        [((size + tail // 2, own.shape[1]), f32), ((max(count - 1, 1), size + tail, own.shape[1]), bf16)],
        which=which,
        count=count,
        tail=tail // 2,
    )


def ffn_split_body(here, *refs, chunks):
    done, core, other = refs[-3:]
    each = (len(refs) - 3) // chunks
    zl, k = here[at_zl], here[at_k]
    for j in range(chunks):
        own, *got = refs[j * each : (j + 1) * each]

        def total(depth, slice_):
            value = own[depth, slice_]
            for ref in got:
                value = value + ref[depth, slice_].astype(f32)
            return value

        done[j] = total(zl, k)
        core[j] = total(zl, 1 - k).astype(bf16)
        other[j, 0] = total(1 - zl, 0).astype(bf16)
        other[j, 1] = total(1 - zl, 1).astype(bf16)


def last_y_body(here, own, got, keep, send):
    zl = here[at_zl]
    for h in range(keep.shape[0]):
        keep[h] = own[h, zl] + got[h, zl].astype(f32)
        send[h] = (own[h, 1 - zl] + got[h, 1 - zl].astype(f32)).astype(bf16)


def ahead(here, which, count, e):
    at = here[which] + e
    return jnp.where(at >= count, at - count, at)


def last_z_body(here, own, got, send):
    count = own.shape[0]
    for e in range(1, count):
        at = ahead(here, at_zh, count, e)
        send[e - 1, 0] = own[at].astype(bf16)
        send[e - 1, 1] = got[at]


def last_body(here, own, got, *refs):
    *arrived, done, core, other = refs
    part = done.shape[1]
    zh, k = here[at_zh], here[at_k]
    mine, theirs = own[zh], got[zh].astype(f32)
    for ref in arrived:
        mine = mine + ref[0].astype(f32)
        theirs = theirs + ref[1].astype(f32)
    low, high = mine[:part], mine[part:]
    done[0] = jnp.where(k == 0, low, high)
    core[0] = jnp.where(k == 0, high, low).astype(bf16)
    other[0, 0] = theirs[:part].astype(bf16)
    other[0, 1] = theirs[part:].astype(bf16)


def sum_row(values):
    sums = jnp.sum(values, axis=1, keepdims=True)
    return jnp.broadcast_to(sums, (values.shape[0], lane)).T[0:1]


def ffn_final_body(here, *refs, groups):
    parts, rest = refs[: 4 * groups], refs[4 * groups :]
    wg, wu, gain, first_row, grad_g, grad_u, grad_d, grad_gain, room = rest
    hidden = wg.shape[1]
    chunks = room.shape[2] // (4 * lane)
    zl, k = here[at_zl], here[at_k]
    j = 0
    for group in range(groups):
        done, other, core, far = parts[4 * group : 4 * group + 4]
        for at in range(done.shape[0]):
            for h, c, value in (
                (zl, k, done[at]),
                (1 - zl, k, other[at, k].astype(f32)),
                (zl, 1 - k, core[at].astype(f32)),
                (1 - zl, 1 - k, far[at, k].astype(f32)),
            ):
                for m in range(3):
                    room[m, :, aligned((2 * h + c) * chunks + j, lane)] = value[
                        :, m * lane : (m + 1) * lane
                    ]
            j += 1
    gate, up = room[0, :, :hidden], room[1, :, :hidden]
    grad_g[...] = gate
    grad_u[...] = up
    grad_d[...] = room[2, :, :hidden]
    sums = gate * wg[...].astype(f32) + up * wu[...].astype(f32)
    grad_gain[0:1] = first_row[...]
    grad_gain[1:2] = sum_row(sums) / gain[...].astype(f32)


def pair_body(here, own, got, keep, send):
    keep[...] = own[0] + got[0].astype(f32)
    send[...] = (own[1] + got[1].astype(f32)).astype(bf16)


def residual_back_body(here, own, got, residual, cotangent, gains, d_residual, d_low, *, dims):
    total = own[...].astype(f32) + got[...].astype(f32)
    grad_normed = reorder(total, dims, ffn_order, True) * gains[1:2]
    values = residual[...]
    scale = inv_scale(values)
    back = cotangent[...].astype(f32) + norm_back(scale, values * scale, grad_normed)
    d_residual[...] = back
    d_low[...] = reorder(back, dims, attn_order).astype(bf16)


def attend_back_body(
    here, qkv, probs_in, d_own, d_far, w_own, w_other,
    d_query, d_keep, d_send, table, lines, d_att, *, sizes, buckets
):
    rows, heads, width, query_blocks, key_blocks, span = sizes
    inner = heads * width
    half = w_own.shape[0]
    places = [here[at_lists + i] for i in range(key_blocks)]
    mine, other = aligned(here[at_k], half), aligned(1 - here[at_k], half)
    d_rows = (d_own, d_far)
    d_att[...] = (
        dot(tall(d_rows, mine), w_own[:, 3 * inner :])
        + dot(tall(d_rows, other), w_other[:, 3 * inner :])
    ).astype(bf16)
    lines[...] = jnp.zeros_like(lines)
    up, down = (lax.broadcasted_iota(jnp.int32, (rows, rows), axis) for axis in (0, 1))
    flip = (up + down == rows - 1).astype(bf16)
    for head in range(heads):
        lanes = slice(head * width, (head + 1) * width)
        value_lanes = slice(inner + head * width, inner + (head + 1) * width)
        keys = qkv[:, inner + head * width : inner + (head + 1) * width]
        values = qkv[:, 2 * inner + head * width : 2 * inner + (head + 1) * width]
        d_key, d_value = None, None
        for at, block in enumerate(query_blocks):
            queries = qkv[block * rows : (block + 1) * rows, lanes]
            d_attended = d_att[at * rows : (at + 1) * rows, lanes]
            probs = probs_in[head, at * rows : (at + 1) * rows, :]
            d_probs = dot_nt(d_attended, values)
            delta = jnp.sum(probs * d_probs, axis=1, keepdims=True)
            d_scores = (probs * (d_probs - delta)).astype(bf16)
            d_query[at * rows : (at + 1) * rows, lanes] = dot(d_scores, keys).astype(bf16)
            key_part = dot_tn(d_scores, queries)
            value_part = dot_tn(probs.astype(bf16), d_attended)
            d_key = key_part if d_key is None else d_key + key_part
            d_value = value_part if d_value is None else d_value + value_part
            upward = dot(flip, d_scores)
            for key_at, key_block in enumerate(places):
                start = (key_block - places[block]) * rows + span - rows
                piece = upward[:, key_at * rows : (key_at + 1) * rows]
                padded = jnp.concatenate([piece, jnp.zeros_like(piece)], axis=1)
                turned = pltpu.roll(padded, 1, 1, stride=1, stride_axis=0)
                span_at = pl.ds(pl.multiple_of(start, rows), 2 * rows)
                lines[pl.ds(head, 1), span_at] += jnp.sum(turned, axis=0, keepdims=True)
        for key_at in range(key_blocks):
            from_, to = slice(key_at * rows, (key_at + 1) * rows), key_at // 2
            for out, parity in ((d_keep, 0), (d_send, 1)):
                if key_at % 2 == parity:
                    out[to, :, lanes] = d_key[from_].astype(out.dtype)
                    out[to, :, value_lanes] = d_value[from_].astype(out.dtype)
    row = buckets_row(span, buckets)
    column = lax.broadcasted_iota(jnp.int32, table.shape, 1)
    total = jnp.zeros(table.shape, f32)
    for b in range(buckets):
        one = jnp.sum(jnp.where(row == b, lines[...], 0.0), axis=1, keepdims=True)
        total = jnp.where(column == b, one, total)
    table[...] = total


def attn_grad_body(
    here, inputs, d_query, d_keep, d_got, d_own, d_far, attended, w_own, w_other, table,
    g_keep, g_send, keep, send, d_qkv, *, sizes
):
    rows, heads, width, query_blocks, key_blocks, span = sizes
    inner = heads * width
    half = w_own.shape[0]
    mine, other = aligned(here[at_k], half), aligned(1 - here[at_k], half)
    d_qkv[:, :inner] = d_query[...]
    for at in range(2):
        d_qkv[at * rows : (at + 1) * rows, inner:] = (d_keep[at] + d_got[at].astype(f32)).astype(bf16)
    for lanes, weights, out in ((mine, w_own, keep), (other, w_other, send)):
        part = dot_nt(d_qkv[...], weights[:, : 3 * inner])
        g_keep[:, lanes] = part[:rows]
        g_send[:, lanes] = part[rows:].astype(bf16)
        two = jnp.concatenate([inputs[b * rows : (b + 1) * rows, lanes] for b in query_blocks], axis=0)
        out[:half, : 3 * inner] = dot_tn(two, d_qkv[...]).astype(out.dtype)
        out[:half, 3 * inner :] = dot_tn(tall((d_own, d_far), lanes), attended[...]).astype(out.dtype)
    parts = table_parts(table[...])
    keep[half:] = jnp.zeros((keep.shape[0] - half, keep.shape[1]), f32)
    send[half:] = jnp.zeros((send.shape[0] - half, send.shape[1]), bf16)
    keep[half:, :lane] = table_value(parts)
    send[half:, :lane] = parts


def input_grad_body(here, own, got, tokens, gains, d_residual, out, *, dims):
    total = own[...].astype(f32) + got[...].astype(f32)
    grad_normed = reorder(total, dims, attn_order, True) * gains[0:1]
    values = tokens[...].astype(f32)
    scale = inv_scale(values)
    out[...] = (d_residual[...] + norm_back(scale, values * scale, grad_normed)).astype(bf16)


def mixed_body(here, own, got, residual, out, *, dims):
    total = own[...].astype(f32) + got[...].astype(f32)
    out[...] = (residual[...] + reorder(total, dims, ffn_order, True)).astype(bf16)


def attn_final_body(here, own, got, wq, wk, wv, gain, gq, gk, gv, go, grad_gain, table, *, heads):
    part, inner = gq.shape[0], own.shape[1] // 4

    def finish(low, high, low_table, high_table):
        grads = [
            jnp.concatenate([m[:, i * inner : (i + 1) * inner] for m in (low, high)], axis=1)
            for i in range(4)
        ]
        sums = 0.0
        for out, weights, grad in ((gq, wq, grads[0]), (gk, wk, grads[1]), (gv, wv, grads[2])):
            out[...] = grad
            sums = sums + grad * weights[...].astype(f32)
        go[...] = grads[3]
        grad_gain[...] = sum_row(sums) / gain[...].astype(f32)
        table[...] = jnp.concatenate([low_table[:heads], high_table[:heads]], axis=0)

    values = own[:part], got[:part].astype(f32)
    tables = own[part:, :lane], table_value(got[part:, :lane])

    @pl.when(here[at_yl] == 0)
    def _():
        finish(*values, *tables)

    @pl.when(here[at_yl] != 0)
    def _():
        finish(*values[::-1], *tables[::-1])


def local(
    tokens,
    cotangent,
    prefix,
    norm_one,
    w_query,
    w_key,
    w_value,
    w_out,
    position_bias_matrix,
    norm_two,
    w_gate,
    w_up,
    w_down,
):
    outer, deep = lax.axis_size("yh"), lax.axis_size("zh")
    rows, wide = tokens.shape[1:]
    part = w_query.shape[0]
    heads_dev, buckets = position_bias_matrix.shape
    heads = heads_dev // 2
    width = w_query.shape[1] // heads_dev
    inner = heads * width
    hidden_dev = w_gate.shape[1]
    chunks = -(-hidden_dev // (4 * lane))
    length = rows * outer * 4
    dims = (deep, 2, outer, 2, 2, part)
    half = wide // 2
    key_blocks = 4 * outer
    sizes = (rows, heads, width, (0, 2), key_blocks, length)

    tail = 16
    split_deep = deep == 2 and (4 * part) % lane == 0
    deep_blocks = deep if split_deep else 1
    yh, yl, k, zl, zh = (lax.axis_index(a) for a in ("yh", "yl", "k", "zl", "zh"))
    relative = [(e, a) for a in range(2) for e in range(outer)]
    ys = [((yh + e) % outer) * 2 + (yl + a) % 2 for e, a in relative]
    where = at_lists + key_blocks
    here = [k, yl, zl, zh, yh, prefix[0]]
    here += [
        ((yh + e) % outer) * 4 + ((yl + a) % 2) * 2 + (k + b) % 2
        for e in range(outer)
        for a in range(2)
        for b in range(2)
    ]
    here += [y * deep_blocks + (zh + d) % deep_blocks for d in range(deep_blocks) for y in ys]
    here = jnp.stack([jnp.asarray(v, jnp.int32) for v in here])
    tick = Clock(here).tick
    which = {"k": at_k, "yl": at_yl, "zl": at_zl, "zh": at_zh, "yh": at_yh}

    def kernel(body, name, arrays, outs, scratch=(), **static):
        return call(body, name, here, arrays, outs, scratch, **static)

    def place(pieces, axis):
        size, shape = len(pieces), pieces[0].shape
        if size == 1:
            return pieces[0][None]
        if size == 2:
            outs = [((2, *shape), pieces[0].dtype)]
            return kernel(place_body, "place", pieces, outs, which=which[axis])[0]
        stack = jnp.zeros((size, *shape), pieces[0].dtype)
        for e, piece in enumerate(pieces):
            at = (lax.axis_index(axis) + e) % size
            stack = lax.dynamic_update_slice_in_dim(stack, piece[None], at, 0)
        return stack

    def both(value, axis):
        return place(gather(value, axis), axis)

    tall_part = 8 + part
    own, send = kernel(
        pack_attn_body,
        "pack_attn",
        [w_query, w_key, w_value, w_out.T, norm_one[None], norm_two[None]],
        [((tall_part, 4 * inner), bf16)] * 2,
        [
            pltpu.VMEM((4, part, 2 * inner), bf16),
            pltpu.VMEM((2, 1, part), bf16),
            pltpu.SemaphoreType.DMA((6,)),
        ],
        raw=6,
    )
    own, send, own_grad, *ffn_in = tick(own, send, cotangent[0], w_gate, w_up, w_down.T)
    pack_got = swap(send, "yl")
    far_grad = swap(own_grad, "zl")
    ffn_own, ffn_send = kernel(
        pack_ffn_body,
        "pack_ffn",
        ffn_in,
        [((2, chunks, part, 3 * lane), bf16)] * 2,
        [pltpu.VMEM((3, part, 4 * chunks * lane), bf16)],
        chunks=chunks,
    )
    pack = place([own, pack_got], "yl")

    pack, ffn_own, ffn_send, own_tokens = tick(pack, ffn_own, ffn_send, tokens[0])
    pack_all = gather(pack, "zh")
    far_tokens = swap(own_tokens, "yl")
    near, near_first, near_rest = kernel(
        place_ffn_body,
        "place_ffn",
        [ffn_own, swap(ffn_send, "k")],
        [((n, 2, part, 3 * lane), bf16) for n in (chunks, 1, chunks - 1)],
        chunks=chunks,
    )
    pack = place(pack_all, "zh")

    pack, near, near_first, near_rest, far_tokens, own_tokens, far_grad, own_grad = tick(
        pack, near, near_first, near_rest, far_tokens, own_tokens, far_grad, own_grad
    )
    pack_all = gather(pack, "zl")
    first_got = swap(near_first, "zl")
    row_blocks = [p for pair in zip(gather(own_tokens, "yh"), gather(far_tokens, "yh")) for p in pair]
    row_blocks = [p for b in row_blocks for p in gather(b, "k")]
    grad_blocks = [p for b in (own_grad, far_grad) for p in gather(b, "k")]
    normed, grad_rows, lines = kernel(
        rows_body,
        "rows",
        [position_bias_matrix, *grad_blocks, *row_blocks],
        [((length, wide), f32), ((4 * rows, wide), bf16), ((8, 2 * length), f32)],
        dims=dims,
        heads=heads,
    )
    pack = place(pack_all, "zl")
    (near_zero,) = kernel(
        place_first_body, "place_first", [near, first_got], [((2, 2, part, 3 * lane), bf16)]
    )

    pack, near, near_zero, first_got, near_rest, normed, grad_rows, lines = tick(
        pack, near, near_zero, first_got, near_rest, normed, grad_rows, lines
    )
    pack = both(pack, "yh").reshape(half // part, tall_part, 4 * inner)
    pack_own, pack_other = gather(pack, "k")
    rest_got = swap(near_rest, "zl")

    groups = [[0], list(range(1, chunks - 1)), [chunks - 1]]

    def over_zh(value):
        pieces = gather(value, "zh")
        if split_deep:
            return pieces[1]
        return place(pieces, "zh").swapaxes(0, 1)

    def over_y(value):
        value = value.reshape(value.shape[0], -1, 3 * lane)
        return [p for b in gather(value, "yl") for p in gather(b, "yh")]

    far, far_y = [None] * 3, [None] * 3
    near_zero = near_zero[None]
    far[0] = over_zh(near_zero)
    zero_y = over_y(near_zero) if split_deep else []
    qkv, probs, attended, out_keep, out_send, attn_input, w_own, w_other, gains = kernel(
        attend_body,
        "attend",
        [normed, pack_own, pack_other, lines],
        [
            ((length, 3 * inner), bf16),
            ((heads, 2 * rows, length), f32),
            ((2 * rows, inner), bf16),
            ((rows, wide), f32),
            ((rows, wide), bf16),
            ((length, wide), bf16),
            ((half, 4 * inner), bf16),
            ((half, 4 * inner), bf16),
            ((2, wide), f32),
        ],
        sizes=sizes,
        dims=dims,
    )

    out_keep, out_send = tick(out_keep, out_send)
    out_got = swap(out_send, "yl")
    near, rest_got, far[0], *zero_y = tick(near, rest_got, far[0], *zero_y)
    shape = (2, 2, part, 3 * lane)
    whole, *nears = kernel(
        place_rest_body,
        "place_rest",
        [near, rest_got],
        [((chunks - 1, *shape), bf16)] + [((len(g), *shape), bf16) for g in groups[1:]],
    )
    out_keep, whole, *nears = tick(out_keep, whole, *nears)
    far[1] = over_zh(nears[0])
    rest_y = over_y(whole) if split_deep else []
    out_sum = (out_keep + out_got.astype(f32)).astype(bf16)

    out_sum, far[0] = tick(out_sum, far[0])
    out_other = swap(out_sum, "x")
    residual, low_two = kernel(
        norm_body,
        "norm",
        [out_sum, out_other, tokens[0], gains],
        [((rows, wide), f32), ((rows, wide), bf16)],
        dims=dims,
    )

    low_two, far[0], nears[1] = tick(low_two, far[0], nears[1])
    far_two, core_two = swap(low_two, "zl"), swap(low_two, "k")
    far_y[0] = over_y(far[0])
    core_two, far[1], nears[1], *rest_y = tick(core_two, far[1], nears[1], *rest_y)
    far[2] = over_zh(nears[1])
    far_y[1] = over_y(far[1])


    def weights_of(j):
        g = next(g for g, group in enumerate(groups) if j in group)
        at = j - groups[g][0]
        near_blocks = []
        if split_deep:
            own, others, near_at = (near_zero, zero_y, 0) if j == 0 else (whole, rest_y, j - 1)
            own = own.reshape(own.shape[0], -1, 3 * lane)
            near_blocks = [(v, near_at) for v in (own, *others[1:])]
        return near_blocks + [(v, at) for v in far_y[g]]

    def ffn(j):
        weights = weights_of(j)
        return kernel(
            ffn_body,
            "ffn",
            [*ffn_rows, grad_rows, *(w for w, _ in weights)],
            [((4 * rows, 2 * lane), bf16), ((4 * rows, lane), bf16)],
            where=where,
            picks=tuple(at for _, at in weights),
        )

    def back(lefts, lanes):
        weights = [w for j in range(chunks) for w in weights_of(j)]
        return kernel(
            back_body,
            "back",
            [*lefts, *(w for w, _ in weights)],
            [((2, rows, wide), f32), ((2, rows, wide), bf16)],
            where=where,
            chunks=chunks,
            picks=tuple(at for _, at in weights),
            lanes=lanes,
        )

    def ffn_grad(first, hidden):
        return kernel(
            ffn_grad_body,
            "ffn_grad",
            [*ffn_rows, grad_rows, first, hidden],
            [((outer, half // outer, 3 * lane), kind) for kind in (f32, bf16)],
            outer=outer,
        )

    def sum_yh(keep, got):
        if outer == 1:
            return keep, [got]
        total = keep + got.astype(f32)
        return total[0], send_sums([total[e].astype(bf16) for e in range(1, outer)], "yh")

    def sum_y(keep, got):
        keep, got = sum_yh(keep, got)
        flat = [v.reshape(deep * 4 * part, 3 * lane) for v in (keep, *got)]
        return split(here, at_zh, deep, flat[0], flat[1:])

    def sum_y_last(keep, got):
        keep, got = sum_yh(keep, got)
        shape = (deep, 2, 2 * part, 3 * lane)
        return kernel(
            last_y_body,
            "last_y",
            [keep.reshape(shape), sum(g.astype(f32) for g in got).reshape(shape) if outer > 1 else got[0].reshape(shape)],
            [((deep, *shape[2:]), f32), ((deep, *shape[2:]), bf16)],
        )

    def sum_zh(keep, send):
        got = send_sums([send[e] for e in range(deep - 1)], "zh")
        return [v.reshape(2, 2, part, 3 * lane) for v in (keep, *got)]

    def pair(keep, got):
        shape = keep.shape[1:]
        return kernel(pair_body, "pair", [keep, got], [(shape, f32), (shape, bf16)])

    def ffn_split(group):
        count = len(group)
        return kernel(
            ffn_split_body,
            "ffn_split",
            [v for each in group for v in each],
            [
                ((count, part, 3 * lane), f32),
                ((count, part, 3 * lane), bf16),
                ((count, 2, part, 3 * lane), bf16),
            ],
            chunks=count,
        )

    far[2], far_two, core_two, *far_y[0] = tick(far[2], far_two, core_two, *far_y[0])
    far_y[2] = over_y(far[2])
    farcore_two = swap(far_two, "k")
    ffn_rows = [low_two, core_two, far_two, farcore_two]
    first_0, hidden_0 = ffn(0)
    grads = [None] * chunks
    grad_got, sums, zh_sums = [None] * chunks, [None] * chunks, [None] * chunks
    firsts, hiddens = [first_0], [hidden_0]
    for j in range(1, chunks):
        if j == chunks - 1:
            grads[0] = ffn_grad(firsts[0], hiddens[0])
            low_two, *flat = tick(low_two, *firsts, *hiddens, *grads[0])
            firsts, hiddens, grads[0] = flat[:j], flat[j : 2 * j], flat[2 * j :]
        elif j == 1:
            low_two, *flat = tick(low_two, *firsts, *hiddens)
            firsts, hiddens = flat[:1], flat[1:]
        ffn_rows[0] = low_two
        first, hidden = ffn(j)
        firsts.append(first)
        hiddens.append(hidden)
    keep, send = back(firsts, slice(0, 2 * lane))

    keep, send, *flat = tick(keep, send, *grads[0], *firsts[1:], *hiddens)
    grads[0], firsts, hiddens = flat[:2], [None, *flat[2:5]], flat[5:]
    core_got = swap(send, "k")
    grad_got[0] = swap(grads[0][1], "yl")
    grads[1] = ffn_grad(firsts[1], hiddens[1])
    core_keep, core_send = pair(keep, core_got)

    core_keep, core_send, *flat = tick(core_keep, core_send, *grads[1], *firsts[2:], *hiddens)
    grads[1], firsts, hiddens = flat[:2], [None, None, *flat[2:4]], flat[4:]
    core_got = swap(core_send, "zl")
    grad_got[1] = swap(grads[1][1], "yl")
    mixed_keep, mixed_send = back(hiddens, slice(2 * lane, 3 * lane))
    mixed_keep, mixed_send, *flat = tick(mixed_keep, mixed_send, *firsts[2:], *hiddens)
    firsts, hiddens = [None, None, *flat[:2]], flat[2:]
    mixed_got = swap(mixed_send, "k")
    grads[2] = ffn_grad(firsts[2], hiddens[2])
    grads[3] = ffn_grad(firsts[3], hiddens[3])
    mixed_keep, mixed_got, *flat = tick(mixed_keep, mixed_got, grads[0][0], *grads[2], *grads[3])
    grad_keep, grads[2], grads[3] = flat[0], flat[1:3], flat[3:]
    mixed_keep, mixed_send = pair(mixed_keep, mixed_got)
    sums[0] = sum_y(grad_keep, grad_got[0])
    core = (core_keep + core_got.astype(f32)).astype(bf16)

    core, mixed_keep, mixed_send, grad_keep, *flat = tick(
        core, mixed_keep, mixed_send, grads[1][0], *sums[0], *grads[2], *grads[3]
    )
    sums[0], grads[2], grads[3] = flat[:2], flat[2:4], flat[4:]
    core_other = swap(core, "x")
    zh_sums[0] = sum_zh(*sums[0])
    mixed_got = swap(mixed_send, "zl")
    sums[1] = sum_y(grad_keep, grad_got[1])
    d_residual, d_low = kernel(
        residual_back_body,
        "residual_back",
        [core, core_other, residual, cotangent[0], gains],
        [((rows, wide), f32), ((rows, wide), bf16)],
        dims=dims,
    )

    d_low, *flat = tick(d_low, *sums[1], *grads[2], *zh_sums[0])
    sums[1], grads[2], zh_sums[0] = flat[:2], flat[2:4], flat[4:]
    d_far = swap(d_low, "yl")
    grad_got[2] = swap(grads[2][1], "yl")
    zh_sums[1] = sum_zh(*sums[1])

    d_far, mixed_keep, mixed_got = tick(d_far, mixed_keep, mixed_got)
    mixed_half = (mixed_keep + mixed_got.astype(f32)).astype(bf16)
    mixed_other = swap(mixed_half, "x")
    d_query, d_keep, d_send, grad_table = kernel(
        attend_back_body,
        "attend_back",
        [qkv, probs, d_low, d_far, w_own, w_other],
        [
            ((2 * rows, inner), bf16),
            ((2 * outer, rows, 2 * inner), f32),
            ((2 * outer, rows, 2 * inner), bf16),
            ((8, lane), f32),
        ],
        [pltpu.VMEM((8, 2 * length), f32), pltpu.VMEM((2 * rows, inner), bf16)],
        sizes=sizes,
        buckets=buckets,
    )

    d_query, d_keep, d_send, grad_table, *zh_sums[1] = tick(
        d_query, d_keep, d_send, grad_table, *zh_sums[1]
    )
    d_got = swap(d_send, "k")
    if outer > 1:
        total = (d_keep + d_got.astype(f32)).reshape(outer, 2, rows, 2 * inner)
        arrived = send_sums([total[e].astype(bf16) for e in range(1, outer)], "yh")
        d_keep, d_got = total[0], sum(a.astype(f32) for a in arrived)
    g_keep, g_send, keep, send = kernel(
        attn_grad_body,
        "attn_grad",
        [attn_input, d_query, d_keep, d_got, d_low, d_far, attended, w_own, w_other, grad_table],
        [
            ((rows, wide), f32),
            ((rows, wide), bf16),
            ((half + tail // 2, 4 * inner), f32),
            ((half + tail, 4 * inner), bf16),
        ],
        [pltpu.VMEM((2 * rows, 3 * inner), bf16)],
        sizes=sizes,
    )

    g_keep, g_send, keep, send, grad_got[2], *grads[3] = tick(
        g_keep, g_send, keep, send, grad_got[2], *grads[3]
    )
    got = [swap(send, "k")]
    grad_got[3] = swap(grads[3][1], "yl")
    keep, grad_keep = tick(keep, grads[2][0])
    if outer > 1:
        keep, send = split(here, at_yh, outer, keep, got, tail)
        got = send_sums([send[e] for e in range(outer - 1)], "yh")
    sums[2] = sum_y(grad_keep, grad_got[2])
    keep, send = split(here, at_zl, 2, keep, got, tail)

    keep, send, g_keep, g_send, residual, grad_keep, *sums[2] = tick(
        keep, send, g_keep, g_send, residual, grads[3][0], *sums[2]
    )
    got = send_sums([send[0]], "zl")
    zh_sums[2] = sum_zh(*sums[2])
    g_got = swap(g_send, "yl")
    last_keep, last_send = sum_y_last(grad_keep, grad_got[3])
    last_got = swap(last_send, "zl")
    residual, *zh_sums[2] = tick(residual, *zh_sums[2])
    (mixed,) = kernel(
        mixed_body, "mixed", [mixed_half, mixed_other, residual], [((rows, wide), bf16)], dims=dims
    )
    keep, send = split(here, at_zh, deep, keep, got, tail)

    keep, send, mixed, last_keep, *zh_sums[2] = tick(keep, send, mixed, last_keep, *zh_sums[2])
    got = send_sums([send[e] for e in range(deep - 1)], "zh")
    (last_send,) = kernel(
        last_z_body,
        "last_z",
        [last_keep, last_got],
        [((max(deep - 1, 1), 2, 2 * part, 3 * lane), bf16)],
    )
    last_sums = send_sums([last_send[e] for e in range(deep - 1)], "zh")
    done = ffn_split(zh_sums[:-1])
    other = swap(done[2], "zl")
    group_a = [done[0], other, swap(done[1], "k")]
    keep, send = split(here, at_yl, 2, keep, got, tail)

    keep, send, g_keep, g_got, last_keep = tick(keep, send, g_keep, g_got, last_keep)
    got = swap(send[0], "yl")
    group_a.append(swap(other, "k"))
    g_sum = (g_keep + g_got.astype(f32)).astype(bf16)
    g_other = swap(g_sum, "x")
    grad_query, grad_key, grad_value, grad_out, gain_row, grad_table = kernel(
        attn_final_body,
        "attn_final",
        [keep, got, w_query, w_key, w_value, norm_one[None]],
        [((part, 2 * inner), f32)] * 4 + [((1, part), f32), ((heads_dev, lane), f32)],
        heads=heads,
    )
    gain_row, last_keep = tick(gain_row, last_keep)
    done = kernel(
        last_body,
        "last",
        [last_keep, last_got, *last_sums],
        [
            ((1, part, 3 * lane), f32),
            ((1, part, 3 * lane), bf16),
            ((1, 2, part, 3 * lane), bf16),
        ],
    )
    group_b = [done[0], done[2], swap(done[1], "k"), swap(done[2], "k")]
    grad_gate, grad_up, grad_down, grad_gains = kernel(
        ffn_final_body,
        "ffn_final",
        [*group_a, *group_b, w_gate, w_up, norm_two[None], gain_row],
        [((part, hidden_dev), f32)] * 3 + [((2, part), f32)],
        [pltpu.VMEM((3, part, 4 * chunks * lane), f32)],
        groups=2,
    )
    grad_gains, d_residual = tick(grad_gains, d_residual)
    gains_got = swap(grad_gains, "x")
    (input_grad,) = kernel(
        input_grad_body,
        "input_grad",
        [g_sum, g_other, tokens[0], gains, d_residual],
        [((rows, wide), bf16)],
        dims=dims,
    )
    grad_gains = grad_gains + gains_got
    return (
        mixed[None],
        input_grad[None],
        grad_gains[0],
        grad_query,
        grad_key,
        grad_value,
        grad_out.T,
        grad_table[:, :buckets],
        grad_gains[1],
        grad_gate,
        grad_up,
        grad_down.T,
    )


def solution(mesh):
    depths, lines, halves = (mesh.shape[a] for a in ("fsdp", "ctx", "tp"))
    fine = Mesh(
        mesh.devices.reshape(depths // 2, 2, lines // 4, 2, 2, halves),
        ("zh", "zl", "yh", "yl", "k", "x"),
    )
    depth, line = ("zh", "zl"), ("yh", "yl", "k")
    every = (*depth, *line)
    in_specs = (
        P(depth, line, None),
        P(depth, line, None),
        P(depth),
        P(every),
        P(every, "x"),
        P(every, "x"),
        P(every, "x"),
        P("x", every),
        P("x", None),
        P(every),
        P(every, "x"),
        P(every, "x"),
        P("x", every),
    )
    out_specs = (
        P(depth, line, None),
        P(depth, line, None),
        P(every),
        P(every, "x"),
        P(every, "x"),
        P(every, "x"),
        P("x", every),
        P("x", None),
        P(every),
        P(every, "x"),
        P(every, "x"),
        P("x", every),
    )
    return jax.shard_map(local, mesh=fine, in_specs=in_specs, out_specs=out_specs, check_vma=False)
```

```python
import functools

import jax
import jax.numpy as jnp
import numpy as np
from jax import lax
from jax.experimental import pallas as pl
from jax.experimental.pallas import tpu as pltpu
from jax.sharding import Mesh, PartitionSpec as P

epsilon = 1e-06
masked_value = -1e30
far_bounds = (12, 16, 23, 32, 46, 64, 91)
f32 = jnp.float32
bf16 = jnp.bfloat16
lane = 128
ffn_order = (2, 3, 0, 1, 4, 5)
attn_order = (4, 2, 1, 0, 3, 5)
at_k, at_yl, at_zl, at_zh, at_yh, at_prefix, at_lists = range(7)


def bucket_of(relative, buckets):
    offset = jnp.abs(relative)
    far = jnp.full(offset.shape, buckets // 4, jnp.int32)
    for threshold in far_bounds:
        far = far + (offset >= threshold).astype(jnp.int32)
    return jnp.where(offset < buckets // 4, offset, far) + buckets // 2 * (relative > 0).astype(
        jnp.int32
    )


def dot(left, right, dims=((1,), (0,))):
    return lax.dot_general(left, right, (dims, ((), ())), preferred_element_type=f32)


def dot_nt(left, right):
    return dot(left, right, ((1,), (1,)))


def dot_tn(left, right):
    return dot(left, right, ((0,), (0,)))


def fetch(value, axis, step):
    size = lax.axis_size(axis)
    return lax.ppermute(value, axis, [((i + step) % size, i) for i in range(size)])


def swap(value, axis):
    return fetch(value, axis, 1)


def gather(value, axis):
    return [value] + [fetch(value, axis, e) for e in range(1, lax.axis_size(axis))]


def send_sums(sends, axis):
    size = lax.axis_size(axis)
    return [fetch(sends[e - 1], axis, size - e) for e in range(1, size)]


class Clock:
    def __init__(self, token):
        self.token = token

    def tick(self, *values):
        self.token, *values = lax.optimization_barrier((self.token, *values))
        return values


costs = {"attn_final": 200, "back": 200, "last_z": 40, "mixed": 40, "place": 200}


def runs_of(dims, order, inverse):
    index = np.arange(int(np.prod(dims))).reshape(dims).transpose(order).reshape(-1)
    if inverse:
        index = np.argsort(index)
    cuts = [0, *(np.flatnonzero(np.diff(index) != 1) + 1).tolist(), len(index)]
    return [(int(index[a]), int(index[a]) + b - a) for a, b in zip(cuts[:-1], cuts[1:])]


def reorder(value, dims, order, inverse=False):
    return jnp.concatenate([value[:, a:b] for a, b in runs_of(dims, order, inverse)], axis=1)


def inv_scale(values):
    return lax.rsqrt(jnp.mean(values * values, axis=-1, keepdims=True) + epsilon)


def norm_back(scale, normed, grad_normed):
    return scale * (grad_normed - normed * jnp.mean(grad_normed * normed, axis=-1, keepdims=True))


def aligned(index, size):
    return pl.ds(pl.multiple_of(index * size, size), size)


def call(body, name, here, arrays, outs, scratch=(), raw=0, **static):
    cost = costs.get(name, 100)
    space = pl.BlockSpec(memory_space=pltpu.VMEM)
    spaces = [pl.BlockSpec(memory_space=pltpu.HBM)] * raw + [space] * (len(arrays) - raw)
    need = sum(int(np.prod(s.shape)) * jnp.dtype(s.dtype).itemsize for s in scratch[: len(scratch) - bool(raw)])
    need += (6 << 20) if static.get("dims", (lane,))[-1] >= 32 else (40 << 20)
    return pl.pallas_call(
        functools.partial(body, **static),
        out_shape=tuple(jax.ShapeDtypeStruct(shape, kind) for shape, kind in outs),
        in_specs=[pl.BlockSpec(memory_space=pltpu.SMEM)] + spaces,
        out_specs=tuple(space for _ in outs),
        scratch_shapes=scratch,
        compiler_params=pltpu.CompilerParams(vmem_limit_bytes=(56 << 20) if raw else need),
        cost_estimate=pl.CostEstimate(
            flops=20_000_000 * cost, bytes_accessed=80_000 * cost, transcendentals=0
        ),
        name=name,
    )(here, *arrays)


def place_body(here, own, got, out, *, which):
    at = here[which]
    out[at] = own[...]
    out[1 - at] = got[...]


def pack_attn_body(here, wq, wk, wv, wo, one, two, own, send, mats, gains, sems):
    part, wide = mats.shape[1:]
    half = wide // 2
    copies = [
        pltpu.make_async_copy(ref, room, sems.at[i])
        for i, (ref, room) in enumerate(
            [*((ref, mats.at[i]) for i, ref in enumerate((wq, wk, wv, wo))), (one, gains.at[0]), (two, gains.at[1])]
        )
    ]
    for copy in copies:
        copy.start()
    for copy in copies:
        copy.wait()
    low = jnp.concatenate([mats[i, :, :half] for i in range(4)], axis=1)
    high = jnp.concatenate([mats[i, :, half:] for i in range(4)], axis=1)
    row = lax.broadcasted_iota(jnp.int32, (8, part), 0)
    first, second = (jnp.broadcast_to(gains[i].astype(f32), (8, part)) for i in range(2))
    head = jnp.where(row == 0, first, jnp.where(row == 1, second, 0.0)).astype(bf16)

    def write(out, mat):
        out[:8] = jnp.zeros((8, out.shape[1]), bf16)
        out[:8, :part] = head
        out[8:] = mat

    @pl.when(here[at_yl] == 0)
    def _():
        write(own, low)
        write(send, high)

    @pl.when(here[at_yl] != 0)
    def _():
        write(own, high)
        write(send, low)


def pack_ffn_body(here, wg, wu, wd, own, send, room, *, chunks):
    hidden = wg.shape[1]
    whole = hidden // lane * lane
    room[:, :, whole:] = jnp.zeros((3, wg.shape[0], 4 * chunks * lane - whole), bf16)
    room[0, :, :hidden] = wg[...]
    room[1, :, :hidden] = wu[...]
    room[2, :, :hidden] = wd[...]
    for out, core in ((own, here[at_k]), (send, 1 - here[at_k])):
        for h in range(2):
            for j in range(chunks):
                for m in range(3):
                    out[h, j, :, m * lane : (m + 1) * lane] = room[
                        m, :, aligned((2 * h + core) * chunks + j, lane)
                    ]


def place_ffn_body(here, own, got, near, first, rest, *, chunks):
    k, zl = here[at_k], here[at_zl]
    for j in range(chunks):
        near[j, k] = own[zl, j]
        near[j, 1 - k] = got[zl, j]
        out, at = (rest, j - 1) if j else (first, 0)
        out[at, k] = own[1 - zl, j]
        out[at, 1 - k] = got[1 - zl, j]


def place_first_body(here, near, got, out):
    zl = here[at_zl]
    out[zl] = near[0]
    out[1 - zl] = got[0]


def place_rest_body(here, near, rest, whole, *outs):
    zl = here[at_zl]
    j = 0
    for group in outs:
        for at in range(group.shape[0]):
            for out in (whole.at[j], group.at[at]):
                out[zl] = near[j + 1]
                out[1 - zl] = rest[j]
            j += 1


def buckets_row(span, buckets):
    return bucket_of(lax.broadcasted_iota(jnp.int32, (1, 2 * span), 1) - span, buckets)


def rows_body(here, table, *refs, dims, heads):
    *blocks, out, grads_out, lines = refs
    grads, blocks = blocks[:4], blocks[4:]
    rows = grads[0].shape[0]
    for at, block in enumerate(blocks):
        values = block[...].astype(f32)
        out[at * rows : (at + 1) * rows] = reorder(values * inv_scale(values), dims, attn_order)
    for at, block in enumerate(grads):
        low = reorder(block[...].astype(f32), dims, ffn_order)
        grads_out[at * rows : (at + 1) * rows] = low.astype(bf16)
    buckets = table.shape[1]
    values = table[...].astype(f32)
    mine = jnp.where(here[at_yl] == 0, values[:heads], values[heads:])
    row = buckets_row(lines.shape[1] // 2, buckets)
    line = jnp.zeros((heads, lines.shape[1]), f32)
    for b in range(buckets):
        line = line + jnp.where(row == b, mine[:, b : b + 1], 0.0)
    lines[...] = jnp.zeros_like(lines)
    lines[:heads] = line


def bias_block(line_ref, head, start, rows):
    line = line_ref[pl.ds(head, 1), pl.ds(pl.multiple_of(start, rows), 2 * rows)]
    spread = jnp.broadcast_to(line, (rows, 2 * rows))
    return pltpu.roll(spread, 0, 1, stride=1, stride_axis=0)[:, rows:]


def attend_body(
    here, normed, pack_own, pack_other, lines,
    qkv, probs_out, attended, keep, send, inputs, w_own, w_other, gains, *, sizes, dims
):
    rows, heads, width, query_blocks, key_blocks, span = sizes
    prefix = here[at_prefix]
    inner = heads * width
    half = w_own.shape[0]
    part = dims[-1]
    gain_parts = []
    for pack, weights in ((pack_own, w_own), (pack_other, w_other)):
        for at in range(half // part):
            weights[at * part : (at + 1) * part] = pack[at, 8:]
        gain_parts.append(
            [
                jnp.concatenate([pack[at, i : i + 1, :part].astype(f32) for at in range(half // part)], axis=1)
                for i in range(2)
            ]
        )
    for i in range(2):
        low, high = gain_parts[0][i], gain_parts[1][i]
        gain = jnp.where(
            here[at_k] == 0,
            jnp.concatenate([low, high], axis=1),
            jnp.concatenate([high, low], axis=1),
        )
        if i == 0:
            inputs[...] = (normed[...] * gain).astype(bf16)
        gains[i : i + 1] = reorder(gain, dims, attn_order, True)
    places = [here[at_lists + i] for i in range(key_blocks)]
    mine, other = aligned(here[at_k], half), aligned(1 - here[at_k], half)
    qkv[...] = (
        dot(inputs[:, mine], w_own[:, : 3 * inner]) + dot(inputs[:, other], w_other[:, : 3 * inner])
    ).astype(bf16)
    for head in range(heads):
        lanes = slice(head * width, (head + 1) * width)
        keys = qkv[:, inner + head * width : inner + (head + 1) * width]
        values = qkv[:, 2 * inner + head * width : 2 * inner + (head + 1) * width]
        for at, block in enumerate(query_blocks):
            query_block = places[block]
            queries = qkv[block * rows : (block + 1) * rows, lanes]
            raw = dot_nt(queries, keys)
            query_pos = query_block * rows + lax.broadcasted_iota(jnp.int32, (rows, rows), 0)
            parts = []
            for key_at, key_block in enumerate(places):
                start = (key_block - query_block) * rows + span - rows
                key_pos = key_block * rows + lax.broadcasted_iota(jnp.int32, (rows, rows), 1)
                allowed = (key_pos <= query_pos) | (key_pos < prefix)
                biased = raw[:, key_at * rows : (key_at + 1) * rows] + bias_block(
                    lines, head, start, rows
                )
                parts.append(jnp.where(allowed, biased, masked_value))
            scores = jnp.concatenate(parts, axis=1)
            top = jnp.max(scores, axis=1, keepdims=True)
            powers = jnp.exp(scores - top)
            probs = powers / jnp.sum(powers, axis=1, keepdims=True)
            probs_out[head, at * rows : (at + 1) * rows, :] = probs
            attended[at * rows : (at + 1) * rows, lanes] = dot(probs.astype(bf16), values).astype(
                bf16
            )
    for lanes, weights in ((mine, w_own), (other, w_other)):
        out = dot_nt(attended[...], weights[:, 3 * inner :])
        keep[:, lanes] = out[:rows]
        send[:, lanes] = out[rows:].astype(bf16)


def norm_body(here, own, got, tokens, gains, residual, low, *, dims):
    total = own[...].astype(f32) + got[...].astype(f32)
    values = tokens[...].astype(f32) + reorder(total, dims, attn_order, True)
    residual[...] = values
    low[...] = reorder(values * inv_scale(values) * gains[1:2], dims, ffn_order).astype(bf16)


def tall(refs, lanes):
    return jnp.concatenate([ref[:, lanes] for ref in refs], axis=0)


def ffn_body(here, *refs, where, picks):
    rows, grads, weights, (first_out, hidden_out) = refs[:4], refs[4], refs[5:-2], refs[-2:]
    weights = [w if at is None else w.at[at] for at, w in zip(picks, weights)]
    size = weights[0].shape[0]
    first, d_hidden = None, None
    for at, w in enumerate(weights):
        lanes = aligned(here[where + at], size)
        first_part = dot(tall(rows, lanes), w[:, : 2 * lane])
        d_part = dot(grads[:, lanes], w[:, 2 * lane :])
        first = first_part if first is None else first + first_part
        d_hidden = d_part if d_hidden is None else d_hidden + d_part
    gate, up = first[:, :lane], first[:, lane:]
    root = float(np.sqrt(2.0 / np.pi))
    square = gate * gate
    bend = jnp.tanh(root * gate * (1.0 + 0.044715 * square))
    half = 0.5 * (1.0 + bend)
    active = gate * half
    slope = half + 0.5 * gate * (1.0 - bend * bend) * (root * (1.0 + 3.0 * 0.044715 * square))
    hidden_out[...] = (active * up).astype(bf16)
    first_out[:, :lane] = (d_hidden * up * slope).astype(bf16)
    first_out[:, lane:] = (d_hidden * active).astype(bf16)


def back_body(here, *refs, where, chunks, picks, lanes):
    lefts, weights, (keep, send) = refs[:chunks], refs[chunks:-2], refs[-2:]
    weights = [w if at is None else w.at[at] for at, w in zip(picks, weights)]
    blocks = len(weights) // chunks
    rows = keep.shape[1]
    for at in range(blocks):
        total = None
        for j in range(chunks):
            w = weights[j * blocks + at]
            part = dot_nt(lefts[j][...], w[:, lanes])
            total = part if total is None else total + part
        here_lanes = aligned(here[where + at], w.shape[0])
        for a in range(2):
            keep[a, :, here_lanes] = total[2 * a * rows : (2 * a + 1) * rows]
            send[a, :, here_lanes] = total[(2 * a + 1) * rows : (2 * a + 2) * rows].astype(bf16)


def ffn_grad_body(here, *refs, outer):
    rows, grads, (first, hidden, keep, send) = refs[:4], refs[4], refs[5:]
    size = keep.shape[1]
    for e in range(outer):
        yh = here[at_yh] + e
        yh = jnp.where(yh >= outer, yh - outer, yh) * 2
        for out, y in ((keep, yh + here[at_yl]), (send, yh + 1 - here[at_yl])):
            lanes = aligned(y, size)
            out[e, :, : 2 * lane] = dot_tn(tall(rows, lanes), first[...]).astype(out.dtype)
            out[e, :, 2 * lane :] = dot_tn(grads[:, lanes], hidden[...]).astype(out.dtype)


def table_parts(values):
    high = values.astype(bf16)
    return jnp.concatenate([high, (values - high.astype(f32)).astype(bf16)], axis=0)


def table_value(parts):
    half = parts.shape[0] // 2
    return parts[:half].astype(f32) + parts[half:].astype(f32)


def split_body(here, own, *refs, which, count, tail):
    *got, keep, send = refs
    size = keep.shape[0] - tail

    def piece(ref, at):
        if size % 8 == 0:
            return ref[aligned(at, size)]
        value = ref[:size]
        for i in range(1, count):
            value = jnp.where(at == i, ref[i * size : (i + 1) * size], value)
        return value

    for e in range(count):
        at = here[which] + e
        at = jnp.where(at >= count, at - count, at)
        total = piece(own, at)
        for ref in got:
            total = total + piece(ref, at).astype(f32)
        if e:
            send[e - 1, :size] = total.astype(bf16)
        else:
            keep[:size] = total
    if tail:
        total = own[count * size :]
        for ref in got:
            total = total + table_value(ref[count * size :])
        parts = table_parts(total)
        keep[size:] = table_value(parts)
        for e in range(count - 1):
            send[e, size:] = parts


def split(here, which, count, own, got, tail=0):
    size = (own.shape[0] - tail // 2) // count
    return call(
        split_body,
        "split",
        here,
        [own, *got],
        [((size + tail // 2, own.shape[1]), f32), ((max(count - 1, 1), size + tail, own.shape[1]), bf16)],
        which=which,
        count=count,
        tail=tail // 2,
    )


def ffn_split_body(here, *refs, chunks):
    done, core, other = refs[-3:]
    each = (len(refs) - 3) // chunks
    zl, k = here[at_zl], here[at_k]
    for j in range(chunks):
        own, *got = refs[j * each : (j + 1) * each]

        def total(depth, slice_):
            value = own[depth, slice_]
            for ref in got:
                value = value + ref[depth, slice_].astype(f32)
            return value

        done[j] = total(zl, k)
        core[j] = total(zl, 1 - k).astype(bf16)
        other[j, 0] = total(1 - zl, 0).astype(bf16)
        other[j, 1] = total(1 - zl, 1).astype(bf16)


def last_y_body(here, own, got, keep, send):
    zl = here[at_zl]
    for h in range(keep.shape[0]):
        keep[h] = own[h, zl] + got[h, zl].astype(f32)
        send[h] = (own[h, 1 - zl] + got[h, 1 - zl].astype(f32)).astype(bf16)


def ahead(here, which, count, e):
    at = here[which] + e
    return jnp.where(at >= count, at - count, at)


def last_z_body(here, own, got, send):
    count = own.shape[0]
    for e in range(1, count):
        at = ahead(here, at_zh, count, e)
        send[e - 1, 0] = own[at].astype(bf16)
        send[e - 1, 1] = got[at]


def last_body(here, own, got, *refs):
    *arrived, done, core, other = refs
    part = done.shape[1]
    zh, k = here[at_zh], here[at_k]
    mine, theirs = own[zh], got[zh].astype(f32)
    for ref in arrived:
        mine = mine + ref[0].astype(f32)
        theirs = theirs + ref[1].astype(f32)
    low, high = mine[:part], mine[part:]
    done[0] = jnp.where(k == 0, low, high)
    core[0] = jnp.where(k == 0, high, low).astype(bf16)
    other[0, 0] = theirs[:part].astype(bf16)
    other[0, 1] = theirs[part:].astype(bf16)


def sum_row(values):
    sums = jnp.sum(values, axis=1, keepdims=True)
    return jnp.broadcast_to(sums, (values.shape[0], lane)).T[0:1]


def ffn_final_body(here, *refs, groups):
    parts, rest = refs[: 4 * groups], refs[4 * groups :]
    wg, wu, gain, first_row, grad_g, grad_u, grad_d, grad_gain, room = rest
    hidden = wg.shape[1]
    chunks = room.shape[2] // (4 * lane)
    zl, k = here[at_zl], here[at_k]
    j = 0
    for group in range(groups):
        done, other, core, far = parts[4 * group : 4 * group + 4]
        for at in range(done.shape[0]):
            for h, c, value in (
                (zl, k, done[at]),
                (1 - zl, k, other[at, k].astype(f32)),
                (zl, 1 - k, core[at].astype(f32)),
                (1 - zl, 1 - k, far[at, k].astype(f32)),
            ):
                for m in range(3):
                    room[m, :, aligned((2 * h + c) * chunks + j, lane)] = value[
                        :, m * lane : (m + 1) * lane
                    ]
            j += 1
    gate, up = room[0, :, :hidden], room[1, :, :hidden]
    grad_g[...] = gate
    grad_u[...] = up
    grad_d[...] = room[2, :, :hidden]
    sums = gate * wg[...].astype(f32) + up * wu[...].astype(f32)
    grad_gain[0:1] = first_row[...]
    grad_gain[1:2] = sum_row(sums) / gain[...].astype(f32)


def pair_body(here, own, got, keep, send):
    keep[...] = own[0] + got[0].astype(f32)
    send[...] = (own[1] + got[1].astype(f32)).astype(bf16)


def residual_back_body(here, own, got, residual, cotangent, gains, d_residual, d_low, *, dims):
    total = own[...].astype(f32) + got[...].astype(f32)
    grad_normed = reorder(total, dims, ffn_order, True) * gains[1:2]
    values = residual[...]
    scale = inv_scale(values)
    back = cotangent[...].astype(f32) + norm_back(scale, values * scale, grad_normed)
    d_residual[...] = back
    d_low[...] = reorder(back, dims, attn_order).astype(bf16)


def attend_back_body(
    here, qkv, probs_in, d_own, d_far, w_own, w_other,
    d_query, d_keep, d_send, table, lines, d_att, *, sizes, buckets
):
    rows, heads, width, query_blocks, key_blocks, span = sizes
    inner = heads * width
    half = w_own.shape[0]
    places = [here[at_lists + i] for i in range(key_blocks)]
    mine, other = aligned(here[at_k], half), aligned(1 - here[at_k], half)
    d_rows = (d_own, d_far)
    d_att[...] = (
        dot(tall(d_rows, mine), w_own[:, 3 * inner :])
        + dot(tall(d_rows, other), w_other[:, 3 * inner :])
    ).astype(bf16)
    lines[...] = jnp.zeros_like(lines)
    up, down = (lax.broadcasted_iota(jnp.int32, (rows, rows), axis) for axis in (0, 1))
    flip = (up + down == rows - 1).astype(bf16)
    for head in range(heads):
        lanes = slice(head * width, (head + 1) * width)
        value_lanes = slice(inner + head * width, inner + (head + 1) * width)
        keys = qkv[:, inner + head * width : inner + (head + 1) * width]
        values = qkv[:, 2 * inner + head * width : 2 * inner + (head + 1) * width]
        d_key, d_value = None, None
        for at, block in enumerate(query_blocks):
            queries = qkv[block * rows : (block + 1) * rows, lanes]
            d_attended = d_att[at * rows : (at + 1) * rows, lanes]
            probs = probs_in[head, at * rows : (at + 1) * rows, :]
            d_probs = dot_nt(d_attended, values)
            delta = jnp.sum(probs * d_probs, axis=1, keepdims=True)
            d_scores = (probs * (d_probs - delta)).astype(bf16)
            d_query[at * rows : (at + 1) * rows, lanes] = dot(d_scores, keys).astype(bf16)
            key_part = dot_tn(d_scores, queries)
            value_part = dot_tn(probs.astype(bf16), d_attended)
            d_key = key_part if d_key is None else d_key + key_part
            d_value = value_part if d_value is None else d_value + value_part
            upward = dot(flip, d_scores)
            for key_at, key_block in enumerate(places):
                start = (key_block - places[block]) * rows + span - rows
                piece = upward[:, key_at * rows : (key_at + 1) * rows]
                padded = jnp.concatenate([piece, jnp.zeros_like(piece)], axis=1)
                turned = pltpu.roll(padded, 1, 1, stride=1, stride_axis=0)
                span_at = pl.ds(pl.multiple_of(start, rows), 2 * rows)
                lines[pl.ds(head, 1), span_at] += jnp.sum(turned, axis=0, keepdims=True)
        for key_at in range(key_blocks):
            from_, to = slice(key_at * rows, (key_at + 1) * rows), key_at // 2
            for out, parity in ((d_keep, 0), (d_send, 1)):
                if key_at % 2 == parity:
                    out[to, :, lanes] = d_key[from_].astype(out.dtype)
                    out[to, :, value_lanes] = d_value[from_].astype(out.dtype)
    row = buckets_row(span, buckets)
    column = lax.broadcasted_iota(jnp.int32, table.shape, 1)
    total = jnp.zeros(table.shape, f32)
    for b in range(buckets):
        one = jnp.sum(jnp.where(row == b, lines[...], 0.0), axis=1, keepdims=True)
        total = jnp.where(column == b, one, total)
    table[...] = total


def attn_grad_body(
    here, inputs, d_query, d_keep, d_got, d_own, d_far, attended, w_own, w_other, table,
    g_keep, g_send, keep, send, d_qkv, *, sizes
):
    rows, heads, width, query_blocks, key_blocks, span = sizes
    inner = heads * width
    half = w_own.shape[0]
    mine, other = aligned(here[at_k], half), aligned(1 - here[at_k], half)
    d_qkv[:, :inner] = d_query[...]
    for at in range(2):
        d_qkv[at * rows : (at + 1) * rows, inner:] = (d_keep[at] + d_got[at].astype(f32)).astype(bf16)
    for lanes, weights, out in ((mine, w_own, keep), (other, w_other, send)):
        part = dot_nt(d_qkv[...], weights[:, : 3 * inner])
        g_keep[:, lanes] = part[:rows]
        g_send[:, lanes] = part[rows:].astype(bf16)
        two = jnp.concatenate([inputs[b * rows : (b + 1) * rows, lanes] for b in query_blocks], axis=0)
        out[:half, : 3 * inner] = dot_tn(two, d_qkv[...]).astype(out.dtype)
        out[:half, 3 * inner :] = dot_tn(tall((d_own, d_far), lanes), attended[...]).astype(out.dtype)
    parts = table_parts(table[...])
    keep[half:] = jnp.zeros((keep.shape[0] - half, keep.shape[1]), f32)
    send[half:] = jnp.zeros((send.shape[0] - half, send.shape[1]), bf16)
    keep[half:, :lane] = table_value(parts)
    send[half:, :lane] = parts


def input_grad_body(here, own, got, tokens, gains, d_residual, out, *, dims):
    total = own[...].astype(f32) + got[...].astype(f32)
    grad_normed = reorder(total, dims, attn_order, True) * gains[0:1]
    values = tokens[...].astype(f32)
    scale = inv_scale(values)
    out[...] = (d_residual[...] + norm_back(scale, values * scale, grad_normed)).astype(bf16)


def mixed_body(here, own, got, residual, out, *, dims):
    total = own[...].astype(f32) + got[...].astype(f32)
    out[...] = (residual[...] + reorder(total, dims, ffn_order, True)).astype(bf16)


def attn_final_body(here, own, got, wq, wk, wv, gain, gq, gk, gv, go, grad_gain, table, *, heads):
    part, inner = gq.shape[0], own.shape[1] // 4

    def finish(low, high, low_table, high_table):
        grads = [
            jnp.concatenate([m[:, i * inner : (i + 1) * inner] for m in (low, high)], axis=1)
            for i in range(4)
        ]
        sums = 0.0
        for out, weights, grad in ((gq, wq, grads[0]), (gk, wk, grads[1]), (gv, wv, grads[2])):
            out[...] = grad
            sums = sums + grad * weights[...].astype(f32)
        go[...] = grads[3]
        grad_gain[...] = sum_row(sums) / gain[...].astype(f32)
        table[...] = jnp.concatenate([low_table[:heads], high_table[:heads]], axis=0)

    values = own[:part], got[:part].astype(f32)
    tables = own[part:, :lane], table_value(got[part:, :lane])

    @pl.when(here[at_yl] == 0)
    def _():
        finish(*values, *tables)

    @pl.when(here[at_yl] != 0)
    def _():
        finish(*values[::-1], *tables[::-1])


def local(
    tokens,
    cotangent,
    prefix,
    norm_one,
    w_query,
    w_key,
    w_value,
    w_out,
    position_bias_matrix,
    norm_two,
    w_gate,
    w_up,
    w_down,
):
    outer, deep = lax.axis_size("yh"), lax.axis_size("zh")
    rows, wide = tokens.shape[1:]
    part = w_query.shape[0]
    heads_dev, buckets = position_bias_matrix.shape
    heads = heads_dev // 2
    width = w_query.shape[1] // heads_dev
    inner = heads * width
    hidden_dev = w_gate.shape[1]
    chunks = -(-hidden_dev // (4 * lane))
    length = rows * outer * 4
    dims = (deep, 2, outer, 2, 2, part)
    half = wide // 2
    key_blocks = 4 * outer
    sizes = (rows, heads, width, (0, 2), key_blocks, length)

    tail = 16
    split_deep = deep == 2 and (4 * part) % lane == 0
    deep_blocks = deep if split_deep else 1
    yh, yl, k, zl, zh = (lax.axis_index(a) for a in ("yh", "yl", "k", "zl", "zh"))
    relative = [(e, a) for a in range(2) for e in range(outer)]
    ys = [((yh + e) % outer) * 2 + (yl + a) % 2 for e, a in relative]
    where = at_lists + key_blocks
    here = [k, yl, zl, zh, yh, prefix[0]]
    here += [
        ((yh + e) % outer) * 4 + ((yl + a) % 2) * 2 + (k + b) % 2
        for e in range(outer)
        for a in range(2)
        for b in range(2)
    ]
    here += [y * deep_blocks + (zh + d) % deep_blocks for d in range(deep_blocks) for y in ys]
    here = jnp.stack([jnp.asarray(v, jnp.int32) for v in here])
    tick = Clock(here).tick
    which = {"k": at_k, "yl": at_yl, "zl": at_zl, "zh": at_zh, "yh": at_yh}

    def kernel(body, name, arrays, outs, scratch=(), **static):
        return call(body, name, here, arrays, outs, scratch, **static)

    def place(pieces, axis):
        size, shape = len(pieces), pieces[0].shape
        if size == 1:
            return pieces[0][None]
        if size == 2:
            outs = [((2, *shape), pieces[0].dtype)]
            return kernel(place_body, "place", pieces, outs, which=which[axis])[0]
        stack = jnp.zeros((size, *shape), pieces[0].dtype)
        for e, piece in enumerate(pieces):
            at = (lax.axis_index(axis) + e) % size
            stack = lax.dynamic_update_slice_in_dim(stack, piece[None], at, 0)
        return stack

    def both(value, axis):
        return place(gather(value, axis), axis)

    tall_part = 8 + part
    own, send = kernel(
        pack_attn_body,
        "pack_attn",
        [w_query, w_key, w_value, w_out.T, norm_one[None], norm_two[None]],
        [((tall_part, 4 * inner), bf16)] * 2,
        [
            pltpu.VMEM((4, part, 2 * inner), bf16),
            pltpu.VMEM((2, 1, part), bf16),
            pltpu.SemaphoreType.DMA((6,)),
        ],
        raw=6,
    )
    own, send, own_grad, *ffn_in = tick(own, send, cotangent[0], w_gate, w_up, w_down.T)
    pack_got = swap(send, "yl")
    far_grad = swap(own_grad, "zl")
    ffn_own, ffn_send = kernel(
        pack_ffn_body,
        "pack_ffn",
        ffn_in,
        [((2, chunks, part, 3 * lane), bf16)] * 2,
        [pltpu.VMEM((3, part, 4 * chunks * lane), bf16)],
        chunks=chunks,
    )
    pack = place([own, pack_got], "yl")

    pack, ffn_own, ffn_send, own_tokens = tick(pack, ffn_own, ffn_send, tokens[0])
    pack_all = gather(pack, "zh")
    far_tokens = swap(own_tokens, "yl")
    near, near_first, near_rest = kernel(
        place_ffn_body,
        "place_ffn",
        [ffn_own, swap(ffn_send, "k")],
        [((n, 2, part, 3 * lane), bf16) for n in (chunks, 1, chunks - 1)],
        chunks=chunks,
    )
    pack = place(pack_all, "zh")

    pack, near, near_first, near_rest, far_tokens, own_tokens, far_grad, own_grad = tick(
        pack, near, near_first, near_rest, far_tokens, own_tokens, far_grad, own_grad
    )
    pack_all = gather(pack, "zl")
    first_got = swap(near_first, "zl")
    row_blocks = [p for pair in zip(gather(own_tokens, "yh"), gather(far_tokens, "yh")) for p in pair]
    row_blocks = [p for b in row_blocks for p in gather(b, "k")]
    grad_blocks = [p for b in (own_grad, far_grad) for p in gather(b, "k")]
    normed, grad_rows, lines = kernel(
        rows_body,
        "rows",
        [position_bias_matrix, *grad_blocks, *row_blocks],
        [((length, wide), f32), ((4 * rows, wide), bf16), ((8, 2 * length), f32)],
        dims=dims,
        heads=heads,
    )
    pack = place(pack_all, "zl")
    (near_zero,) = kernel(
        place_first_body, "place_first", [near, first_got], [((2, 2, part, 3 * lane), bf16)]
    )

    pack, near, near_zero, first_got, near_rest, normed, grad_rows, lines = tick(
        pack, near, near_zero, first_got, near_rest, normed, grad_rows, lines
    )
    pack = both(pack, "yh").reshape(half // part, tall_part, 4 * inner)
    pack_own, pack_other = gather(pack, "k")
    rest_got = swap(near_rest, "zl")

    groups = [[0], list(range(1, chunks - 1)), [chunks - 1]]

    def over_zh(value):
        pieces = gather(value, "zh")
        if split_deep:
            return pieces[1]
        return place(pieces, "zh").swapaxes(0, 1)

    def over_y(value):
        value = value.reshape(value.shape[0], -1, 3 * lane)
        return [p for b in gather(value, "yl") for p in gather(b, "yh")]

    far, far_y = [None] * 3, [None] * 3
    near_zero = near_zero[None]
    far[0] = over_zh(near_zero)
    zero_y = over_y(near_zero) if split_deep else []
    qkv, probs, attended, out_keep, out_send, attn_input, w_own, w_other, gains = kernel(
        attend_body,
        "attend",
        [normed, pack_own, pack_other, lines],
        [
            ((length, 3 * inner), bf16),
            ((heads, 2 * rows, length), f32),
            ((2 * rows, inner), bf16),
            ((rows, wide), f32),
            ((rows, wide), bf16),
            ((length, wide), bf16),
            ((half, 4 * inner), bf16),
            ((half, 4 * inner), bf16),
            ((2, wide), f32),
        ],
        sizes=sizes,
        dims=dims,
    )

    out_keep, out_send = tick(out_keep, out_send)
    out_got = swap(out_send, "yl")
    near, rest_got, far[0], *zero_y = tick(near, rest_got, far[0], *zero_y)
    shape = (2, 2, part, 3 * lane)
    whole, *nears = kernel(
        place_rest_body,
        "place_rest",
        [near, rest_got],
        [((chunks - 1, *shape), bf16)] + [((len(g), *shape), bf16) for g in groups[1:]],
    )
    out_keep, whole, *nears = tick(out_keep, whole, *nears)
    far[1] = over_zh(nears[0])
    rest_y = over_y(whole) if split_deep else []
    out_sum = (out_keep + out_got.astype(f32)).astype(bf16)

    out_sum, far[0] = tick(out_sum, far[0])
    out_other = swap(out_sum, "x")
    residual, low_two = kernel(
        norm_body,
        "norm",
        [out_sum, out_other, tokens[0], gains],
        [((rows, wide), f32), ((rows, wide), bf16)],
        dims=dims,
    )

    low_two, far[0], nears[1] = tick(low_two, far[0], nears[1])
    far_two, core_two = swap(low_two, "zl"), swap(low_two, "k")
    far_y[0] = over_y(far[0])
    core_two, far[1], nears[1], *rest_y = tick(core_two, far[1], nears[1], *rest_y)
    far[2] = over_zh(nears[1])
    far_y[1] = over_y(far[1])


    def weights_of(j):
        g = next(g for g, group in enumerate(groups) if j in group)
        at = j - groups[g][0]
        near_blocks = []
        if split_deep:
            own, others, near_at = (near_zero, zero_y, 0) if j == 0 else (whole, rest_y, j - 1)
            own = own.reshape(own.shape[0], -1, 3 * lane)
            near_blocks = [(v, near_at) for v in (own, *others[1:])]
        return near_blocks + [(v, at) for v in far_y[g]]

    def ffn(j):
        weights = weights_of(j)
        return kernel(
            ffn_body,
            "ffn",
            [*ffn_rows, grad_rows, *(w for w, _ in weights)],
            [((4 * rows, 2 * lane), bf16), ((4 * rows, lane), bf16)],
            where=where,
            picks=tuple(at for _, at in weights),
        )

    def back(lefts, lanes):
        weights = [w for j in range(chunks) for w in weights_of(j)]
        return kernel(
            back_body,
            "back",
            [*lefts, *(w for w, _ in weights)],
            [((2, rows, wide), f32), ((2, rows, wide), bf16)],
            where=where,
            chunks=chunks,
            picks=tuple(at for _, at in weights),
            lanes=lanes,
        )

    def ffn_grad(first, hidden):
        return kernel(
            ffn_grad_body,
            "ffn_grad",
            [*ffn_rows, grad_rows, first, hidden],
            [((outer, half // outer, 3 * lane), kind) for kind in (f32, bf16)],
            outer=outer,
        )

    def sum_yh(keep, got):
        if outer == 1:
            return keep, [got]
        total = keep + got.astype(f32)
        return total[0], send_sums([total[e].astype(bf16) for e in range(1, outer)], "yh")

    def sum_y(keep, got):
        keep, got = sum_yh(keep, got)
        flat = [v.reshape(deep * 4 * part, 3 * lane) for v in (keep, *got)]
        return split(here, at_zh, deep, flat[0], flat[1:])

    def sum_y_last(keep, got):
        keep, got = sum_yh(keep, got)
        shape = (deep, 2, 2 * part, 3 * lane)
        return kernel(
            last_y_body,
            "last_y",
            [keep.reshape(shape), sum(g.astype(f32) for g in got).reshape(shape) if outer > 1 else got[0].reshape(shape)],
            [((deep, *shape[2:]), f32), ((deep, *shape[2:]), bf16)],
        )

    def sum_zh(keep, send):
        got = send_sums([send[e] for e in range(deep - 1)], "zh")
        return [v.reshape(2, 2, part, 3 * lane) for v in (keep, *got)]

    def pair(keep, got):
        shape = keep.shape[1:]
        return kernel(pair_body, "pair", [keep, got], [(shape, f32), (shape, bf16)])

    def ffn_split(group):
        count = len(group)
        return kernel(
            ffn_split_body,
            "ffn_split",
            [v for each in group for v in each],
            [
                ((count, part, 3 * lane), f32),
                ((count, part, 3 * lane), bf16),
                ((count, 2, part, 3 * lane), bf16),
            ],
            chunks=count,
        )

    far[2], far_two, core_two, *far_y[0] = tick(far[2], far_two, core_two, *far_y[0])
    far_y[2] = over_y(far[2])
    farcore_two = swap(far_two, "k")
    ffn_rows = [low_two, core_two, far_two, farcore_two]
    first_0, hidden_0 = ffn(0)
    grads = [None] * chunks
    grad_got, sums, zh_sums = [None] * chunks, [None] * chunks, [None] * chunks
    firsts, hiddens = [first_0], [hidden_0]
    for j in range(1, chunks):
        if j == chunks - 1:
            grads[0] = ffn_grad(firsts[0], hiddens[0])
            low_two, *flat = tick(low_two, *firsts, *hiddens, *grads[0])
            firsts, hiddens, grads[0] = flat[:j], flat[j : 2 * j], flat[2 * j :]
        elif j == 1:
            low_two, *flat = tick(low_two, *firsts, *hiddens)
            firsts, hiddens = flat[:1], flat[1:]
        ffn_rows[0] = low_two
        first, hidden = ffn(j)
        firsts.append(first)
        hiddens.append(hidden)
    keep, send = back(firsts, slice(0, 2 * lane))

    keep, send, *flat = tick(keep, send, *grads[0], *firsts[1:], *hiddens)
    grads[0], firsts, hiddens = flat[:2], [None, *flat[2:5]], flat[5:]
    core_got = swap(send, "k")
    grad_got[0] = swap(grads[0][1], "yl")
    grads[1] = ffn_grad(firsts[1], hiddens[1])
    core_keep, core_send = pair(keep, core_got)

    core_keep, core_send, *flat = tick(core_keep, core_send, *grads[1], *firsts[2:], *hiddens)
    grads[1], firsts, hiddens = flat[:2], [None, None, *flat[2:4]], flat[4:]
    core_got = swap(core_send, "zl")
    grad_got[1] = swap(grads[1][1], "yl")
    mixed_keep, mixed_send = back(hiddens, slice(2 * lane, 3 * lane))
    mixed_keep, mixed_send, *flat = tick(mixed_keep, mixed_send, *firsts[2:], *hiddens)
    firsts, hiddens = [None, None, *flat[:2]], flat[2:]
    mixed_got = swap(mixed_send, "k")
    grads[2] = ffn_grad(firsts[2], hiddens[2])
    grads[3] = ffn_grad(firsts[3], hiddens[3])
    mixed_keep, mixed_got, *flat = tick(mixed_keep, mixed_got, grads[0][0], *grads[2], *grads[3])
    grad_keep, grads[2], grads[3] = flat[0], flat[1:3], flat[3:]
    mixed_keep, mixed_send = pair(mixed_keep, mixed_got)
    sums[0] = sum_y(grad_keep, grad_got[0])
    core = (core_keep + core_got.astype(f32)).astype(bf16)

    core, mixed_keep, mixed_send, grad_keep, *flat = tick(
        core, mixed_keep, mixed_send, grads[1][0], *sums[0], *grads[2], *grads[3]
    )
    sums[0], grads[2], grads[3] = flat[:2], flat[2:4], flat[4:]
    core_other = swap(core, "x")
    zh_sums[0] = sum_zh(*sums[0])
    mixed_got = swap(mixed_send, "zl")
    sums[1] = sum_y(grad_keep, grad_got[1])
    d_residual, d_low = kernel(
        residual_back_body,
        "residual_back",
        [core, core_other, residual, cotangent[0], gains],
        [((rows, wide), f32), ((rows, wide), bf16)],
        dims=dims,
    )

    d_low, *flat = tick(d_low, *sums[1], *grads[2], *zh_sums[0])
    sums[1], grads[2], zh_sums[0] = flat[:2], flat[2:4], flat[4:]
    d_far = swap(d_low, "yl")
    grad_got[2] = swap(grads[2][1], "yl")
    zh_sums[1] = sum_zh(*sums[1])

    d_far, mixed_keep, mixed_got = tick(d_far, mixed_keep, mixed_got)
    mixed_half = (mixed_keep + mixed_got.astype(f32)).astype(bf16)
    mixed_other = swap(mixed_half, "x")
    d_query, d_keep, d_send, grad_table = kernel(
        attend_back_body,
        "attend_back",
        [qkv, probs, d_low, d_far, w_own, w_other],
        [
            ((2 * rows, inner), bf16),
            ((2 * outer, rows, 2 * inner), f32),
            ((2 * outer, rows, 2 * inner), bf16),
            ((8, lane), f32),
        ],
        [pltpu.VMEM((8, 2 * length), f32), pltpu.VMEM((2 * rows, inner), bf16)],
        sizes=sizes,
        buckets=buckets,
    )

    d_query, d_keep, d_send, grad_table, *zh_sums[1] = tick(
        d_query, d_keep, d_send, grad_table, *zh_sums[1]
    )
    d_got = swap(d_send, "k")
    if outer > 1:
        total = (d_keep + d_got.astype(f32)).reshape(outer, 2, rows, 2 * inner)
        arrived = send_sums([total[e].astype(bf16) for e in range(1, outer)], "yh")
        d_keep, d_got = total[0], sum(a.astype(f32) for a in arrived)
    g_keep, g_send, keep, send = kernel(
        attn_grad_body,
        "attn_grad",
        [attn_input, d_query, d_keep, d_got, d_low, d_far, attended, w_own, w_other, grad_table],
        [
            ((rows, wide), f32),
            ((rows, wide), bf16),
            ((half + tail // 2, 4 * inner), f32),
            ((half + tail, 4 * inner), bf16),
        ],
        [pltpu.VMEM((2 * rows, 3 * inner), bf16)],
        sizes=sizes,
    )

    g_keep, g_send, keep, send, grad_got[2], *grads[3] = tick(
        g_keep, g_send, keep, send, grad_got[2], *grads[3]
    )
    got = [swap(send, "k")]
    grad_got[3] = swap(grads[3][1], "yl")
    keep, grad_keep = tick(keep, grads[2][0])
    if outer > 1:
        keep, send = split(here, at_yh, outer, keep, got, tail)
        got = send_sums([send[e] for e in range(outer - 1)], "yh")
    sums[2] = sum_y(grad_keep, grad_got[2])
    keep, send = split(here, at_zl, 2, keep, got, tail)

    keep, send, g_keep, g_send, residual, grad_keep, *sums[2] = tick(
        keep, send, g_keep, g_send, residual, grads[3][0], *sums[2]
    )
    got = send_sums([send[0]], "zl")
    zh_sums[2] = sum_zh(*sums[2])
    g_got = swap(g_send, "yl")
    last_keep, last_send = sum_y_last(grad_keep, grad_got[3])
    last_got = swap(last_send, "zl")
    residual, *zh_sums[2] = tick(residual, *zh_sums[2])
    (mixed,) = kernel(
        mixed_body, "mixed", [mixed_half, mixed_other, residual], [((rows, wide), bf16)], dims=dims
    )
    keep, send = split(here, at_zh, deep, keep, got, tail)

    keep, send, mixed, last_keep, *zh_sums[2] = tick(keep, send, mixed, last_keep, *zh_sums[2])
    got = send_sums([send[e] for e in range(deep - 1)], "zh")
    (last_send,) = kernel(
        last_z_body,
        "last_z",
        [last_keep, last_got],
        [((max(deep - 1, 1), 2, 2 * part, 3 * lane), bf16)],
    )
    last_sums = send_sums([last_send[e] for e in range(deep - 1)], "zh")
    done = ffn_split(zh_sums[:-1])
    other = swap(done[2], "zl")
    group_a = [done[0], other, swap(done[1], "k")]
    keep, send = split(here, at_yl, 2, keep, got, tail)

    keep, send, g_keep, g_got, last_keep = tick(keep, send, g_keep, g_got, last_keep)
    got = swap(send[0], "yl")
    group_a.append(swap(other, "k"))
    g_sum = (g_keep + g_got.astype(f32)).astype(bf16)
    g_other = swap(g_sum, "x")
    grad_query, grad_key, grad_value, grad_out, gain_row, grad_table = kernel(
        attn_final_body,
        "attn_final",
        [keep, got, w_query, w_key, w_value, norm_one[None]],
        [((part, 2 * inner), f32)] * 4 + [((1, part), f32), ((heads_dev, lane), f32)],
        heads=heads,
    )
    gain_row, last_keep = tick(gain_row, last_keep)
    done = kernel(
        last_body,
        "last",
        [last_keep, last_got, *last_sums],
        [
            ((1, part, 3 * lane), f32),
            ((1, part, 3 * lane), bf16),
            ((1, 2, part, 3 * lane), bf16),
        ],
    )
    group_b = [done[0], done[2], swap(done[1], "k"), swap(done[2], "k")]
    grad_gate, grad_up, grad_down, grad_gains = kernel(
        ffn_final_body,
        "ffn_final",
        [*group_a, *group_b, w_gate, w_up, norm_two[None], gain_row],
        [((part, hidden_dev), f32)] * 3 + [((2, part), f32)],
        [pltpu.VMEM((3, part, 4 * chunks * lane), f32)],
        groups=2,
    )
    grad_gains, d_residual = tick(grad_gains, d_residual)
    gains_got = swap(grad_gains, "x")
    (input_grad,) = kernel(
        input_grad_body,
        "input_grad",
        [g_sum, g_other, tokens[0], gains, d_residual],
        [((rows, wide), bf16)],
        dims=dims,
    )
    grad_gains = grad_gains + gains_got
    return (
        mixed[None],
        input_grad[None],
        grad_gains[0],
        grad_query,
        grad_key,
        grad_value,
        grad_out.T,
        grad_table[:, :buckets],
        grad_gains[1],
        grad_gate,
        grad_up,
        grad_down.T,
    )


def solution(mesh):
    depths, lines, halves = (mesh.shape[a] for a in ("fsdp", "ctx", "tp"))
    fine = Mesh(
        mesh.devices.reshape(depths // 2, 2, lines // 4, 2, 2, halves),
        ("zh", "zl", "yh", "yl", "k", "x"),
    )
    depth, line = ("zh", "zl"), ("yh", "yl", "k")
    every = (*depth, *line)
    in_specs = (
        P(depth, line, None),
        P(depth, line, None),
        P(depth),
        P(every),
        P(every, "x"),
        P(every, "x"),
        P(every, "x"),
        P("x", every),
        P("x", None),
        P(every),
        P(every, "x"),
        P(every, "x"),
        P("x", every),
    )
    out_specs = (
        P(depth, line, None),
        P(depth, line, None),
        P(every),
        P(every, "x"),
        P(every, "x"),
        P(every, "x"),
        P("x", every),
        P("x", None),
        P(every),
        P(every, "x"),
        P(every, "x"),
        P("x", every),
    )
    return jax.shard_map(local, mesh=fine, in_specs=in_specs, out_specs=out_specs, check_vma=False)
```
